128 devices in a mesh: gx: 16 (over x, z), gy: 8 (over y, core).
Axes of the slice: x: 4, y: 4, z: 4, core: 2. Of those that a mesh axis runs over, the one named last changes fastest.
Arguments:
- features: bfloat16 [256, 512, 512], P('gx', 'gy'), may hold values from -6 to 6
- cotangent: bfloat16 [256, 512, 512], P('gx', 'gy'), may hold values from -6 to 6
- low: int32 [256, 512], P('gx', 'gy'), may hold values from 0 to 7, as said below
- high: int32 [256, 512], P('gx', 'gy'), may hold values from 0 to 8, as said below
- weight_one: bfloat16 [27, 64, 64], replicated, may hold values from -0.4375 to 0.4375
- weight_two: bfloat16 [27, 64, 64], replicated, may hold values from -0.4375 to 0.4375
- scale_one: float32 [64], replicated, may hold values from 0.5 to 2
- shift_one: float32 [64], replicated, may hold values from -1.5 to 1.5
- scale_two: float32 [64], replicated, may hold values from 0.5 to 2
- shift_two: float32 [64], replicated, may hold values from -1.5 to 1.5
Outputs:
- output: bfloat16 [256, 512, 512], P('gx', 'gy')
- grad_features: bfloat16 [256, 512, 512], P('gx', 'gy')
- grad_weight_one: float32 [27, 64, 64], replicated
- grad_weight_two: float32 [27, 64, 64], replicated
The draws below stay inside these ranges and needn't reach their ends.
Inputs may be any that keep to these rules, and one draw needn't show every extreme that they name: An empty column has low = high = 0; an occupied one has low < high. One device holds at most 4 filled bricks and some device holds exactly that many; the devices that share a gy index hold at most 2 filled bricks a device together, and some such group holds exactly that many. `high`: see low.
All inputs are finite; a program needn't handle non-finite values.
Results may differ from the reference program's by a relative error of at most 0.0071.
Values may be sent and summed in bfloat16 or wider, within the bound.
A program may use at most 256 MiB of HBM per device.

```python
import math
import jax
import jax.numpy as jnp
from jax import lax

C = 64
BRICK = 8
BXL = 2
BYL = 8
ACT_MAX = 4
SHARE = 2
NX = 256
NY = 512
N_GX = 16
N_GY = 8


def occupancy(key):
    key = jax.random.fold_in(key, 17)
    keys = jax.random.split(key, 10)
    groups = N_GX
    rows_count = N_GY
    slot_count = BXL * BYL
    lanes = jnp.arange(groups, dtype=jnp.int32)
    reduction = jax.random.randint(keys[0], (rows_count,), 0, groups // 2 + 1)
    reduction = reduction.at[0].set(0)
    totals = groups * SHARE - reduction
    forced = jax.random.randint(keys[1], (rows_count,), 0, 2)
    forced = forced.at[0].set(1)
    busiest = jax.random.randint(keys[2], (rows_count,), 0, groups)
    initial = jnp.where((lanes[None, :] == busiest[:, None]) & (forced[:, None] == 1), ACT_MAX, 0).astype(jnp.int32)
    weights = jax.random.randint(keys[3], (rows_count, groups), 1, 6)
    lottery = jax.random.randint(keys[4], (groups * SHARE, rows_count, groups), 0, 4096)

    def add_unit(unit_index, counts):
        needed = jnp.sum(counts, axis=1) < totals
        scores = weights * lottery[unit_index] * groups + lanes[None, :]
        scores = jnp.where(counts < ACT_MAX, scores, -1)
        chosen = jnp.argmax(scores, axis=1)
        bumped = (lanes[None, :] == chosen[:, None]) & needed[:, None]
        return counts + bumped.astype(jnp.int32)
    counts = lax.fori_loop(0, groups * SHARE, add_unit, initial)
    priority = jax.random.randint(keys[5], (groups, rows_count, slot_count), 0, 1 << 20) * slot_count
    priority = priority + jnp.arange(slot_count, dtype=jnp.int32)[None, None, :]
    ranking = jnp.argsort(jnp.argsort(priority, axis=-1), axis=-1)
    active = ranking < counts.T[:, :, None]
    active_grid = active.reshape(groups, rows_count, BXL, BYL).transpose(0, 2, 1, 3)
    active_grid = active_grid.reshape(groups * BXL, rows_count * BYL)
    xcoords = jnp.arange(NX)[:, None]
    ycoords = jnp.arange(NY)[None, :]
    live_brick = active_grid[xcoords // BRICK, ycoords // BRICK]
    pick_brick = jax.random.randint(keys[6], (groups * BXL, rows_count * BYL), 0, BRICK * BRICK)
    forced_column = xcoords % BRICK * BRICK + ycoords % BRICK == pick_brick[xcoords // BRICK, ycoords // BRICK]
    sometimes = jax.random.randint(keys[7], (NX, NY), 0, 5) < 3
    bottoms = jax.random.randint(keys[8], (NX, NY), 0, BRICK)
    spans = jax.random.randint(keys[9], (NX, NY), 1, BRICK + 1 - bottoms)
    column_on = live_brick & (sometimes | forced_column)
    low_values = jnp.where(column_on, bottoms, 0).astype(jnp.int32)
    high_values = jnp.where(column_on, bottoms + spans, 0).astype(jnp.int32)
    return (low_values, high_values)


def draw_low(key, part):
    return occupancy(key)[0]


def draw_high(key, part):
    return occupancy(key)[1]


def level_of(key, shape, cuts, low, top_value):
    gain = 1.0
    for dim, shards_of in cuts:
        steps = jax.random.uniform(jax.random.fold_in(jax.random.fold_in(key, 6), dim), (shards_of,), jnp.float32, low / len(cuts), top_value / len(cuts))
        gain = gain * jnp.repeat(jnp.exp(steps), shape[dim] // shards_of).reshape((-1,) + (1,) * (len(shape) - 1 - dim))
    return gain


def scatter_about(rng, dims, width, bound, cuts=(), held_as=jnp.bfloat16):
    factor_of = level_of(rng, dims, cuts, -0.22, 0.18) if cuts else 1.0
    drawn = jax.random.normal(rng, dims, jnp.float32) * width * factor_of
    return jnp.minimum(jnp.maximum(drawn, -bound), bound).astype(held_as)


def setup_inputs(seed: int = 0) -> dict:
    key_list = jax.random.split(jax.random.key(seed), 11)
    return {
        "features": scatter_about(key_list[0], (NX, NY, BRICK * C), 1.0, 6.0, ((0, 16), (1, 8))),
        "cotangent": scatter_about(key_list[1], (NX, NY, BRICK * C), 1.0, 6.0, ((0, 16), (1, 8))),
        "low": draw_low(jax.random.fold_in(key_list[10], 71), 0),
        "high": draw_high(jax.random.fold_in(key_list[10], 71), 0),
        "weight_one": scatter_about(key_list[4], (27, C, C), (3 * C) ** -0.5, 0.4375),
        "weight_two": scatter_about(key_list[5], (27, C, C), (3 * C) ** -0.5, 0.4375),
        "scale_one": jnp.clip(jnp.exp(jax.random.uniform(key_list[6], (C,), jnp.float32, math.log(0.5), math.log(2.0))), 0.5, 2.0),
        "shift_one": scatter_about(key_list[7], (C,), 0.5, 1.5, (), jnp.float32),
        "scale_two": jnp.clip(jnp.exp(jax.random.uniform(key_list[8], (C,), jnp.float32, math.log(0.5), math.log(2.0))), 0.5, 2.0),
        "shift_two": scatter_about(key_list[9], (C,), 0.5, 1.5, (), jnp.float32),
    }


def flat_product(window, weight):
    flat_rows = window.reshape(-1, window.shape[-1])
    return jnp.dot(flat_rows, weight, preferred_element_type=jnp.float32, precision=lax.Precision.HIGHEST)

def forward_conv(source, weight):
    source = lax.optimization_barrier(source)
    extent = source.shape[1] - 2
    layers = source.shape[3]
    channels = source.shape[4]
    padded = jnp.pad(source.astype(jnp.float32), ((0, 0), (0, 0), (0, 0), (1, 1), (0, 0)))
    running = jnp.zeros((source.shape[0], extent, extent, layers, channels), jnp.float32)
    for offset in range(27):
        shift_x, shift_y, shift_z = (offset // 9, offset // 3 % 3, offset % 3)
        window = padded[:, shift_x:shift_x + extent, shift_y:shift_y + extent, shift_z:shift_z + layers, :]
        running = running + flat_product(window, weight[offset]).reshape(running.shape)
    return running

def adjoint_conv(errors, weight):
    errors = lax.optimization_barrier(errors)
    extent = errors.shape[1] + 2
    layers = errors.shape[3]
    channels = errors.shape[4]
    padded = jnp.pad(errors.astype(jnp.float32), ((0, 0), (2, 2), (2, 2), (1, 1), (0, 0)))
    running = jnp.zeros((errors.shape[0], extent, extent, layers, channels), jnp.float32)
    for offset in range(27):
        shift_x, shift_y, shift_z = (2 - offset // 9, 2 - offset // 3 % 3, 2 - offset % 3)
        window = padded[:, shift_x:shift_x + extent, shift_y:shift_y + extent, shift_z:shift_z + layers, :]
        flat_rows = window.reshape(-1, channels)
        product = lax.dot_general(flat_rows, weight[offset], (((1,), (1,)), ((), ())), precision=lax.Precision.HIGHEST, preferred_element_type=jnp.float32)
        running = running + product.reshape(running.shape)
    return running

def weight_grad(source, errors):
    source = lax.optimization_barrier(source)
    errors = lax.optimization_barrier(errors)
    extent = errors.shape[1]
    layers = errors.shape[3]
    channels = errors.shape[4]
    padded = jnp.pad(source.astype(jnp.float32), ((0, 0), (0, 0), (0, 0), (1, 1), (0, 0)))
    flat_errors = errors.astype(jnp.float32).reshape(-1, channels)
    products = []
    for offset in range(27):
        shift_x, shift_y, shift_z = (offset // 9, offset // 3 % 3, offset % 3)
        window = padded[:, shift_x:shift_x + extent, shift_y:shift_y + extent, shift_z:shift_z + layers, :]
        products.append(lax.dot_general(window.reshape(-1, channels), flat_errors, (((0,), (0,)), ((), ())), precision=lax.Precision.HIGHEST, preferred_element_type=jnp.float32))
    return jnp.stack(products)

def silu_slope(values):
    logistic = jax.nn.sigmoid(values)
    return logistic * (1.0 + values * (1.0 - logistic))

def brick_work(regions, occupied, targets, weight_one, weight_two, scale_one, shift_one, scale_two, shift_two):
    margin_mask = occupied.astype(jnp.float32)[..., None]
    interior = margin_mask[:, 1:-1, 1:-1]
    pre_one = forward_conv(regions, weight_one) * scale_one + shift_one
    hidden = (jax.nn.silu(pre_one) * margin_mask).astype(jnp.bfloat16)
    centre = regions[:, 2:-2, 2:-2].astype(jnp.float32)
    pre_two = forward_conv(hidden, weight_two) * scale_two + shift_two + centre
    result = (jax.nn.silu(pre_two) * interior).astype(jnp.bfloat16)
    grad_two = targets.astype(jnp.float32) * interior * silu_slope(pre_two)
    error_two = (grad_two * scale_two).astype(jnp.bfloat16)
    weight_sum_two = weight_grad(hidden, error_two)
    grad_one = adjoint_conv(error_two, weight_two) * margin_mask * silu_slope(pre_one)
    error_one = (grad_one * scale_one).astype(jnp.bfloat16)
    weight_sum_one = weight_grad(regions, error_one)
    grad_input = adjoint_conv(error_one, weight_one) + jnp.pad(grad_two, ((0, 0), (2, 2), (2, 2), (0, 0), (0, 0)))
    return (result, grad_input, weight_sum_one, weight_sum_two)

def reference(features, cotangent, low, high, weight_one, weight_two, scale_one, shift_one, scale_two, shift_two):
    layers = BRICK
    channels = C
    heights = jnp.arange(layers, dtype=jnp.int32)
    column_mask = ((heights >= low[..., None]) & (heights < high[..., None])).astype(jnp.float32)
    grid_values = features.reshape(NX, NY, layers, channels)
    masked = (grid_values.astype(jnp.float32) * column_mask[..., None]).astype(jnp.bfloat16)
    field_pad = jnp.pad(masked, ((2, 2), (2, 2), (0, 0), (0, 0)))
    mask_pad = jnp.pad(column_mask, ((2, 2), (2, 2), (0, 0)))
    targets_all = cotangent.reshape(NX, NY, layers, channels)
    bricks_x = NX // layers
    bricks_y = NY // layers
    filled = (high > low).reshape(bricks_x, layers, bricks_y, layers).any(axis=(1, 3)).reshape(-1).astype(jnp.int32)
    ranked = (jnp.cumsum(filled) - 1).astype(jnp.int32)
    capacity = N_GX * N_GY * SHARE
    place = jnp.where(filled == 1, ranked, capacity).astype(jnp.int32)
    listing = jnp.zeros((capacity,), jnp.int32).at[place].set(jnp.arange(filled.shape[0], dtype=jnp.int32), mode='drop')
    live_count = jnp.sum(filled).astype(jnp.int32)
    weights_one = weight_one.astype(jnp.float32)
    weights_two = weight_two.astype(jnp.float32)
    batch_size = N_GY * SHARE
    zero_index = jnp.zeros((), jnp.int32)

    def cut_brick(slot_id):
        corner_x = (slot_id // bricks_y * layers).astype(jnp.int32)
        corner_y = (slot_id % bricks_y * layers).astype(jnp.int32)
        region = lax.dynamic_slice(field_pad, (corner_x, corner_y, zero_index, zero_index), (layers + 4, layers + 4, layers, channels))
        occupied = lax.dynamic_slice(mask_pad, (corner_x + 1, corner_y + 1, zero_index), (layers + 2, layers + 2, layers))
        target = lax.dynamic_slice(targets_all, (corner_x, corner_y, zero_index, zero_index), (layers, layers, layers, channels))
        return (region, occupied, target)

    def process(step_index, carried):
        out_grid, grad_grid, sum_one, sum_two = carried
        first = (step_index * batch_size).astype(jnp.int32)
        brick_ids = lax.dynamic_slice(listing, (first,), (batch_size,))
        live_rows = first + jnp.arange(batch_size, dtype=jnp.int32) < live_count
        regions, occupied, targets = jax.vmap(cut_brick)(brick_ids)
        regions = jnp.where(live_rows[:, None, None, None, None], regions, jnp.zeros_like(regions))
        occupied = jnp.where(live_rows[:, None, None, None], occupied, jnp.zeros_like(occupied))
        targets = jnp.where(live_rows[:, None, None, None, None], targets, jnp.zeros_like(targets))
        result, grad_input, part_one, part_two = brick_work(regions, occupied, targets, weights_one, weights_two, scale_one, shift_one, scale_two, shift_two)

        def deposit(position, grids):
            grid_out, grid_grad = grids
            slot_id = brick_ids[position]
            corner_x = (slot_id // bricks_y * layers).astype(jnp.int32)
            corner_y = (slot_id % bricks_y * layers).astype(jnp.int32)
            starts = (corner_x, corner_y, zero_index, zero_index)
            current = lax.dynamic_slice(grid_out, starts, (layers, layers, layers, channels))
            grid_out = lax.dynamic_update_slice(grid_out, current + result[position], starts)
            current_grad = lax.dynamic_slice(grid_grad, starts, (layers + 4, layers + 4, layers, channels))
            grid_grad = lax.dynamic_update_slice(grid_grad, current_grad + grad_input[position], starts)
            return (grid_out, grid_grad)
        out_grid, grad_grid = lax.fori_loop(0, batch_size, deposit, (out_grid, grad_grid))
        return (out_grid, grad_grid, sum_one + part_one, sum_two + part_two)
    initial = (jnp.zeros((NX, NY, layers, channels), jnp.bfloat16), jnp.zeros((NX + 4, NY + 4, layers, channels), jnp.float32), jnp.zeros((27, channels, channels), jnp.float32), jnp.zeros((27, channels, channels), jnp.float32))
    out_grid, grad_grid, sum_one, sum_two = lax.fori_loop(0, capacity // batch_size, process, initial)
    output = out_grid.reshape(NX, NY, layers * channels)
    grad_core = grad_grid[2:-2, 2:-2] * column_mask[..., None]
    grad_features = grad_core.astype(jnp.bfloat16).reshape(NX, NY, layers * channels)
    return (output, grad_features, sum_one / capacity, sum_two / capacity)
```

```python
import functools

import jax
import jax.numpy as jnp
from jax import lax
from jax.experimental import pallas as pl
from jax.experimental.pallas import tpu as pltpu
from jax.sharding import PartitionSpec as P

MESH = pl.DeviceIdType.MESH
F32 = jnp.float32
BF16 = jnp.bfloat16
BRICK = 8
C = 64
WIDTH = 512
SLOTS = 4
SHARE = 2
BX, BY = 2, 8
W = 12
ROWS = SLOTS * W
CORE = SLOTS * BRICK
BLOCKS = 16
HALOS = [(dx, dy) for dx in (-1, 0, 1) for dy in (-1, 0, 1) if dx or dy]


def lane(shape):
    return lax.broadcasted_iota(jnp.int32, shape, len(shape) - 1)


def turned(value):
    return pltpu.roll(value, 64, value.ndim - 1)


def height_mask(bounds):
    first = lane(bounds.shape) < 64
    other = turned(bounds)
    low, high = jnp.where(first, bounds, other), jnp.where(first, other, bounds)
    step = jnp.where(first, 0.0, 1.0)
    return [(step + 2.0 * c >= low) & (step + 2.0 * c < high) for c in range(4)]


def toeplitz(one, two, pair_ref, t):
    first = lane(one.shape) < 64
    zero = jnp.zeros_like(one)
    start = jnp.where(first, turned(one), zero)
    end = jnp.where(first, zero, turned(two))
    whole = [zero, start, one, two, end, zero]
    columns = (
        ([one, two, end, zero, zero, zero], whole),
        (whole, [zero, zero, zero, start, one, two]),
    )
    rows = pl.ds(pl.multiple_of(t * 384, 384), 384)
    for g in range(2):
        for c in range(2):
            block = jnp.concatenate(columns[g][c], axis=0).astype(BF16)
            pair_ref[g, rows, 128 * c : 128 * c + 128] = block


def build_weights(w_ref, forward_ref, adjoint_ref):
    def tap(t, carry):
        rows = w_ref[pl.ds(pl.multiple_of(t * 192, 192), 192), :].astype(F32)
        lower, middle, upper = rows[:64], rows[64:128], rows[128:]
        toeplitz(
            jnp.concatenate([middle, lower], axis=1),
            jnp.concatenate([upper, middle], axis=1),
            forward_ref,
            t,
        )
        toeplitz(rows[64:192].T, rows[0:128].T, adjoint_ref, 8 - t)
        return carry

    lax.fori_loop(0, 9, tap, 0)


def conv(source, pair_ref, g, start, count, pitch):
    lanes = slice(128 * g, 128 * g + 384)
    parts = [
        source[oy, start + ox * pitch : start + ox * pitch + count, lanes]
        for ox in range(3)
        for oy in range(3)
    ]
    return jnp.dot(
        jnp.concatenate(parts, axis=1), pair_ref[g], preferred_element_type=F32
    )


def shifted(value):
    count = value.shape[0]
    return (pltpu.roll(value, 1, 0), value, pltpu.roll(value, count - 1, 0))


def fold(results, fold_ref, t0):
    for oy in range(3):
        sums = {}
        for g in range(2):
            for z in range(4 * g, 4 * g + 4):
                for c in range(3):
                    kind = (z % 2, 2 * g + 2 * c - z)
                    if kind in ((0, 0), (0, -2), (1, -1), (1, 1)):
                        zo = z - 4 * g
                        block = results[g][
                            64 * zo : 64 * zo + 64,
                            384 * oy + 128 * c : 384 * oy + 128 * c + 128,
                        ]
                        sums[kind] = sums[kind] + block if kind in sums else block
        p, u, q, s = sums[0, 0], sums[0, -2], sums[1, -1], sums[1, 1]
        first = lane(p.shape) < 64
        fold_ref[t0 + oy] = q + turned(jnp.where(first, p, u))
        fold_ref[9 + t0 + oy] = p + turned(s)


def weight_sums(errors_t, source, start, count, pitch, fold_ref, block_ref):
    def column(ox, carry):
        base = pl.multiple_of(start + ox * pitch, 16)
        results = []
        for g in range(2):
            lanes = slice(128 * g, 128 * g + 384)
            window = jnp.concatenate(
                [source[oy, pl.ds(base, count), lanes] for oy in range(3)], axis=1
            )
            results.append(
                jnp.dot(errors_t[g], window, preferred_element_type=F32)
            )
        fold(results, fold_ref, 3 * ox)
        return carry

    lax.fori_loop(0, 3, column, 0)
    first = lane((64, 128)) < 64
    for t in range(9):
        block_ref[t] = fold_ref[t].astype(BF16)
    for i in range(5):
        even = turned(fold_ref[9 + 2 * i])
        odd = fold_ref[10 + 2 * i] if i < 4 else jnp.zeros_like(even)
        block_ref[9 + i] = jnp.where(first, even, odd).astype(BF16)
    block_ref[14] = jnp.zeros((64, 128), BF16)
    block_ref[15] = jnp.zeros((64, 128), BF16)


def unfold(blocks_ref, per, out_ref, factor):
    for t in range(9):
        block = blocks_ref[t // per, t % per].astype(F32) * factor
        out_ref[192 * t : 192 * t + 128, :] = block.T
    for i in range(5):
        block = (blocks_ref[(9 + i) // per, (9 + i) % per].astype(F32) * factor).T
        out_ref[384 * i + 128 : 384 * i + 192, :] = block[:64]
        if i < 4:
            out_ref[384 * i + 320 : 384 * i + 384, :] = block[64:]


def block_kernel(
    n_gx,
    n_gy,
    feat,
    bounds,
    cot,
    low,
    high,
    w_one,
    w_two,
    par,
    out,
    gfeat,
    gw_one,
    gw_two,
    ext,
    elh,
    pick_in,
    pick_bounds,
    pick_target,
    put_out,
    put_grad,
    src_one,
    src_two,
    err_two,
    err_one,
    msk,
    core_in,
    core_mask,
    target,
    slope,
    frame,
    res,
    grad_region,
    gsum,
    fwd_one,
    adj_one,
    fwd_two,
    adj_two,
    folded,
    blocks,
    got_x,
    half,
    got_y,
    full,
    out_x,
    in_x,
    out_y,
    in_y,
    out_c,
    in_c,
    local_sem,
    halo_send,
    halo_recv,
    edge_send,
    edge_recv,
    sum_send,
    sum_recv,
):
    comm = n_gx * n_gy > 1
    if comm:
        gx, gy = lax.axis_index("gx"), lax.axis_index("gy")
    else:
        gx, gy = 0, 0
    nx, ny = feat.shape[0], feat.shape[1]
    per = BLOCKS // n_gx

    def device(dx, dy):
        return (lax.rem(gx + dx + n_gx, n_gx), lax.rem(gy + dy + n_gy, n_gy))

    if comm:
        barrier = pltpu.get_barrier_semaphore()
        peers = [(d, 0) for d in range(1, n_gx)] + [(0, d) for d in range(1, n_gy)]
        peers += [(dx, dy) for dx, dy in HALOS if dx and dy]
        for dx, dy in peers:
            pl.semaphore_signal(
                barrier, inc=1, device_id=device(dx, dy), device_id_type=MESH
            )
        pl.semaphore_wait(barrier, len(peers))

    def remote(src, dst, send, recv, to):
        return pltpu.make_async_remote_copy(
            src_ref=src,
            dst_ref=dst,
            send_sem=send,
            recv_sem=recv,
            device_id=to,
            device_id_type=MESH,
        )

    halos = []
    if comm:
        x_from = {-1: slice(0, 2), 0: slice(0, nx), 1: slice(nx - 2, nx)}
        x_to = {-1: slice(nx + 2, nx + 4), 0: slice(2, nx + 2), 1: slice(0, 2)}
        y_from = {-1: slice(0, 16), 0: slice(0, ny), 1: slice(ny - 16, ny)}
        y_to = {-1: slice(ny + 16, ny + 32), 0: slice(16, ny + 16), 1: slice(0, 16)}
        order = sorted(HALOS, key=lambda h: -(2 * abs(h[0]) - abs(h[1])))
        for i, (dx, dy) in enumerate(order):
            for k, (src, dst) in enumerate(((feat, ext), (bounds, elh))):
                copy = remote(
                    src.at[x_from[dx], y_from[dy]],
                    dst.at[x_to[dx], y_to[dy]],
                    halo_send.at[k, i],
                    halo_recv.at[k, i],
                    device(dx, dy),
                )
                copy.start()
                halos.append(copy)
    own = [
        pltpu.make_async_copy(
            src, dst.at[2 : nx + 2, 16 : ny + 16], local_sem.at[k]
        )
        for k, (src, dst) in enumerate(((feat, ext), (bounds, elh)))
    ]
    for copy in own:
        copy.start()

    build_weights(w_one, fwd_one, adj_one)
    build_weights(w_two, fwd_two, adj_two)
    nothing = jnp.zeros((3, 2 * ROWS, WIDTH), BF16)
    err_two[:, 0 : 2 * ROWS, :] = nothing
    err_two[:, 10 * ROWS : 12 * ROWS, :] = nothing
    err_one[:, 0 : 2 * ROWS, :] = nothing
    err_one[:, 12 * ROWS : 14 * ROWS, :] = nothing
    frame[...] = jnp.zeros_like(frame)

    occupied = jnp.where(high[...] > low[...], 1, 0)
    by_lane = lane((8, ny))
    count = jnp.int32(0)
    brick = [jnp.int32(-1000)] * SLOTS
    for bx in range(BX):
        rows = occupied[8 * bx : 8 * bx + 8]
        for by in range(BY):
            inside = (by_lane >= 8 * by) & (by_lane < 8 * by + 8)
            filled = jnp.max(jnp.where(inside, rows, 0))
            for j in range(SLOTS):
                hit = (filled > 0) & (count == j)
                brick[j] = jnp.where(hit, 8 * bx + by, brick[j])
            count = count + filled

    def picks(rows, columns, row_dim, per_brick, pitch, offset):
        shape = (rows, columns) if row_dim == 0 else (columns, rows)
        row = lax.broadcasted_iota(jnp.int32, shape, row_dim)
        column = lax.broadcasted_iota(jnp.int32, shape, 1 - row_dim)
        wanted = row + offset
        for j in range(SLOTS):
            b = brick[j]
            bx = jnp.where(b >= BY, 1, 0)
            spot = jnp.where(b < 0, -4000, bx * pitch + 8 * (b - BY * bx)) - per_brick * j
            inside = (row >= per_brick * j) & (row < per_brick * j + per_brick)
            wanted = wanted + jnp.where(inside, spot, 0)
        return jnp.where(column == wanted, 1.0, 0.0).astype(BF16)

    tall = ny + 32
    core_pick = picks(CORE, 2 * tall, 0, BRICK, tall, 16)
    frame_pick = [picks(ROWS, 2 * tall, 0, W, tall, 13 + oy) for oy in range(3)]
    pick_in[...] = jnp.concatenate(frame_pick + [core_pick], axis=0)
    pick_bounds[...] = jnp.concatenate([frame_pick[1], core_pick], axis=0)
    pick_target[...] = picks(CORE, 2 * ny, 0, BRICK, ny, 0)
    put_out[...] = picks(CORE, 2 * ny, 1, BRICK, ny, 0)
    put_grad[...] = picks(ROWS, 2 * (ny + 16), 1, W, ny + 16, 6)

    def cut_target(x, carry):
        rows = jnp.concatenate([cot[x], cot[8 + x]], axis=0)
        spot = pl.ds(pl.multiple_of(x * CORE, CORE), CORE)
        target[spot, :] = jnp.dot(pick_target[...], rows, preferred_element_type=F32)
        return carry

    lax.fori_loop(0, 8, cut_target, 0)

    def mask_in(x, y0, n):
        mask = height_mask(elh[x, y0 : y0 + n, :].astype(F32))
        for c in range(4):
            lanes = slice(128 * c, 128 * c + 128)
            value = ext[x, y0 : y0 + n, lanes].astype(F32)
            ext[x, y0 : y0 + n, lanes] = jnp.where(mask[c], value, 0.0).astype(BF16)

    def mask_rows(*spots):
        def one(x, carry):
            for y0, n in spots:
                mask_in(x, y0, n)
            return carry

        return one

    for copy in own:
        copy.wait()
    lax.fori_loop(2, nx + 2, mask_rows((16, ny)), 0)
    for copy in halos:
        copy.wait()
    if comm:
        for spot, inside in (
            ((slice(0, 2), slice(None)), gx > 0),
            ((slice(nx + 2, nx + 4), slice(None)), gx < n_gx - 1),
            ((slice(None), slice(0, 16)), gy > 0),
            ((slice(None), slice(ny + 16, ny + 32)), gy < n_gy - 1),
        ):
            value = elh[spot[0], spot[1], :].astype(F32)
            elh[spot[0], spot[1], :] = (
                value * jnp.where(inside, 1.0, 0.0).astype(F32)
            ).astype(BF16)
    else:
        for spot in (slice(0, 2), slice(nx + 2, nx + 4)):
            elh[spot] = jnp.zeros_like(elh[spot])
            ext[spot] = jnp.zeros_like(ext[spot])
        for spot in (slice(0, 16), slice(ny + 16, ny + 32)):
            elh[:, spot] = jnp.zeros_like(elh[:, spot])
            ext[:, spot] = jnp.zeros_like(ext[:, spot])

    lax.fori_loop(2, nx + 2, mask_rows((0, 16), (ny + 16, 16)), 0)
    for x in (0, nx + 2):
        lax.fori_loop(x, x + 2, mask_rows((0, tall)), 0)

    def cut(x, carry):
        base = pl.multiple_of(x * ROWS, ROWS)
        core = pl.multiple_of(x * CORE, CORE)
        rows = jnp.concatenate([ext[x], ext[8 + x]], axis=0)
        value = jnp.dot(pick_in[...], rows, preferred_element_type=F32)
        for oy in range(3):
            src_one[oy, pl.ds(base, ROWS), :] = value[
                ROWS * oy : ROWS * oy + ROWS
            ].astype(BF16)
        core_in[pl.ds(core, CORE), :] = value[3 * ROWS :]
        rows = jnp.concatenate([elh[x], elh[8 + x]], axis=0)
        mask = height_mask(
            jnp.dot(pick_bounds[...], rows, preferred_element_type=F32)
        )
        for c in range(4):
            lanes = slice(128 * c, 128 * c + 128)
            value = jnp.where(mask[c], 1.0, 0.0)
            msk[pl.ds(base, ROWS), lanes] = value[:ROWS]
            core_mask[pl.ds(core, CORE), lanes] = value[ROWS:]
        return carry

    lax.fori_loop(0, W, cut, 0)

    scale_one, shift_one = par[0:1, :], par[1:2, :]
    scale_two, shift_two = par[2:3, :], par[3:4, :]

    for g in range(2):
        lanes = slice(256 * g, 256 * g + 256)
        pre = conv(src_one, fwd_one, g, 0, 10 * ROWS, ROWS) * scale_one + shift_one
        s = jax.nn.sigmoid(pre)
        mask = msk[ROWS : 11 * ROWS, lanes]
        hidden = pre * s * mask
        slope[:, lanes] = s * (1.0 + pre * (1.0 - s)) * mask * scale_one
        for x in range(10):
            rows = hidden[ROWS * x : ROWS * x + ROWS]
            for oy in range(3):
                for j in range(0, SLOTS, 2):
                    both = [
                        rows[W * i + 1 + oy : W * i + 9 + oy] for i in (j, j + 1)
                    ]
                    src_two[oy, CORE * x + 8 * j : CORE * x + 8 * j + 16, lanes] = (
                        jnp.concatenate(both, axis=0).astype(BF16)
                    )

    middle = slice(2 * CORE, 10 * CORE)
    errors_t = []
    for g in range(2):
        lanes = slice(256 * g, 256 * g + 256)
        pre = conv(src_two, fwd_two, g, 0, 8 * CORE, CORE) * scale_two + shift_two
        pre = pre + core_in[middle, lanes]
        s = jax.nn.sigmoid(pre)
        mask = core_mask[middle, lanes]
        result = pre * s * mask
        grad = target[:, lanes] * mask * (s * (1.0 + pre * (1.0 - s)))
        errors_t.append((grad * scale_two).T.astype(BF16))
        res[:, lanes] = result.astype(BF16)
        for x in range(8):
            for j in range(SLOTS):
                spot = CORE * x + 8 * j
                frame[x, W * j + 2 : W * j + 10, lanes] = grad[spot : spot + 8]

    def spread(x, carry):
        base = pl.multiple_of((x + 2) * ROWS, ROWS)
        for g in range(2):
            lanes = slice(256 * g, 256 * g + 256)
            for oy, moved in enumerate(shifted(frame[x, :, lanes] * scale_two)):
                err_two[oy, pl.ds(base, ROWS), lanes] = moved.astype(BF16)
        return carry

    lax.fori_loop(0, 8, spread, 0)

    def exchange(conv_id):
        copies = []
        for d in range(1, n_gx):
            to = lax.rem(gx + d, n_gx)
            copy = remote(
                blocks.at[conv_id, pl.ds(to * per, per)],
                got_x.at[conv_id, gx],
                sum_send.at[conv_id, 0, d],
                sum_recv.at[conv_id, 0, d],
                (to, gy),
            )
            copy.start()
            copies.append(copy)
        got_x[conv_id, gx] = blocks[conv_id, pl.ds(gx * per, per)]
        return copies

    def add_up(conv_id, copies, source, where, n):
        for copy in copies:
            copy.wait_recv()
        total = source[conv_id, 0].astype(F32)
        for s in range(1, n):
            total = total + source[conv_id, s].astype(F32)
        where[conv_id] = total.astype(BF16)
        return copies

    def exchange_y(conv_id):
        copies = []
        for d in range(1, n_gy):
            copy = remote(
                half.at[0, conv_id],
                got_y.at[conv_id, gy],
                sum_send.at[conv_id, 1, d],
                sum_recv.at[conv_id, 1, d],
                (gx, lax.rem(gy + d, n_gy)),
            )
            copy.start()
            copies.append(copy)
        got_y[conv_id, gy] = half[0, conv_id]
        return copies

    def gather(conv_id):
        copies = []
        for d in range(1, n_gx):
            copy = remote(
                half.at[1, conv_id],
                full.at[conv_id, gx],
                sum_send.at[conv_id, 2, d],
                sum_recv.at[conv_id, 2, d],
                (lax.rem(gx + d, n_gx), gy),
            )
            copy.start()
            copies.append(copy)
        full[conv_id, gx] = half[1, conv_id]
        return copies

    weight_sums(
        errors_t, src_two, 0, 8 * CORE, CORE, folded, blocks.at[1]
    )
    sent_two = exchange(1)

    errors_t = []
    for g in range(2):
        lanes = slice(256 * g, 256 * g + 256)
        back = conv(err_two, adj_two, g, 0, 10 * ROWS, ROWS)
        error = back * slope[:, lanes]
        errors_t.append(error.T.astype(BF16))
        for x in range(10):
            rows = error[ROWS * x : ROWS * x + ROWS]
            spot = slice(ROWS * (x + 2), ROWS * (x + 3))
            for oy, moved in enumerate(shifted(rows)):
                err_one[oy, spot, lanes] = moved.astype(BF16)
    weight_sums(errors_t, src_one, 0, 10 * ROWS, ROWS, folded, blocks.at[0])
    sent_one = exchange(0)
    add_up(1, sent_two, got_x, half.at[0], n_gx)
    sent_two_y = exchange_y(1)

    for g in range(2):
        lanes = slice(256 * g, 256 * g + 256)
        back = conv(err_one, adj_one, g, 0, 12 * ROWS, ROWS)
        for x in range(W):
            rows = back[ROWS * x : ROWS * x + ROWS]
            if 2 <= x < 10:
                rows = rows + frame[x - 2, :, lanes]
            grad_region[x, :, lanes] = rows.astype(BF16)

    add_up(0, sent_one, got_x, half.at[0], n_gx)
    sent_one_y = exchange_y(0)
    add_up(1, sent_two_y, got_y, half.at[1], n_gy)
    sent_two_full = gather(1)

    for bxs, start, stop in (((0,), 0, 8), ((0, 1), 8, W), ((1,), W, 20)):

        def collect(x, carry, bxs=bxs):
            total = None
            for bx in bxs:
                part = jnp.dot(
                    put_grad[bx * (ny + 16) : (bx + 1) * (ny + 16), :],
                    grad_region[x - 8 * bx],
                    preferred_element_type=F32,
                )
                total = part if total is None else total + part
            gsum[x] = total
            return carry

        lax.fori_loop(start, stop, collect, 0)

    edges = []
    if comm:
        out_x[0] = gsum[0:2, 8 : ny + 8, :].astype(BF16)
        out_x[1] = gsum[nx + 2 : nx + 4, 8 : ny + 8, :].astype(BF16)
        for side, t in enumerate((0, ny + 8)):
            for i in range(nx // 2):
                both = [gsum[2 + 2 * i + k, t : t + 8, :] for k in range(2)]
                out_y[side, i] = jnp.concatenate(both, axis=0).astype(BF16)
            for up, x in enumerate((0, nx + 2)):
                both = [gsum[x + k, t : t + 8, :] for k in range(2)]
                out_c[up, side] = jnp.concatenate(both, axis=0).astype(BF16)
        for i, (dx, dy) in enumerate(HALOS):
            a, b = (dx + 1) // 2, (dy + 1) // 2
            if dy == 0:
                src, dst = out_x.at[a], in_x.at[1 - a]
            elif dx == 0:
                src, dst = out_y.at[b], in_y.at[1 - b]
            else:
                src, dst = out_c.at[a, b], in_c.at[1 - a, 1 - b]
            copy = remote(
                src, dst, edge_send.at[i], edge_recv.at[i], device(dx, dy)
            )
            copy.start()
            edges.append(copy)

    def deposit(x, carry):
        rows = res[pl.ds(pl.multiple_of(x * CORE, CORE), CORE), :]
        value = jnp.dot(put_out[...], rows, preferred_element_type=F32).astype(BF16)
        out[x] = value[:ny]
        out[8 + x] = value[ny:]
        return carry

    lax.fori_loop(0, 8, deposit, 0)

    add_up(0, sent_one_y, got_y, half.at[1], n_gy)
    sent_one_full = gather(0)

    if comm:
        for copy in edges:
            copy.wait_recv()
        x_in = [
            jnp.where(inside, 1.0, 0.0).astype(F32)
            for inside in (gx > 0, gx < n_gx - 1)
        ]
        y_in = [
            jnp.where(inside, 1.0, 0.0).astype(F32)
            for inside in (gy > 0, gy < n_gy - 1)
        ]
        for a, x in enumerate((2, nx)):
            gsum[x : x + 2, 8 : ny + 8, :] += in_x[a].astype(F32) * x_in[a]
            for b, t in enumerate((8, ny)):
                rows = in_c[a, b].astype(F32) * (x_in[a] * y_in[b])
                for k in range(2):
                    gsum[x + k, t : t + 8, :] += rows[8 * k : 8 * k + 8]
        for b, t in enumerate((8, ny)):
            for i in range(nx // 2):
                rows = in_y[b, i].astype(F32) * y_in[b]
                for k in range(2):
                    gsum[2 + 2 * i + k, t : t + 8, :] += rows[8 * k : 8 * k + 8]

    def finish(x, carry):
        mask = height_mask(elh[x + 2, 16 : ny + 16, :].astype(F32))
        for c in range(4):
            lanes = slice(128 * c, 128 * c + 128)
            value = gsum[x + 2, 8 : ny + 8, lanes]
            gfeat[x, :, lanes] = jnp.where(mask[c], value, 0.0).astype(BF16)
        return carry

    lax.fori_loop(0, nx, finish, 0)

    for conv_id, copies, gw in ((1, sent_two_full, gw_two), (0, sent_one_full, gw_one)):
        for copy in copies:
            copy.wait_recv()
        unfold(full.at[conv_id], per, gw, 1.0 / (n_gx * n_gy * SHARE))
    for copies in (
        edges,
        sent_one,
        sent_two,
        sent_one_y,
        sent_two_y,
        sent_one_full,
        sent_two_full,
    ):
        for copy in copies:
            copy.wait_send()


def run(
    n_gx,
    n_gy,
    features,
    cotangent,
    low,
    high,
    weight_one,
    weight_two,
    scale_one,
    shift_one,
    scale_two,
    shift_two,
):
    nx, ny = features.shape[0], features.shape[1]
    per = BLOCKS // n_gx
    first = lax.broadcasted_iota(jnp.int32, (nx, ny, 128), 2) < 64
    bounds = jnp.where(first, low[..., None], high[..., None]).astype(BF16)
    par = jnp.stack(
        [jnp.tile(v, 4) for v in (scale_one, shift_one, scale_two, shift_two)]
    )
    whole = pl.BlockSpec(memory_space=pltpu.VMEM)
    left = pl.BlockSpec(memory_space=pl.ANY)
    vm = pltpu.VMEM
    dma = pltpu.SemaphoreType.DMA
    scratch = [
        vm((nx + 4, ny + 32, WIDTH), BF16),
        vm((nx + 4, ny + 32, 128), BF16),
        vm((3 * ROWS + CORE, 2 * ny + 64), BF16),
        vm((ROWS + CORE, 2 * ny + 64), BF16),
        vm((CORE, 2 * ny), BF16),
        vm((2 * ny, CORE), BF16),
        vm((2 * ny + 32, ROWS), BF16),
        vm((3, W * ROWS, WIDTH), BF16),
        vm((3, 10 * CORE, WIDTH), BF16),
        vm((3, W * ROWS, WIDTH), BF16),
        vm((3, (W + 2) * ROWS, WIDTH), BF16),
        vm((W * ROWS, WIDTH), F32),
        vm((W * CORE, WIDTH), F32),
        vm((W * CORE, WIDTH), F32),
        vm((8 * CORE, WIDTH), F32),
        vm((10 * ROWS, WIDTH), F32),
        vm((8, ROWS, WIDTH), F32),
        vm((8 * CORE, WIDTH), BF16),
        vm((W, ROWS, WIDTH), BF16),
        vm((nx + 4, ny + 16, WIDTH), F32),
        vm((2, 27 * 128, 256), BF16),
        vm((2, 27 * 128, 256), BF16),
        vm((2, 27 * 128, 256), BF16),
        vm((2, 27 * 128, 256), BF16),
        vm((18, 64, 128), F32),
        vm((2, BLOCKS, 64, 128), BF16),
        vm((2, n_gx, per, 64, 128), BF16),
        vm((2, 2, per, 64, 128), BF16),
        vm((2, n_gy, per, 64, 128), BF16),
        vm((2, n_gx, per, 64, 128), BF16),
        vm((2, 2, ny, WIDTH), BF16),
        vm((2, 2, ny, WIDTH), BF16),
        vm((2, nx // 2, 16, WIDTH), BF16),
        vm((2, nx // 2, 16, WIDTH), BF16),
        vm((2, 2, 16, WIDTH), BF16),
        vm((2, 2, 16, WIDTH), BF16),
        dma((2,)),
        dma((2, 8)),
        dma((2, 8)),
        dma((8,)),
        dma((8,)),
        dma((2, 3, 16)),
        dma((2, 3, 16)),
    ]
    comm = n_gx * n_gy > 1
    params = pltpu.CompilerParams(
        collective_id=0 if comm else None,
        has_side_effects=comm,
        vmem_limit_bytes=60 * 2**20,
    )
    out, gfeat, gw_one, gw_two = pl.pallas_call(
        functools.partial(block_kernel, n_gx, n_gy),
        out_shape=(
            jax.ShapeDtypeStruct(features.shape, BF16),
            jax.ShapeDtypeStruct(features.shape, BF16),
            jax.ShapeDtypeStruct((27 * C, C), F32),
            jax.ShapeDtypeStruct((27 * C, C), F32),
        ),
        in_specs=[left, left] + [whole] * 6,
        out_specs=(whole,) * 4,
        scratch_shapes=scratch,
        compiler_params=params,
        name="residual_block",
    )(
        features,
        bounds,
        cotangent,
        low,
        high,
        weight_one.reshape(27 * C, C),
        weight_two.reshape(27 * C, C),
        par,
    )
    return out, gfeat, gw_one.reshape(27, C, C), gw_two.reshape(27, C, C)


def solution(mesh):
    columns = P("gx", "gy", None)
    placed = (columns, columns, P("gx", "gy"), P("gx", "gy")) + (P(),) * 6
    return jax.shard_map(
        functools.partial(run, mesh.shape["gx"], mesh.shape["gy"]),
        mesh=mesh,
        in_specs=placed,
        out_specs=(columns, columns, P(), P()),
        check_vma=False,
    )
```

```python
import functools

import jax
import jax.numpy as jnp
from jax import lax
from jax.experimental import pallas as pl
from jax.experimental.pallas import tpu as pltpu
from jax.sharding import PartitionSpec as P

MESH = pl.DeviceIdType.MESH
F32 = jnp.float32
BF16 = jnp.bfloat16
BRICK = 8
C = 64
WIDTH = 512
SLOTS = 4
SHARE = 2
BX, BY = 2, 8
W = 12
ROWS = SLOTS * W
CORE = SLOTS * BRICK
BLOCKS = 16
HALOS = [(dx, dy) for dx in (-1, 0, 1) for dy in (-1, 0, 1) if dx or dy]


def lane(shape):
    return lax.broadcasted_iota(jnp.int32, shape, len(shape) - 1)


def turned(value):
    return pltpu.roll(value, 64, value.ndim - 1)


def height_mask(bounds):
    first = lane(bounds.shape) < 64
    other = turned(bounds)
    low, high = jnp.where(first, bounds, other), jnp.where(first, other, bounds)
    step = jnp.where(first, 0.0, 1.0)
    return [(step + 2.0 * c >= low) & (step + 2.0 * c < high) for c in range(4)]


def toeplitz(one, two, pair_ref, t):
    first = lane(one.shape) < 64
    zero = jnp.zeros_like(one)
    start = jnp.where(first, turned(one), zero)
    end = jnp.where(first, zero, turned(two))
    whole = [zero, start, one, two, end, zero]
    columns = (
        ([one, two, end, zero, zero, zero], whole),
        (whole, [zero, zero, zero, start, one, two]),
    )
    rows = pl.ds(pl.multiple_of(t * 384, 384), 384)
    for g in range(2):
        for c in range(2):
            block = jnp.concatenate(columns[g][c], axis=0).astype(BF16)
            pair_ref[g, rows, 128 * c : 128 * c + 128] = block


def build_weights(w_ref, forward_ref, adjoint_ref):
    def tap(t, carry):
        rows = w_ref[pl.ds(pl.multiple_of(t * 192, 192), 192), :].astype(F32)
        lower, middle, upper = rows[:64], rows[64:128], rows[128:]
        toeplitz(
            jnp.concatenate([middle, lower], axis=1),
            jnp.concatenate([upper, middle], axis=1),
            forward_ref,
            t,
        )
        toeplitz(rows[64:192].T, rows[0:128].T, adjoint_ref, 8 - t)
        return carry

    lax.fori_loop(0, 9, tap, 0)


def conv(source, pair_ref, g, start, count, pitch):
    lanes = slice(128 * g, 128 * g + 384)
    parts = [
        source[oy, start + ox * pitch : start + ox * pitch + count, lanes]
        for ox in range(3)
        for oy in range(3)
    ]
    return jnp.dot(
        jnp.concatenate(parts, axis=1), pair_ref[g], preferred_element_type=F32
    )


def shifted(value):
    count = value.shape[0]
    return (pltpu.roll(value, 1, 0), value, pltpu.roll(value, count - 1, 0))


def fold(results, fold_ref, t0):
    for oy in range(3):
        sums = {}
        for g in range(2):
            for z in range(4 * g, 4 * g + 4):
                for c in range(3):
                    kind = (z % 2, 2 * g + 2 * c - z)
                    if kind in ((0, 0), (0, -2), (1, -1), (1, 1)):
                        zo = z - 4 * g
                        block = results[g][
                            64 * zo : 64 * zo + 64,
                            384 * oy + 128 * c : 384 * oy + 128 * c + 128,
                        ]
                        sums[kind] = sums[kind] + block if kind in sums else block
        p, u, q, s = sums[0, 0], sums[0, -2], sums[1, -1], sums[1, 1]
        first = lane(p.shape) < 64
        fold_ref[t0 + oy] = q + turned(jnp.where(first, p, u))
        fold_ref[9 + t0 + oy] = p + turned(s)


def weight_sums(errors_t, source, start, count, pitch, fold_ref, block_ref):
    def column(ox, carry):
        base = pl.multiple_of(start + ox * pitch, 16)
        results = []
        for g in range(2):
            lanes = slice(128 * g, 128 * g + 384)
            window = jnp.concatenate(
                [source[oy, pl.ds(base, count), lanes] for oy in range(3)], axis=1
            )
            results.append(
                jnp.dot(errors_t[g], window, preferred_element_type=F32)
            )
        fold(results, fold_ref, 3 * ox)
        return carry

    lax.fori_loop(0, 3, column, 0)
    first = lane((64, 128)) < 64
    for t in range(9):
        block_ref[t] = fold_ref[t].astype(BF16)
    for i in range(5):
        even = turned(fold_ref[9 + 2 * i])
        odd = fold_ref[10 + 2 * i] if i < 4 else jnp.zeros_like(even)
        block_ref[9 + i] = jnp.where(first, even, odd).astype(BF16)
    block_ref[14] = jnp.zeros((64, 128), BF16)
    block_ref[15] = jnp.zeros((64, 128), BF16)


def unfold(blocks_ref, per, out_ref, factor):
    for t in range(9):
        block = blocks_ref[t // per, t % per].astype(F32) * factor
        out_ref[192 * t : 192 * t + 128, :] = block.T
    for i in range(5):
        block = (blocks_ref[(9 + i) // per, (9 + i) % per].astype(F32) * factor).T
        out_ref[384 * i + 128 : 384 * i + 192, :] = block[:64]
        if i < 4:
            out_ref[384 * i + 320 : 384 * i + 384, :] = block[64:]


def block_kernel(
    n_gx,
    n_gy,
    feat,
    cot_in,
    w_one_in,
    w_two_in,
    low_in,
    high_in,
    scale_one_in,
    shift_one_in,
    scale_two_in,
    shift_two_in,
    out,
    gfeat,
    full,
    cot,
    w_one,
    w_two,
    low,
    high,
    scales,
    bounds,
    ext,
    elh,
    pick_in,
    pick_bounds,
    pick_target,
    put_out,
    put_grad,
    src_one,
    src_two,
    err_two,
    err_one,
    msk,
    core_in,
    core_mask,
    target,
    slope,
    frame,
    res,
    grad_region,
    gsum,
    fwd_one,
    adj_one,
    fwd_two,
    adj_two,
    folded,
    blocks,
    got_x,
    half,
    got_y,
    out_x,
    in_x,
    out_y,
    in_y,
    out_c,
    in_c,
    local_sem,
    halo_send,
    halo_recv,
    edge_send,
    edge_recv,
    sum_send,
    sum_recv,
):
    comm = n_gx * n_gy > 1
    if comm:
        gx, gy = lax.axis_index("gx"), lax.axis_index("gy")
    else:
        gx, gy = 0, 0
    nx, ny = feat.shape[0], feat.shape[1]
    per = BLOCKS // n_gx

    inputs = [
        pltpu.make_async_copy(src, dst, local_sem.at[2 + k])
        for k, (src, dst) in enumerate(
            ((w_one_in, w_one), (w_two_in, w_two), (cot_in, cot))
        )
    ]

    def device(dx, dy):
        return (lax.rem(gx + dx + n_gx, n_gx), lax.rem(gy + dy + n_gy, n_gy))

    if comm:
        barrier = pltpu.get_barrier_semaphore()
        peers = [(d, 0) for d in range(1, n_gx)] + [(0, d) for d in range(1, n_gy)]
        peers += [(dx, dy) for dx, dy in HALOS if dx and dy]
        for dx, dy in peers:
            pl.semaphore_signal(
                barrier, inc=1, device_id=device(dx, dy), device_id_type=MESH
            )

    own = pltpu.make_async_copy(
        feat, ext.at[2 : nx + 2, 16 : ny + 16], local_sem.at[0]
    )
    own.start()
    small = [
        pltpu.make_async_copy(src, dst, local_sem.at[5 + k])
        for k, (src, dst) in enumerate(
            (
                (low_in, low),
                (high_in, high),
                (scale_one_in, scales.at[0]),
                (shift_one_in, scales.at[1]),
                (scale_two_in, scales.at[2]),
                (shift_two_in, scales.at[3]),
            )
        )
    ]
    for copy in small + inputs:
        copy.start()
    for copy in small:
        copy.wait()

    first = lane((ny, 128)) < 64
    square = jnp.zeros((ny, ny), F32)
    lows = jnp.concatenate([low[...].astype(F32), square[nx:]], axis=0).T
    highs = jnp.concatenate([high[...].astype(F32), square[nx:]], axis=0).T
    for x in range(nx):
        both = jnp.where(first, lows[:, x : x + 1], highs[:, x : x + 1]).astype(BF16)
        bounds[x] = both
        elh[x + 2, 16 : ny + 16, :] = both
    if comm:
        pl.semaphore_wait(barrier, len(peers))

    def remote(src, dst, send, recv, to):
        return pltpu.make_async_remote_copy(
            src_ref=src,
            dst_ref=dst,
            send_sem=send,
            recv_sem=recv,
            device_id=to,
            device_id_type=MESH,
        )

    halos = []
    if comm:
        x_from = {-1: slice(0, 2), 0: slice(0, nx), 1: slice(nx - 2, nx)}
        x_to = {-1: slice(nx + 2, nx + 4), 0: slice(2, nx + 2), 1: slice(0, 2)}
        y_from = {-1: slice(0, 16), 0: slice(0, ny), 1: slice(ny - 16, ny)}
        y_to = {-1: slice(ny + 16, ny + 32), 0: slice(16, ny + 16), 1: slice(0, 16)}
        order = sorted(HALOS, key=lambda h: -(2 * abs(h[0]) - abs(h[1])))
        for i, (dx, dy) in enumerate(order):
            for k, (src, dst) in enumerate(((feat, ext), (bounds, elh))):
                copy = remote(
                    src.at[x_from[dx], y_from[dy]],
                    dst.at[x_to[dx], y_to[dy]],
                    halo_send.at[k, i],
                    halo_recv.at[k, i],
                    device(dx, dy),
                )
                copy.start()
                halos.append(copy)
    inputs[0].wait()
    build_weights(w_one, fwd_one, adj_one)
    inputs[1].wait()
    build_weights(w_two, fwd_two, adj_two)
    nothing = jnp.zeros((3, 2 * ROWS, WIDTH), BF16)
    err_two[:, 0 : 2 * ROWS, :] = nothing
    err_two[:, 10 * ROWS : 12 * ROWS, :] = nothing
    err_one[:, 0 : 2 * ROWS, :] = nothing
    err_one[:, 12 * ROWS : 14 * ROWS, :] = nothing
    frame[...] = jnp.zeros_like(frame)

    occupied = jnp.where(high[...] > low[...], 1, 0)
    by_lane = lane((8, ny))
    count = jnp.int32(0)
    brick = [jnp.int32(-1000)] * SLOTS
    for bx in range(BX):
        rows = occupied[8 * bx : 8 * bx + 8]
        for by in range(BY):
            inside = (by_lane >= 8 * by) & (by_lane < 8 * by + 8)
            filled = jnp.max(jnp.where(inside, rows, 0))
            for j in range(SLOTS):
                hit = (filled > 0) & (count == j)
                brick[j] = jnp.where(hit, 8 * bx + by, brick[j])
            count = count + filled

    def picks(rows, columns, row_dim, per_brick, pitch, offset):
        shape = (rows, columns) if row_dim == 0 else (columns, rows)
        row = lax.broadcasted_iota(jnp.int32, shape, row_dim)
        column = lax.broadcasted_iota(jnp.int32, shape, 1 - row_dim)
        wanted = row + offset
        for j in range(SLOTS):
            b = brick[j]
            bx = jnp.where(b >= BY, 1, 0)
            spot = jnp.where(b < 0, -4000, bx * pitch + 8 * (b - BY * bx)) - per_brick * j
            inside = (row >= per_brick * j) & (row < per_brick * j + per_brick)
            wanted = wanted + jnp.where(inside, spot, 0)
        return jnp.where(column == wanted, 1.0, 0.0).astype(BF16)

    tall = ny + 32
    core_pick = picks(CORE, 2 * tall, 0, BRICK, tall, 16)
    frame_pick = [picks(ROWS, 2 * tall, 0, W, tall, 13 + oy) for oy in range(3)]
    pick_in[...] = jnp.concatenate(frame_pick + [core_pick], axis=0)
    pick_bounds[...] = jnp.concatenate([frame_pick[1], core_pick], axis=0)
    pick_target[...] = picks(CORE, 2 * ny, 0, BRICK, ny, 0)
    put_out[...] = picks(CORE, 2 * ny, 1, BRICK, ny, 0)
    put_grad[...] = picks(ROWS, 2 * (ny + 16), 1, W, ny + 16, 6)

    inputs[2].wait()
    def cut_target(x, carry):
        rows = jnp.concatenate([cot[x], cot[8 + x]], axis=0)
        spot = pl.ds(pl.multiple_of(x * CORE, CORE), CORE)
        target[spot, :] = jnp.dot(pick_target[...], rows, preferred_element_type=F32)
        return carry

    lax.fori_loop(0, 8, cut_target, 0, unroll=8)

    def mask_in(xs, ys):
        mask = height_mask(elh[xs, ys, :].astype(F32))
        for c in range(4):
            lanes = slice(128 * c, 128 * c + 128)
            value = ext[xs, ys, lanes].astype(F32)
            ext[xs, ys, lanes] = jnp.where(mask[c], value, 0.0).astype(BF16)

    def mask_inner(i, carry):
        mask_in(pl.ds(2 + 2 * i, 2), slice(16, ny + 16))
        return carry

    own.wait()
    lax.fori_loop(0, nx // 2, mask_inner, 0, unroll=2)
    for copy in halos:
        copy.wait()
    if comm:
        for spot, inside in (
            ((slice(0, 2), slice(None)), gx > 0),
            ((slice(nx + 2, nx + 4), slice(None)), gx < n_gx - 1),
            ((slice(None), slice(0, 16)), gy > 0),
            ((slice(None), slice(ny + 16, ny + 32)), gy < n_gy - 1),
        ):
            value = elh[spot[0], spot[1], :].astype(F32)
            elh[spot[0], spot[1], :] = (
                value * jnp.where(inside, 1.0, 0.0).astype(F32)
            ).astype(BF16)
    else:
        for spot in (slice(0, 2), slice(nx + 2, nx + 4)):
            elh[spot] = jnp.zeros_like(elh[spot])
            ext[spot] = jnp.zeros_like(ext[spot])
        for spot in (slice(0, 16), slice(ny + 16, ny + 32)):
            elh[:, spot] = jnp.zeros_like(elh[:, spot])
            ext[:, spot] = jnp.zeros_like(ext[:, spot])

    for x in range(2, nx + 2, 4):
        mask_in(slice(x, x + 4), slice(0, 16))
        mask_in(slice(x, x + 4), slice(ny + 16, tall))
    for x in (0, 1, nx + 2, nx + 3):
        mask_in(slice(x, x + 1), slice(0, tall))

    def cut(x, carry):
        base = pl.multiple_of(x * ROWS, ROWS)
        core = pl.multiple_of(x * CORE, CORE)
        rows = jnp.concatenate([ext[x], ext[8 + x]], axis=0)
        value = jnp.dot(pick_in[...], rows, preferred_element_type=F32)
        for oy in range(3):
            src_one[oy, pl.ds(base, ROWS), :] = value[
                ROWS * oy : ROWS * oy + ROWS
            ].astype(BF16)
        core_in[pl.ds(core, CORE), :] = value[3 * ROWS :]
        rows = jnp.concatenate([elh[x], elh[8 + x]], axis=0)
        mask = height_mask(
            jnp.dot(pick_bounds[...], rows, preferred_element_type=F32)
        )
        for c in range(4):
            lanes = slice(128 * c, 128 * c + 128)
            value = jnp.where(mask[c], 1.0, 0.0)
            msk[pl.ds(base, ROWS), lanes] = value[:ROWS]
            core_mask[pl.ds(core, CORE), lanes] = value[ROWS:]
        return carry

    lax.fori_loop(0, W, cut, 0, unroll=4)

    scale_one, shift_one, scale_two, shift_two = (
        jnp.concatenate([scales[k]] * 4, axis=1) for k in range(4)
    )

    for g in range(2):
        lanes = slice(256 * g, 256 * g + 256)
        pre = conv(src_one, fwd_one, g, 0, 10 * ROWS, ROWS) * scale_one + shift_one
        s = jax.nn.sigmoid(pre)
        mask = msk[ROWS : 11 * ROWS, lanes]
        hidden = pre * s * mask
        slope[:, lanes] = s * (1.0 + pre * (1.0 - s)) * mask * scale_one
        for x in range(10):
            rows = hidden[ROWS * x : ROWS * x + ROWS]
            for oy in range(3):
                for j in range(0, SLOTS, 2):
                    both = [
                        rows[W * i + 1 + oy : W * i + 9 + oy] for i in (j, j + 1)
                    ]
                    src_two[oy, CORE * x + 8 * j : CORE * x + 8 * j + 16, lanes] = (
                        jnp.concatenate(both, axis=0).astype(BF16)
                    )

    middle = slice(2 * CORE, 10 * CORE)
    errors_t = []
    for g in range(2):
        lanes = slice(256 * g, 256 * g + 256)
        pre = conv(src_two, fwd_two, g, 0, 8 * CORE, CORE) * scale_two + shift_two
        pre = pre + core_in[middle, lanes]
        s = jax.nn.sigmoid(pre)
        mask = core_mask[middle, lanes]
        result = pre * s * mask
        grad = target[:, lanes] * mask * (s * (1.0 + pre * (1.0 - s)))
        errors_t.append((grad * scale_two).T.astype(BF16))
        res[:, lanes] = result.astype(BF16)
        for x in range(8):
            for j in range(SLOTS):
                spot = CORE * x + 8 * j
                frame[x, W * j + 2 : W * j + 10, lanes] = grad[spot : spot + 8]

    def spread(x, carry):
        base = pl.multiple_of((x + 2) * ROWS, ROWS)
        for g in range(2):
            lanes = slice(256 * g, 256 * g + 256)
            for oy, moved in enumerate(shifted(frame[x, :, lanes] * scale_two)):
                err_two[oy, pl.ds(base, ROWS), lanes] = moved.astype(BF16)
        return carry

    lax.fori_loop(0, 8, spread, 0, unroll=2)

    def exchange(conv_id):
        copies = []
        for d in range(1, n_gx):
            to = lax.rem(gx + d, n_gx)
            copy = remote(
                blocks.at[conv_id, pl.ds(to * per, per)],
                got_x.at[conv_id, gx],
                sum_send.at[conv_id, 0, d],
                sum_recv.at[conv_id, 0, d],
                (to, gy),
            )
            copy.start()
            copies.append(copy)
        got_x[conv_id, gx] = blocks[conv_id, pl.ds(gx * per, per)]
        return copies

    def add_up(conv_id, copies, source, where, n):
        for copy in copies:
            copy.wait_recv()
        total = source[conv_id, 0].astype(F32)
        for s in range(1, n):
            total = total + source[conv_id, s].astype(F32)
        where[conv_id] = total.astype(BF16)
        return copies

    def exchange_y(conv_id):
        copies = []
        for d in range(1, n_gy):
            copy = remote(
                half.at[0, conv_id],
                got_y.at[conv_id, gy],
                sum_send.at[conv_id, 1, d],
                sum_recv.at[conv_id, 1, d],
                (gx, lax.rem(gy + d, n_gy)),
            )
            copy.start()
            copies.append(copy)
        got_y[conv_id, gy] = half[0, conv_id]
        return copies

    def gather(conv_id):
        copies = []
        for d in range(1, n_gx):
            copy = remote(
                half.at[1, conv_id],
                full.at[conv_id, gx],
                sum_send.at[conv_id, 2, d],
                sum_recv.at[conv_id, 2, d],
                (lax.rem(gx + d, n_gx), gy),
            )
            copy.start()
            copies.append(copy)
        full[conv_id, gx] = half[1, conv_id]
        return copies

    weight_sums(
        errors_t, src_two, 0, 8 * CORE, CORE, folded, blocks.at[1]
    )
    sent_two = exchange(1)

    errors_t = []
    for g in range(2):
        lanes = slice(256 * g, 256 * g + 256)
        back = conv(err_two, adj_two, g, 0, 10 * ROWS, ROWS)
        error = back * slope[:, lanes]
        errors_t.append(error.T.astype(BF16))
        for x in range(10):
            rows = error[ROWS * x : ROWS * x + ROWS]
            spot = slice(ROWS * (x + 2), ROWS * (x + 3))
            for oy, moved in enumerate(shifted(rows)):
                err_one[oy, spot, lanes] = moved.astype(BF16)
    weight_sums(errors_t, src_one, 0, 10 * ROWS, ROWS, folded, blocks.at[0])
    sent_one = exchange(0)
    add_up(1, sent_two, got_x, half.at[0], n_gx)
    sent_two_y = exchange_y(1)

    for g in range(2):
        lanes = slice(256 * g, 256 * g + 256)
        back = conv(err_one, adj_one, g, 0, 12 * ROWS, ROWS)
        for x in range(W):
            rows = back[ROWS * x : ROWS * x + ROWS]
            if 2 <= x < 10:
                rows = rows + frame[x - 2, :, lanes]
            grad_region[x, :, lanes] = rows.astype(BF16)

    add_up(0, sent_one, got_x, half.at[0], n_gx)
    sent_one_y = exchange_y(0)
    add_up(1, sent_two_y, got_y, half.at[1], n_gy)
    sent_two_full = gather(1)

    for bxs, start, stop in (((0,), 0, 8), ((0, 1), 8, W), ((1,), W, 20)):

        def collect(x, carry, bxs=bxs):
            total = None
            for bx in bxs:
                part = jnp.dot(
                    put_grad[bx * (ny + 16) : (bx + 1) * (ny + 16), :],
                    grad_region[x - 8 * bx],
                    preferred_element_type=F32,
                )
                total = part if total is None else total + part
            gsum[x] = total
            return carry

        lax.fori_loop(start, stop, collect, 0, unroll=4)

    edges = []
    if comm:
        out_x[0] = gsum[0:2, 8 : ny + 8, :].astype(BF16)
        out_x[1] = gsum[nx + 2 : nx + 4, 8 : ny + 8, :].astype(BF16)
        for side, t in enumerate((0, ny + 8)):
            for i in range(nx // 2):
                both = [gsum[2 + 2 * i + k, t : t + 8, :] for k in range(2)]
                out_y[side, i] = jnp.concatenate(both, axis=0).astype(BF16)
            for up, x in enumerate((0, nx + 2)):
                both = [gsum[x + k, t : t + 8, :] for k in range(2)]
                out_c[up, side] = jnp.concatenate(both, axis=0).astype(BF16)
        for i, (dx, dy) in enumerate(HALOS):
            a, b = (dx + 1) // 2, (dy + 1) // 2
            if dy == 0:
                src, dst = out_x.at[a], in_x.at[1 - a]
            elif dx == 0:
                src, dst = out_y.at[b], in_y.at[1 - b]
            else:
                src, dst = out_c.at[a, b], in_c.at[1 - a, 1 - b]
            copy = remote(
                src, dst, edge_send.at[i], edge_recv.at[i], device(dx, dy)
            )
            copy.start()
            edges.append(copy)

    def deposit(x, carry):
        rows = res[pl.ds(pl.multiple_of(x * CORE, CORE), CORE), :]
        value = jnp.dot(put_out[...], rows, preferred_element_type=F32).astype(BF16)
        out[x] = value[:ny]
        out[8 + x] = value[ny:]
        return carry

    lax.fori_loop(0, 8, deposit, 0, unroll=4)

    add_up(0, sent_one_y, got_y, half.at[1], n_gy)
    sent_one_full = gather(0)

    if comm:
        for copy in edges:
            copy.wait_recv()
        x_in = [
            jnp.where(inside, 1.0, 0.0).astype(F32)
            for inside in (gx > 0, gx < n_gx - 1)
        ]
        y_in = [
            jnp.where(inside, 1.0, 0.0).astype(F32)
            for inside in (gy > 0, gy < n_gy - 1)
        ]
        for a, x in enumerate((2, nx)):
            gsum[x : x + 2, 8 : ny + 8, :] += in_x[a].astype(F32) * x_in[a]
            for b, t in enumerate((8, ny)):
                rows = in_c[a, b].astype(F32) * (x_in[a] * y_in[b])
                for k in range(2):
                    gsum[x + k, t : t + 8, :] += rows[8 * k : 8 * k + 8]
        for b, t in enumerate((8, ny)):
            for i in range(nx // 2):
                rows = in_y[b, i].astype(F32) * y_in[b]
                for k in range(2):
                    gsum[2 + 2 * i + k, t : t + 8, :] += rows[8 * k : 8 * k + 8]

    def finish(x, carry):
        mask = height_mask(elh[x + 2, 16 : ny + 16, :].astype(F32))
        for c in range(4):
            lanes = slice(128 * c, 128 * c + 128)
            value = gsum[x + 2, 8 : ny + 8, lanes]
            gfeat[x, :, lanes] = jnp.where(mask[c], value, 0.0).astype(BF16)
        return carry

    lax.fori_loop(0, nx, finish, 0, unroll=4)

    for copies in (sent_two_full, sent_one_full):
        for copy in copies:
            copy.wait_recv()
    for copies in (
        edges,
        sent_one,
        sent_two,
        sent_one_y,
        sent_two_y,
        sent_one_full,
        sent_two_full,
    ):
        for copy in copies:
            copy.wait_send()


def result_kernel(
    factor, per, out_in, gfeat_in, full, out, gfeat, gw_one, gw_two, one, two, sem
):
    copies = [
        pltpu.make_async_copy(out_in, out, sem.at[0]),
        pltpu.make_async_copy(gfeat_in, gfeat, sem.at[1]),
    ]
    for copy in copies:
        copy.start()
    for k, (ref, gw) in enumerate(((one, gw_one), (two, gw_two))):
        unfold(full.at[k], per, ref, factor)
        copy = pltpu.make_async_copy(ref, gw, sem.at[2 + k])
        copy.start()
        copies.append(copy)
    for copy in copies:
        copy.wait()


def run(
    n_gx,
    n_gy,
    features,
    cotangent,
    low,
    high,
    weight_one,
    weight_two,
    scale_one,
    shift_one,
    scale_two,
    shift_two,
):
    nx, ny = features.shape[0], features.shape[1]
    per = BLOCKS // n_gx
    whole = pl.BlockSpec(memory_space=pltpu.VMEM)
    left = pl.BlockSpec(memory_space=pl.ANY)
    vm = pltpu.VMEM
    dma = pltpu.SemaphoreType.DMA
    scratch = [
        vm((nx, ny, WIDTH), BF16),
        vm((27 * C, C), BF16),
        vm((27 * C, C), BF16),
        vm((nx, ny), jnp.int32),
        vm((nx, ny), jnp.int32),
        vm((4, 1, C), F32),
        vm((nx, ny, 128), BF16),
        vm((nx + 4, ny + 32, WIDTH), BF16),
        vm((nx + 4, ny + 32, 128), BF16),
        vm((3 * ROWS + CORE, 2 * ny + 64), BF16),
        vm((ROWS + CORE, 2 * ny + 64), BF16),
        vm((CORE, 2 * ny), BF16),
        vm((2 * ny, CORE), BF16),
        vm((2 * ny + 32, ROWS), BF16),
        vm((3, W * ROWS, WIDTH), BF16),
        vm((3, 10 * CORE, WIDTH), BF16),
        vm((3, W * ROWS, WIDTH), BF16),
        vm((3, (W + 2) * ROWS, WIDTH), BF16),
        vm((W * ROWS, WIDTH), F32),
        vm((W * CORE, WIDTH), F32),
        vm((W * CORE, WIDTH), F32),
        vm((8 * CORE, WIDTH), F32),
        vm((10 * ROWS, WIDTH), F32),
        vm((8, ROWS, WIDTH), F32),
        vm((8 * CORE, WIDTH), BF16),
        vm((W, ROWS, WIDTH), BF16),
        vm((nx + 4, ny + 16, WIDTH), F32),
        vm((2, 27 * 128, 256), BF16),
        vm((2, 27 * 128, 256), BF16),
        vm((2, 27 * 128, 256), BF16),
        vm((2, 27 * 128, 256), BF16),
        vm((18, 64, 128), F32),
        vm((2, BLOCKS, 64, 128), BF16),
        vm((2, n_gx, per, 64, 128), BF16),
        vm((2, 2, per, 64, 128), BF16),
        vm((2, n_gy, per, 64, 128), BF16),
        vm((2, 2, ny, WIDTH), BF16),
        vm((2, 2, ny, WIDTH), BF16),
        vm((2, nx // 2, 16, WIDTH), BF16),
        vm((2, nx // 2, 16, WIDTH), BF16),
        vm((2, 2, 16, WIDTH), BF16),
        vm((2, 2, 16, WIDTH), BF16),
        dma((11,)),
        dma((2, 8)),
        dma((2, 8)),
        dma((8,)),
        dma((8,)),
        dma((2, 3, 16)),
        dma((2, 3, 16)),
    ]
    comm = n_gx * n_gy > 1
    params = pltpu.CompilerParams(
        collective_id=0 if comm else None,
        has_side_effects=comm,
        vmem_limit_bytes=46 * 2**20,
    )
    in_hbm = functools.partial(
        pltpu.with_memory_space_constraint, memory_space=pltpu.HBM
    )
    columns = jax.ShapeDtypeStruct(features.shape, BF16)
    out, gfeat, full = pl.pallas_call(
        functools.partial(block_kernel, n_gx, n_gy),
        out_shape=(
            columns,
            columns,
            jax.ShapeDtypeStruct((2, n_gx, per, 64, 128), BF16),
        ),
        in_specs=[pl.BlockSpec(memory_space=pltpu.HBM)] * 10,
        out_specs=(whole,) * 3,
        scratch_shapes=scratch,
        compiler_params=params,
        name="residual_block",
    )(
        in_hbm(features),
        in_hbm(cotangent),
        in_hbm(weight_one.reshape(27 * C, C)),
        in_hbm(weight_two.reshape(27 * C, C)),
        in_hbm(low),
        in_hbm(high),
        in_hbm(scale_one.reshape(1, C)),
        in_hbm(shift_one.reshape(1, C)),
        in_hbm(scale_two.reshape(1, C)),
        in_hbm(shift_two.reshape(1, C)),
    )
    sums = jax.ShapeDtypeStruct((27 * C, C), F32)
    out, gfeat, gw_one, gw_two = pl.pallas_call(
        functools.partial(result_kernel, 1.0 / (n_gx * n_gy * SHARE), per),
        out_shape=(columns, columns, sums, sums),
        in_specs=[left, left, whole],
        out_specs=(left,) * 4,
        scratch_shapes=[vm((27 * C, C), F32), vm((27 * C, C), F32), dma((4,))],
        compiler_params=pltpu.CompilerParams(vmem_limit_bytes=8 * 2**20),
        name="results",
    )(out, gfeat, full)
    return out, gfeat, gw_one.reshape(27, C, C), gw_two.reshape(27, C, C)


def solution(mesh):
    columns = P("gx", "gy", None)
    placed = (columns, columns, P("gx", "gy"), P("gx", "gy")) + (P(),) * 6
    return jax.shard_map(
        functools.partial(run, mesh.shape["gx"], mesh.shape["gy"]),
        mesh=mesh,
        in_specs=placed,
        out_specs=(columns, columns, P(), P()),
        check_vma=False,
    )
```

```python
import functools

import jax
import jax.numpy as jnp
from jax import lax
from jax.experimental import pallas as pl
from jax.experimental.pallas import tpu as pltpu
from jax.sharding import PartitionSpec as P

MESH = pl.DeviceIdType.MESH
F32 = jnp.float32
BF16 = jnp.bfloat16
BRICK = 8
C = 64
WIDTH = 512
SLOTS = 4
SHARE = 2
BX, BY = 2, 8
W = 12
ROWS = SLOTS * W
CORE = SLOTS * BRICK
BLOCKS = 16
USED = 14
HALOS = [(dx, dy) for dx in (-1, 0, 1) for dy in (-1, 0, 1) if dx or dy]


def lane(shape):
    return lax.broadcasted_iota(jnp.int32, shape, len(shape) - 1)


def turned(value):
    return pltpu.roll(value, 64, value.ndim - 1)


def height_mask(bounds):
    first = lane(bounds.shape) < 64
    other = turned(bounds)
    low, high = jnp.where(first, bounds, other), jnp.where(first, other, bounds)
    step = jnp.where(first, 0.0, 1.0)
    return [(step + 2.0 * c >= low) & (step + 2.0 * c < high) for c in range(4)]


def toeplitz(one, two, pair_ref, t):
    first = lane(one.shape) < 64
    zero = jnp.zeros(one.shape, BF16)
    start = jnp.where(first, turned(one), 0.0).astype(BF16)
    end = jnp.where(first, 0.0, turned(two)).astype(BF16)
    one, two = one.astype(BF16), two.astype(BF16)
    rows = pl.ds(pl.multiple_of(t * 512, 512), 512)
    columns = (
        [zero, start, one, two, end, zero, zero, zero],
        [zero, zero, zero, start, one, two, end, zero],
    )
    for c in range(2):
        pair_ref[rows, 128 * c : 128 * c + 128] = jnp.concatenate(columns[c], axis=0)


def build_weights(w_ref, forward_ref, adjoint_ref):
    def tap(t, carry):
        rows = w_ref[pl.ds(pl.multiple_of(t * 192, 192), 192), :].astype(F32)
        lower, middle, upper = rows[:64], rows[64:128], rows[128:]
        toeplitz(
            jnp.concatenate([middle, lower], axis=1),
            jnp.concatenate([upper, middle], axis=1),
            forward_ref,
            t,
        )
        toeplitz(rows[64:192].T, rows[0:128].T, adjoint_ref, 8 - t)
        return carry

    lax.fori_loop(0, 9, tap, 0)


def conv(source, band_ref, g, spans, pitch):
    lanes = slice(128 * g, 128 * g + 384)
    parts = [
        jnp.concatenate(
            [
                source[oy, start + ox * pitch : start + ox * pitch + count, lanes]
                for ox in range(3)
                for oy in range(3)
            ],
            axis=1,
        )
        for start, count in spans
    ]
    rows = parts[0] if len(parts) == 1 else jnp.concatenate(parts, axis=0)
    skip = 128 * (1 - g)
    band = jnp.concatenate(
        [band_ref[512 * t + skip : 512 * t + skip + 384, :] for t in range(9)], axis=0
    )
    return jnp.dot(rows, band, preferred_element_type=F32)


def shifted(value):
    count = value.shape[0]
    return (pltpu.roll(value, 1, 0), value, pltpu.roll(value, count - 1, 0))


def fold(results, fold_ref, block_ref, t0):
    for oy in range(3):
        sums = {}
        for g in range(2):
            for z in range(4 * g, 4 * g + 4):
                for c in range(3):
                    kind = (z % 2, 2 * g + 2 * c - z)
                    if kind in ((0, 0), (0, -2), (1, -1), (1, 1)):
                        zo = z - 4 * g
                        block = results[g][
                            64 * zo : 64 * zo + 64,
                            384 * oy + 128 * c : 384 * oy + 128 * c + 128,
                        ]
                        sums[kind] = sums[kind] + block if kind in sums else block
        p, u, q, s = sums[0, 0], sums[0, -2], sums[1, -1], sums[1, 1]
        first = lane(p.shape) < 64
        block_ref[t0 + oy] = (q + turned(jnp.where(first, p, u))).astype(BF16)
        fold_ref[t0 + oy] = p + turned(s)


def weight_sums(errors_t, source, count, pitch, fold_ref, block_ref, send):
    def column(ox, carry):
        base = pl.multiple_of(ox * pitch, 16)
        results = []
        for g in range(2):
            lanes = slice(128 * g, 128 * g + 384)
            window = jnp.concatenate(
                [source[oy, pl.ds(base, count), lanes] for oy in range(3)], axis=1
            )
            results.append(
                jnp.dot(errors_t[g], window, preferred_element_type=F32)
            )
        fold(results, fold_ref, block_ref, 3 * ox)
        for oy in range(3):
            send(3 * ox + oy)
        return carry

    lax.fori_loop(0, 3, column, 0)
    first = lane((64, 128)) < 64
    for i in range(5):
        even = turned(fold_ref[2 * i])
        odd = fold_ref[2 * i + 1] if i < 4 else jnp.zeros_like(even)
        block_ref[9 + i] = jnp.where(first, even, odd).astype(BF16)
        send(9 + i)


def unfold(blocks_ref, per, out_ref, factor):
    for t in range(9):
        block = blocks_ref[t // per, t % per].astype(F32) * factor
        out_ref[192 * t : 192 * t + 128, :] = block.T
    for i in range(5):
        block = (blocks_ref[(9 + i) // per, (9 + i) % per].astype(F32) * factor).T
        out_ref[384 * i + 128 : 384 * i + 192, :] = block[:64]
        if i < 4:
            out_ref[384 * i + 320 : 384 * i + 384, :] = block[64:]


def block_kernel(
    n_gx,
    n_gy,
    feat,
    cot_in,
    w_one_in,
    w_two_in,
    low_in,
    high_in,
    scale_one_in,
    shift_one_in,
    scale_two_in,
    shift_two_in,
    out,
    gfeat,
    full,
    cot,
    w_one,
    w_two,
    low,
    high,
    scales,
    bounds,
    ext,
    elh,
    pick_in,
    pick_bounds,
    pick_target,
    put_out,
    put_grad,
    src_one,
    src_two,
    err_two,
    err_one,
    msk,
    core_in,
    core_mask,
    target,
    slope,
    frame,
    res,
    grad_region,
    gsum,
    fwd_one,
    adj_one,
    fwd_two,
    adj_two,
    folded,
    blocks,
    got_x,
    half,
    got_y,
    out_x,
    in_x,
    edge_rows,
    out_y,
    in_y,
    out_c,
    in_c,
    local_sem,
    halo_send,
    halo_recv,
    edge_send,
    edge_recv,
    sum_send,
    sum_recv,
):
    comm = n_gx * n_gy > 1
    if comm:
        gx, gy = lax.axis_index("gx"), lax.axis_index("gy")
    else:
        gx, gy = 0, 0
    nx, ny = feat.shape[0], feat.shape[1]
    per = BLOCKS // n_gx

    inputs = [
        pltpu.make_async_copy(src, dst, local_sem.at[2 + k])
        for k, (src, dst) in enumerate(
            ((w_one_in, w_one), (w_two_in, w_two), (cot_in, cot))
        )
    ]

    def device(dx, dy):
        return (lax.rem(gx + dx + n_gx, n_gx), lax.rem(gy + dy + n_gy, n_gy))

    if comm:
        barrier = pltpu.get_barrier_semaphore()
        peers = [(d, 0) for d in range(1, n_gx)] + [(0, d) for d in range(1, n_gy)]
        peers += [(dx, dy) for dx, dy in HALOS if dx and dy]
        for dx, dy in peers:
            pl.semaphore_signal(
                barrier, inc=1, device_id=device(dx, dy), device_id_type=MESH
            )

    own = pltpu.make_async_copy(
        feat, ext.at[2 : nx + 2, 16 : ny + 16], local_sem.at[0]
    )
    own.start()
    small = [
        pltpu.make_async_copy(src, dst, local_sem.at[5 + k])
        for k, (src, dst) in enumerate(
            (
                (low_in, low),
                (high_in, high),
                (scale_one_in, scales.at[0]),
                (shift_one_in, scales.at[1]),
                (scale_two_in, scales.at[2]),
                (shift_two_in, scales.at[3]),
            )
        )
    ]
    for copy in small + inputs:
        copy.start()
    for copy in small:
        copy.wait()

    first = lane((ny, 128)) < 64
    square = jnp.zeros((ny, ny), F32)
    lows = jnp.concatenate([low[...].astype(F32), square[nx:]], axis=0).T
    highs = jnp.concatenate([high[...].astype(F32), square[nx:]], axis=0).T
    for x in range(nx):
        both = jnp.where(first, lows[:, x : x + 1], highs[:, x : x + 1]).astype(BF16)
        bounds[x] = both
        elh[x + 2, 16 : ny + 16, :] = both
    def remote(src, dst, send, recv, to):
        return pltpu.make_async_remote_copy(
            src_ref=src,
            dst_ref=dst,
            send_sem=send,
            recv_sem=recv,
            device_id=to,
            device_id_type=MESH,
        )

    inputs[0].wait()
    build_weights(w_one, fwd_one, adj_one)

    if comm:
        pl.semaphore_wait(barrier, len(peers))
    halos = []
    if comm:
        x_from = {-1: slice(0, 2), 0: slice(0, nx), 1: slice(nx - 2, nx)}
        x_to = {-1: slice(nx + 2, nx + 4), 0: slice(2, nx + 2), 1: slice(0, 2)}
        y_from = {-1: slice(0, 16), 0: slice(0, ny), 1: slice(ny - 16, ny)}
        y_to = {-1: slice(ny + 16, ny + 32), 0: slice(16, ny + 16), 1: slice(0, 16)}
        order = sorted(HALOS, key=lambda h: -(2 * abs(h[0]) - abs(h[1])))
        for i, (dx, dy) in enumerate(order):
            for k, (src, dst) in enumerate(((feat, ext), (bounds, elh))):
                copy = remote(
                    src.at[x_from[dx], y_from[dy]],
                    dst.at[x_to[dx], y_to[dy]],
                    halo_send.at[k, i],
                    halo_recv.at[k, i],
                    device(dx, dy),
                )
                copy.start()
                halos.append(copy)
    inputs[1].wait()
    build_weights(w_two, fwd_two, adj_two)
    nothing = jnp.zeros((3, 2 * ROWS, WIDTH), BF16)
    err_two[:, 0 : 2 * ROWS, :] = nothing
    err_two[:, 10 * ROWS : 12 * ROWS, :] = nothing
    err_one[:, 0 : 2 * ROWS, :] = nothing
    err_one[:, 12 * ROWS : 14 * ROWS, :] = nothing
    frame[...] = jnp.zeros_like(frame)

    occupied = jnp.where(high[...] > low[...], 1, 0)
    by_lane = lane((8, ny))
    count = jnp.int32(0)
    brick = [jnp.int32(-1000)] * SLOTS
    for bx in range(BX):
        rows = occupied[8 * bx : 8 * bx + 8]
        for by in range(BY):
            inside = (by_lane >= 8 * by) & (by_lane < 8 * by + 8)
            filled = jnp.max(jnp.where(inside, rows, 0))
            for j in range(SLOTS):
                hit = (filled > 0) & (count == j)
                brick[j] = jnp.where(hit, 8 * bx + by, brick[j])
            count = count + filled

    def picks(rows, columns, row_dim, per_brick, pitch, offset):
        shape = (rows, columns) if row_dim == 0 else (columns, rows)
        row = lax.broadcasted_iota(jnp.int32, shape, row_dim)
        column = lax.broadcasted_iota(jnp.int32, shape, 1 - row_dim)
        wanted = row + offset
        for j in range(SLOTS):
            b = brick[j]
            bx = jnp.where(b >= BY, 1, 0)
            spot = jnp.where(b < 0, -4000, bx * pitch + 8 * (b - BY * bx)) - per_brick * j
            inside = (row >= per_brick * j) & (row < per_brick * j + per_brick)
            wanted = wanted + jnp.where(inside, spot, 0)
        return jnp.where(column == wanted, 1.0, 0.0).astype(BF16)

    tall = ny + 32
    core_pick = picks(CORE, 2 * tall, 0, BRICK, tall, 16)
    frame_pick = [picks(ROWS, 2 * tall, 0, W, tall, 13 + oy) for oy in range(3)]
    pick_in[...] = jnp.concatenate(frame_pick + [core_pick], axis=0)
    pick_bounds[...] = jnp.concatenate([frame_pick[1], core_pick], axis=0)
    pick_target[...] = picks(CORE, 2 * ny, 0, BRICK, ny, 0)
    put_out[...] = picks(CORE, 2 * ny, 1, BRICK, ny, 0)
    put_grad[...] = picks(ROWS, 2 * (ny + 16), 1, W, ny + 16, 6)

    inputs[2].wait()
    def cut_target(x, carry):
        rows = jnp.concatenate([cot[x], cot[8 + x]], axis=0)
        spot = pl.ds(pl.multiple_of(x * CORE, CORE), CORE)
        target[spot, :] = jnp.dot(pick_target[...], rows, preferred_element_type=F32)
        return carry

    lax.fori_loop(0, 8, cut_target, 0, unroll=8)

    def mask_in(xs, ys):
        mask = height_mask(elh[xs, ys, :].astype(F32))
        for c in range(4):
            lanes = slice(128 * c, 128 * c + 128)
            value = ext[xs, ys, lanes].astype(F32)
            ext[xs, ys, lanes] = jnp.where(mask[c], value, 0.0).astype(BF16)

    def mask_inner(i, carry):
        mask_in(pl.ds(2 + 2 * i, 2), slice(16, ny + 16))
        return carry

    own.wait()
    lax.fori_loop(0, nx // 2, mask_inner, 0, unroll=2)
    for copy in halos:
        copy.wait()
    if comm:
        for spot, inside in (
            ((slice(0, 2), slice(None)), gx > 0),
            ((slice(nx + 2, nx + 4), slice(None)), gx < n_gx - 1),
            ((slice(None), slice(0, 16)), gy > 0),
            ((slice(None), slice(ny + 16, ny + 32)), gy < n_gy - 1),
        ):
            value = elh[spot[0], spot[1], :].astype(F32)
            elh[spot[0], spot[1], :] = (
                value * jnp.where(inside, 1.0, 0.0).astype(F32)
            ).astype(BF16)
    else:
        for spot in (slice(0, 2), slice(nx + 2, nx + 4)):
            elh[spot] = jnp.zeros_like(elh[spot])
            ext[spot] = jnp.zeros_like(ext[spot])
        for spot in (slice(0, 16), slice(ny + 16, ny + 32)):
            elh[:, spot] = jnp.zeros_like(elh[:, spot])
            ext[:, spot] = jnp.zeros_like(ext[:, spot])

    for x in range(2, nx + 2, 4):
        mask_in(slice(x, x + 4), slice(0, 16))
        mask_in(slice(x, x + 4), slice(ny + 16, tall))
    for x in (0, 1, nx + 2, nx + 3):
        mask_in(slice(x, x + 1), slice(0, tall))

    def cut(x, carry):
        base = pl.multiple_of(x * ROWS, ROWS)
        core = pl.multiple_of(x * CORE, CORE)
        rows = jnp.concatenate([ext[x], ext[8 + x]], axis=0)
        value = jnp.dot(pick_in[...], rows, preferred_element_type=F32)
        for oy in range(3):
            src_one[oy, pl.ds(base, ROWS), :] = value[
                ROWS * oy : ROWS * oy + ROWS
            ].astype(BF16)
        core_in[pl.ds(core, CORE), :] = value[3 * ROWS :]
        rows = jnp.concatenate([elh[x], elh[8 + x]], axis=0)
        mask = height_mask(
            jnp.dot(pick_bounds[...], rows, preferred_element_type=F32)
        )
        for c in range(4):
            lanes = slice(128 * c, 128 * c + 128)
            value = jnp.where(mask[c], 1.0, 0.0)
            msk[pl.ds(base, ROWS), lanes] = value[:ROWS]
            core_mask[pl.ds(core, CORE), lanes] = value[ROWS:]
        return carry

    lax.fori_loop(0, W, cut, 0, unroll=4)

    scale_one, shift_one, scale_two, shift_two = (
        jnp.concatenate([scales[k]] * 4, axis=1) for k in range(4)
    )

    for g in range(2):
        lanes = slice(256 * g, 256 * g + 256)
        pre = conv(src_one, fwd_one, g, [(0, 10 * ROWS)], ROWS) * scale_one + shift_one
        s = jax.nn.sigmoid(pre)
        mask = msk[ROWS : 11 * ROWS, lanes]
        hidden = pre * s * mask
        slope[:, lanes] = s * (1.0 + pre * (1.0 - s)) * mask * scale_one
        for x in range(10):
            rows = hidden[ROWS * x : ROWS * x + ROWS]
            for oy in range(3):
                for j in range(0, SLOTS, 2):
                    both = [
                        rows[W * i + 1 + oy : W * i + 9 + oy] for i in (j, j + 1)
                    ]
                    src_two[oy, CORE * x + 8 * j : CORE * x + 8 * j + 16, lanes] = (
                        jnp.concatenate(both, axis=0).astype(BF16)
                    )

    middle = slice(2 * CORE, 10 * CORE)
    errors_t = []
    for g in range(2):
        lanes = slice(256 * g, 256 * g + 256)
        pre = conv(src_two, fwd_two, g, [(0, 8 * CORE)], CORE) * scale_two + shift_two
        pre = pre + core_in[middle, lanes]
        s = jax.nn.sigmoid(pre)
        mask = core_mask[middle, lanes]
        result = pre * s * mask
        grad = target[:, lanes] * mask * (s * (1.0 + pre * (1.0 - s)))
        errors_t.append((grad * scale_two).T.astype(BF16))
        res[:, lanes] = result.astype(BF16)
        for x in range(8):
            for j in range(SLOTS):
                spot = CORE * x + 8 * j
                frame[x, W * j + 2 : W * j + 10, lanes] = grad[spot : spot + 8]

    def spread(x, carry):
        base = pl.multiple_of((x + 2) * ROWS, ROWS)
        for g in range(2):
            lanes = slice(256 * g, 256 * g + 256)
            for oy, moved in enumerate(shifted(frame[x, :, lanes] * scale_two)):
                err_two[oy, pl.ds(base, ROWS), lanes] = moved.astype(BF16)
        return carry

    lax.fori_loop(0, 8, spread, 0, unroll=2)

    def block_copy(conv_id, b, sender):
        return remote(
            blocks.at[conv_id, b],
            got_x.at[conv_id, sender, 0],
            sum_send.at[conv_id, 0, b],
            sum_recv.at[conv_id, 0, sender],
            (b, gy),
        )

    def sender_of(conv_id):
        def send(b):
            if not comm:
                got_x[conv_id, 0, b] = blocks[conv_id, b]
                return

            @pl.when(gx != b)
            def _():
                block_copy(conv_id, b, gx).start()

            @pl.when(gx == b)
            def _():
                got_x[conv_id, gx, 0] = blocks[conv_id, b]

        return send

    def y_copy(conv_id, d):
        return remote(
            half.at[0, conv_id],
            got_y.at[conv_id, gy],
            sum_send.at[conv_id, 1, d],
            sum_recv.at[conv_id, 1, d],
            (gx, lax.rem(gy + d, n_gy)),
        )

    def full_copy(conv_id, to, owner):
        return remote(
            half.at[1, conv_id],
            full.at[conv_id, owner],
            sum_send.at[conv_id, 2, to],
            sum_recv.at[conv_id, 2, owner],
            (to, gy),
        )

    def owners(act):
        if comm:
            pl.when(gx < USED)(act)
        else:
            act()

    def others(n, act):
        for k in range(n):
            pl.when(gx != k)(functools.partial(act, k))

    def reduce_x(conv_id):
        def act():
            if comm:
                others(n_gx, lambda s: block_copy(conv_id, 0, s).wait_recv())
            total = got_x[conv_id, 0].astype(F32)
            for s in range(1, n_gx):
                total = total + got_x[conv_id, s].astype(F32)
            half[0, conv_id] = total.astype(BF16)
            for d in range(1, n_gy):
                y_copy(conv_id, d).start()
            got_y[conv_id, gy] = half[0, conv_id]

        owners(act)

    def reduce_y(conv_id):
        def act():
            for d in range(1, n_gy):
                y_copy(conv_id, d).wait_recv()
            total = got_y[conv_id, 0].astype(F32)
            for s in range(1, n_gy):
                total = total + got_y[conv_id, s].astype(F32)
            half[1, conv_id] = total.astype(BF16)
            if comm:
                others(n_gx, lambda to: full_copy(conv_id, to, gx).start())
            full[conv_id, gx] = half[1, conv_id]

        owners(act)

    weight_sums(
        errors_t, src_two, 8 * CORE, CORE, folded, blocks.at[1], sender_of(1)
    )

    errors_t = []
    for g in range(2):
        lanes = slice(256 * g, 256 * g + 256)
        back = conv(err_two, adj_two, g, [(0, 10 * ROWS)], ROWS)
        error = back * slope[:, lanes]
        errors_t.append(error.T.astype(BF16))
        for x in range(10):
            rows = error[ROWS * x : ROWS * x + ROWS]
            spot = slice(ROWS * (x + 2), ROWS * (x + 3))
            for oy, moved in enumerate(shifted(rows)):
                err_one[oy, spot, lanes] = moved.astype(BF16)
    weight_sums(
        errors_t, src_one, 10 * ROWS, ROWS, folded, blocks.at[0], sender_of(0)
    )
    reduce_x(1)

    def adjoint_one(g, columns):
        lanes = slice(256 * g, 256 * g + 256)
        spans = [(ROWS * x, ROWS * n) for x, n in columns]
        back = conv(err_one, adj_one, g, spans, ROWS)
        done = 0
        for start, n in columns:
            for x in range(start, start + n):
                rows = back[ROWS * done : ROWS * done + ROWS]
                if 2 <= x < 10:
                    rows = rows + frame[x - 2, :, lanes]
                grad_region[x, :, lanes] = rows.astype(BF16)
                done += 1

    def collect(x):
        total = None
        for bx in range(BX):
            if 0 <= x - 8 * bx < W:
                part = jnp.dot(
                    put_grad[bx * (ny + 16) : (bx + 1) * (ny + 16), :],
                    grad_region[x - 8 * bx],
                    preferred_element_type=F32,
                )
                total = part if total is None else total + part
        return total

    for g in range(2):
        adjoint_one(g, [(0, 2), (10, 2)])
    edges = []

    def send_edges(kinds):
        for i, (dx, dy) in enumerate(HALOS):
            if (dx, dy) not in kinds:
                continue
            a, b = (dx + 1) // 2, (dy + 1) // 2
            if dy == 0:
                src, dst = out_x.at[a], in_x.at[1 - a]
            elif dx == 0:
                src, dst = out_y.at[b], in_y.at[1 - b]
            else:
                src, dst = out_c.at[a, b], in_c.at[1 - a, 1 - b]
            copy = remote(
                src, dst, edge_send.at[i], edge_recv.at[i], device(dx, dy)
            )
            copy.start()
            edges.append(copy)

    if comm:
        for a, x in enumerate((0, nx + 2)):
            pair = [collect(x + k) for k in range(2)]
            for k in range(2):
                out_x[a, k] = pair[k][8 : ny + 8].astype(BF16)
            for b, t in enumerate((0, ny + 8)):
                both = [value[t : t + 8] for value in pair]
                out_c[a, b] = jnp.concatenate(both, axis=0).astype(BF16)
        send_edges([h for h in HALOS if h[0]])

    adjoint_one(0, [(2, 8)])
    reduce_x(0)
    adjoint_one(1, [(2, 8)])
    reduce_y(1)

    for x in range(2, nx + 2):
        value = collect(x)
        gsum[x] = value
        if comm:
            rows = slice(2 * (x - 2), 2 * (x - 2) + 2)
            edge_rows[0, rows, :] = value[6:8]
            edge_rows[1, rows, :] = value[ny + 8 : ny + 10]
    if comm:
        out_y[...] = edge_rows[...].astype(BF16)
        send_edges([h for h in HALOS if not h[0]])
    reduce_y(0)

    def deposit(x, carry):
        rows = res[pl.ds(pl.multiple_of(x * CORE, CORE), CORE), :]
        value = jnp.dot(put_out[...], rows, preferred_element_type=F32).astype(BF16)
        out[x] = value[:ny]
        out[8 + x] = value[ny:]
        return carry

    lax.fori_loop(0, 8, deposit, 0, unroll=4)

    if comm:
        for copy in edges:
            copy.wait_recv()
        x_in = [
            jnp.where(inside, 1.0, 0.0).astype(F32)
            for inside in (gx > 0, gx < n_gx - 1)
        ]
        y_in = [
            jnp.where(inside, 1.0, 0.0).astype(F32)
            for inside in (gy > 0, gy < n_gy - 1)
        ]
        for a, x in enumerate((2, nx)):
            gsum[x : x + 2, 8 : ny + 8, :] += in_x[a].astype(F32) * x_in[a]
            for b, t in enumerate((8, ny)):
                rows = in_c[a, b].astype(F32) * (x_in[a] * y_in[b])
                for k in range(2):
                    gsum[x + k, t : t + 8, :] += rows[8 * k : 8 * k + 8]
        for b, t in enumerate((8, ny + 6)):
            rows = in_y[b].astype(F32) * y_in[b]
            for i in range(nx):
                gsum[2 + i, t : t + 2, :] += rows[2 * i : 2 * i + 2]

    def finish(x, carry):
        mask = height_mask(elh[x + 2, 16 : ny + 16, :].astype(F32))
        for c in range(4):
            lanes = slice(128 * c, 128 * c + 128)
            value = gsum[x + 2, 8 : ny + 8, lanes]
            gfeat[x, :, lanes] = jnp.where(mask[c], value, 0.0).astype(BF16)
        return carry

    lax.fori_loop(0, nx, finish, 0, unroll=4)

    if comm:
        for conv_id in (1, 0):
            others(USED, lambda k: full_copy(conv_id, 0, k).wait_recv())
        for copy in edges:
            copy.wait_send()
        for conv_id in (1, 0):
            others(USED, lambda b: block_copy(conv_id, b, gx).wait_send())

            def sent(conv_id=conv_id):
                for d in range(1, n_gy):
                    y_copy(conv_id, d).wait_send()
                others(n_gx, lambda to: full_copy(conv_id, to, gx).wait_send())

            owners(sent)


def result_kernel(
    factor, per, out_in, gfeat_in, full, out, gfeat, gw_one, gw_two, one, two, sem
):
    copies = [
        pltpu.make_async_copy(out_in, out, sem.at[0]),
        pltpu.make_async_copy(gfeat_in, gfeat, sem.at[1]),
    ]
    for copy in copies:
        copy.start()
    for k, (ref, gw) in enumerate(((one, gw_one), (two, gw_two))):
        unfold(full.at[k], per, ref, factor)
        copy = pltpu.make_async_copy(ref, gw, sem.at[2 + k])
        copy.start()
        copies.append(copy)
    for copy in copies:
        copy.wait()


def run(
    n_gx,
    n_gy,
    features,
    cotangent,
    low,
    high,
    weight_one,
    weight_two,
    scale_one,
    shift_one,
    scale_two,
    shift_two,
):
    nx, ny = features.shape[0], features.shape[1]
    per = BLOCKS // n_gx
    whole = pl.BlockSpec(memory_space=pltpu.VMEM)
    left = pl.BlockSpec(memory_space=pl.ANY)
    vm = pltpu.VMEM
    dma = pltpu.SemaphoreType.DMA
    scratch = [
        vm((nx, ny, WIDTH), BF16),
        vm((27 * C, C), BF16),
        vm((27 * C, C), BF16),
        vm((nx, ny), jnp.int32),
        vm((nx, ny), jnp.int32),
        vm((4, 1, C), F32),
        vm((nx, ny, 128), BF16),
        vm((nx + 4, ny + 32, WIDTH), BF16),
        vm((nx + 4, ny + 32, 128), BF16),
        vm((3 * ROWS + CORE, 2 * ny + 64), BF16),
        vm((ROWS + CORE, 2 * ny + 64), BF16),
        vm((CORE, 2 * ny), BF16),
        vm((2 * ny, CORE), BF16),
        vm((2 * ny + 32, ROWS), BF16),
        vm((3, W * ROWS, WIDTH), BF16),
        vm((3, 10 * CORE, WIDTH), BF16),
        vm((3, W * ROWS, WIDTH), BF16),
        vm((3, (W + 2) * ROWS, WIDTH), BF16),
        vm((W * ROWS, WIDTH), F32),
        vm((W * CORE, WIDTH), F32),
        vm((W * CORE, WIDTH), F32),
        vm((8 * CORE, WIDTH), F32),
        vm((10 * ROWS, WIDTH), F32),
        vm((8, ROWS, WIDTH), F32),
        vm((8 * CORE, WIDTH), BF16),
        vm((W, ROWS, WIDTH), BF16),
        vm((nx + 4, ny + 16, WIDTH), F32),
        vm((9 * 512, 256), BF16),
        vm((9 * 512, 256), BF16),
        vm((9 * 512, 256), BF16),
        vm((9 * 512, 256), BF16),
        vm((9, 64, 128), F32),
        vm((2, BLOCKS, 64, 128), BF16),
        vm((2, n_gx, per, 64, 128), BF16),
        vm((2, 2, per, 64, 128), BF16),
        vm((2, n_gy, per, 64, 128), BF16),
        vm((2, 2, ny, WIDTH), BF16),
        vm((2, 2, ny, WIDTH), BF16),
        vm((2, 2 * nx, WIDTH), F32),
        vm((2, 2 * nx, WIDTH), BF16),
        vm((2, 2 * nx, WIDTH), BF16),
        vm((2, 2, 16, WIDTH), BF16),
        vm((2, 2, 16, WIDTH), BF16),
        dma((11,)),
        dma((2, 8)),
        dma((2, 8)),
        dma((8,)),
        dma((8,)),
        dma((2, 3, 16)),
        dma((2, 3, 16)),
    ]
    comm = n_gx * n_gy > 1
    params = pltpu.CompilerParams(
        collective_id=0 if comm else None,
        has_side_effects=comm,
        vmem_limit_bytes=46 * 2**20,
    )
    in_hbm = functools.partial(
        pltpu.with_memory_space_constraint, memory_space=pltpu.HBM
    )
    columns = jax.ShapeDtypeStruct(features.shape, BF16)
    out, gfeat, full = pl.pallas_call(
        functools.partial(block_kernel, n_gx, n_gy),
        out_shape=(
            columns,
            columns,
            jax.ShapeDtypeStruct((2, n_gx, per, 64, 128), BF16),
        ),
        in_specs=[pl.BlockSpec(memory_space=pltpu.HBM)] * 10,
        out_specs=(whole,) * 3,
        scratch_shapes=scratch,
        compiler_params=params,
        name="residual_block",
    )(
        in_hbm(features),
        in_hbm(cotangent),
        in_hbm(weight_one.reshape(27 * C, C)),
        in_hbm(weight_two.reshape(27 * C, C)),
        in_hbm(low),
        in_hbm(high),
        in_hbm(scale_one.reshape(1, C)),
        in_hbm(shift_one.reshape(1, C)),
        in_hbm(scale_two.reshape(1, C)),
        in_hbm(shift_two.reshape(1, C)),
    )
    sums = jax.ShapeDtypeStruct((27 * C, C), F32)
    out, gfeat, gw_one, gw_two = pl.pallas_call(
        functools.partial(result_kernel, 1.0 / (n_gx * n_gy * SHARE), per),
        out_shape=(columns, columns, sums, sums),
        in_specs=[left, left, whole],
        out_specs=(left,) * 4,
        scratch_shapes=[vm((27 * C, C), F32), vm((27 * C, C), F32), dma((4,))],
        compiler_params=pltpu.CompilerParams(vmem_limit_bytes=8 * 2**20),
        name="results",
    )(out, gfeat, full)
    return out, gfeat, gw_one.reshape(27, C, C), gw_two.reshape(27, C, C)


def solution(mesh):
    columns = P("gx", "gy", None)
    placed = (columns, columns, P("gx", "gy"), P("gx", "gy")) + (P(),) * 6
    return jax.shard_map(
        functools.partial(run, mesh.shape["gx"], mesh.shape["gy"]),
        mesh=mesh,
        in_specs=placed,
        out_specs=(columns, columns, P(), P()),
        check_vma=False,
    )
```

```python
import functools

import jax
import jax.numpy as jnp
from jax import lax
from jax.experimental import pallas as pl
from jax.experimental.pallas import tpu as pltpu
from jax.sharding import PartitionSpec as P

MESH = pl.DeviceIdType.MESH
F32 = jnp.float32
BF16 = jnp.bfloat16
BRICK = 8
C = 64
WIDTH = 512
SLOTS = 4
SHARE = 2
BX, BY = 2, 8
W = 12
ROWS = SLOTS * W
CORE = SLOTS * BRICK
BLOCKS = 16
USED = 14
HALOS = [(dx, dy) for dx in (-1, 0, 1) for dy in (-1, 0, 1) if dx or dy]


def lane(shape):
    return lax.broadcasted_iota(jnp.int32, shape, len(shape) - 1)


def turned(value):
    return pltpu.roll(value, 64, value.ndim - 1)


def height_mask(bounds):
    first = lane(bounds.shape) < 64
    other = turned(bounds)
    low, high = jnp.where(first, bounds, other), jnp.where(first, other, bounds)
    step = jnp.where(first, 0.0, 1.0)
    return [(step + 2.0 * c >= low) & (step + 2.0 * c < high) for c in range(4)]


def toeplitz(one, two, pair_ref, t):
    first = lane(one.shape) < 64
    zero = jnp.zeros(one.shape, BF16)
    start = jnp.where(first, turned(one), 0.0).astype(BF16)
    end = jnp.where(first, 0.0, turned(two)).astype(BF16)
    one, two = one.astype(BF16), two.astype(BF16)
    rows = pl.ds(pl.multiple_of(t * 512, 512), 512)
    columns = (
        [zero, start, one, two, end, zero, zero, zero],
        [zero, zero, zero, start, one, two, end, zero],
    )
    for c in range(2):
        pair_ref[rows, 128 * c : 128 * c + 128] = jnp.concatenate(columns[c], axis=0)


def build_weights(w_ref, forward_ref, adjoint_ref):
    def tap(t, carry):
        rows = w_ref[pl.ds(pl.multiple_of(t * 192, 192), 192), :].astype(F32)
        lower, middle, upper = rows[:64], rows[64:128], rows[128:]
        toeplitz(
            jnp.concatenate([middle, lower], axis=1),
            jnp.concatenate([upper, middle], axis=1),
            forward_ref,
            t,
        )
        toeplitz(rows[64:192].T, rows[0:128].T, adjoint_ref, 8 - t)
        return carry

    lax.fori_loop(0, 9, tap, 0)


def conv(source, band_ref, g, spans, pitch):
    lanes = slice(128 * g, 128 * g + 384)
    parts = [
        jnp.concatenate(
            [
                source[oy, start + ox * pitch : start + ox * pitch + count, lanes]
                for ox in range(3)
                for oy in range(3)
            ],
            axis=1,
        )
        for start, count in spans
    ]
    rows = parts[0] if len(parts) == 1 else jnp.concatenate(parts, axis=0)
    skip = 128 * (1 - g)
    band = jnp.concatenate(
        [band_ref[512 * t + skip : 512 * t + skip + 384, :] for t in range(9)], axis=0
    )
    return jnp.dot(rows, band, preferred_element_type=F32)


def shifted(value):
    count = value.shape[0]
    return (pltpu.roll(value, 1, 0), value, pltpu.roll(value, count - 1, 0))


def fold(results, fold_ref, block_ref, k, t0):
    for oy in range(3):
        sums = {}
        for g in range(2):
            for z in range(4 * g, 4 * g + 4):
                for c in range(3):
                    kind = (z % 2, 2 * g + 2 * c - z)
                    if kind in ((0, 0), (0, -2), (1, -1), (1, 1)):
                        zo = z - 4 * g
                        block = results[g][
                            64 * zo : 64 * zo + 64,
                            384 * oy + 128 * c : 384 * oy + 128 * c + 128,
                        ]
                        sums[kind] = sums[kind] + block if kind in sums else block
        p, u, q, s = sums[0, 0], sums[0, -2], sums[1, -1], sums[1, 1]
        first = lane(p.shape) < 64
        block_ref[k, t0 + oy] = (q + turned(jnp.where(first, p, u))).astype(BF16)
        fold_ref[t0 + oy] = p + turned(s)


def weight_sums(errors_t, source, count, pitch, fold_ref, block_ref, k, send):
    def column(ox, carry):
        base = pl.multiple_of(ox * pitch, 16)
        results = []
        for g in range(2):
            lanes = slice(128 * g, 128 * g + 384)
            window = jnp.concatenate(
                [source[oy, pl.ds(base, count), lanes] for oy in range(3)], axis=1
            )
            results.append(
                jnp.dot(errors_t[g], window, preferred_element_type=F32)
            )
        fold(results, fold_ref, block_ref, k, 3 * ox)
        if send:
            for oy in range(3):
                send(k, 3 * ox + oy)
        return carry

    lax.fori_loop(0, 3, column, 0)
    first = lane((64, 128)) < 64
    for i in range(5):
        even = turned(fold_ref[2 * i])
        odd = fold_ref[2 * i + 1] if i < 4 else jnp.zeros_like(even)
        block_ref[k, 9 + i] = jnp.where(first, even, odd).astype(BF16)
        if send:
            send(k, 9 + i)


def unfold(blocks_ref, per, k, out_ref, factor):
    for t in range(9):
        block = blocks_ref[k, t // per, t % per].astype(F32) * factor
        out_ref[192 * t : 192 * t + 128, :] = block.T
    for i in range(5):
        block = (blocks_ref[k, (9 + i) // per, (9 + i) % per].astype(F32) * factor).T
        out_ref[384 * i + 128 : 384 * i + 192, :] = block[:64]
        if i < 4:
            out_ref[384 * i + 320 : 384 * i + 384, :] = block[64:]


def block_kernel(
    n_gx,
    n_gy,
    feat,
    cot_in,
    w_one_in,
    w_two_in,
    low_in,
    high_in,
    scale_one_in,
    shift_one_in,
    scale_two_in,
    shift_two_in,
    out,
    gfeat,
    full,
    cot,
    w_one,
    w_two,
    low,
    high,
    scales,
    bounds,
    ext,
    elh,
    pick_in,
    pick_bounds,
    pick_target,
    put_out,
    put_grad,
    src_one,
    src_two,
    err_two,
    err_one,
    msk,
    core_in,
    core_mask,
    target,
    slope,
    frame,
    res,
    grad_region,
    gsum,
    fwd_one,
    adj_one,
    fwd_two,
    adj_two,
    folded,
    blocks,
    got_x,
    half,
    got_y,
    out_x,
    in_x,
    edge_rows,
    out_y,
    in_y,
    out_c,
    in_c,
    local_sem,
    halo_send,
    halo_recv,
    edge_send,
    edge_recv,
    sum_send,
    sum_recv,
):
    comm = n_gx * n_gy > 1
    if comm:
        gx, gy = lax.axis_index("gx"), lax.axis_index("gy")
    else:
        gx, gy = 0, 0
    nx, ny = feat.shape[0], feat.shape[1]
    per = BLOCKS // n_gx

    inputs = [
        pltpu.make_async_copy(src, dst, local_sem.at[2 + k])
        for k, (src, dst) in enumerate(
            ((w_one_in, w_one), (w_two_in, w_two), (cot_in, cot))
        )
    ]

    def device(dx, dy):
        return (lax.rem(gx + dx + n_gx, n_gx), lax.rem(gy + dy + n_gy, n_gy))

    if comm:
        barrier = pltpu.get_barrier_semaphore()
        peers = [(d, 0) for d in range(1, n_gx)] + [(0, d) for d in range(1, n_gy)]
        peers += [(dx, dy) for dx, dy in HALOS if dx and dy]
        for dx, dy in peers:
            pl.semaphore_signal(
                barrier, inc=1, device_id=device(dx, dy), device_id_type=MESH
            )

    own = pltpu.make_async_copy(
        feat, ext.at[2 : nx + 2, 16 : ny + 16], local_sem.at[0]
    )
    own.start()
    small = [
        pltpu.make_async_copy(src, dst, local_sem.at[5 + k])
        for k, (src, dst) in enumerate(
            (
                (low_in, low),
                (high_in, high),
                (scale_one_in, scales.at[0]),
                (shift_one_in, scales.at[1]),
                (scale_two_in, scales.at[2]),
                (shift_two_in, scales.at[3]),
            )
        )
    ]
    for copy in small + inputs:
        copy.start()
    for copy in small:
        copy.wait()

    first = lane((ny, 128)) < 64
    square = jnp.zeros((ny, ny), F32)
    lows = jnp.concatenate([low[...].astype(F32), square[nx:]], axis=0).T
    highs = jnp.concatenate([high[...].astype(F32), square[nx:]], axis=0).T
    for x in range(nx):
        both = jnp.where(first, lows[:, x : x + 1], highs[:, x : x + 1]).astype(BF16)
        bounds[x] = both
        elh[x + 2, 16 : ny + 16, :] = both
    def all_wait(like, sem):
        pltpu.make_async_copy(like, like, sem).wait()

    def remote(src, dst, send, recv, to):
        return pltpu.make_async_remote_copy(
            src_ref=src,
            dst_ref=dst,
            send_sem=send,
            recv_sem=recv,
            device_id=to,
            device_id_type=MESH,
        )

    inputs[0].wait()
    build_weights(w_one, fwd_one, adj_one)

    if comm:
        pl.semaphore_wait(barrier, len(peers))
    if comm:
        x_from = {-1: slice(0, 2), 0: slice(0, nx), 1: slice(nx - 2, nx)}
        x_to = {-1: slice(nx + 2, nx + 4), 0: slice(2, nx + 2), 1: slice(0, 2)}
        y_from = {-1: slice(0, 16), 0: slice(0, ny), 1: slice(ny - 16, ny)}
        y_to = {-1: slice(ny + 16, ny + 32), 0: slice(16, ny + 16), 1: slice(0, 16)}
        order = sorted(HALOS, key=lambda h: -(2 * abs(h[0]) - abs(h[1])))
        for dx, dy in order:
            for k, (src, dst) in enumerate(((feat, ext), (bounds, elh))):
                copy = remote(
                    src.at[x_from[dx], y_from[dy]],
                    dst.at[x_to[dx], y_to[dy]],
                    halo_send.at[k],
                    halo_recv.at[k],
                    device(dx, dy),
                )
                copy.start()
    inputs[1].wait()
    build_weights(w_two, fwd_two, adj_two)
    nothing = jnp.zeros((3, 2 * ROWS, WIDTH), BF16)
    err_two[:, 0 : 2 * ROWS, :] = nothing
    err_two[:, 10 * ROWS : 12 * ROWS, :] = nothing
    err_one[:, 0 : 2 * ROWS, :] = nothing
    err_one[:, 12 * ROWS : 14 * ROWS, :] = nothing
    frame[...] = jnp.zeros_like(frame)

    occupied = jnp.where(high[...] > low[...], 1, 0)
    by_lane = lane((8, ny))
    count = jnp.int32(0)
    brick = [jnp.int32(-1000)] * SLOTS
    for bx in range(BX):
        rows = occupied[8 * bx : 8 * bx + 8]
        for by in range(BY):
            inside = (by_lane >= 8 * by) & (by_lane < 8 * by + 8)
            filled = jnp.max(jnp.where(inside, rows, 0))
            for j in range(SLOTS):
                hit = (filled > 0) & (count == j)
                brick[j] = jnp.where(hit, 8 * bx + by, brick[j])
            count = count + filled

    def picks(rows, columns, row_dim, per_brick, pitch, offset):
        shape = (rows, columns) if row_dim == 0 else (columns, rows)
        row = lax.broadcasted_iota(jnp.int32, shape, row_dim)
        column = lax.broadcasted_iota(jnp.int32, shape, 1 - row_dim)
        wanted = row + offset
        for j in range(SLOTS):
            b = brick[j]
            bx = jnp.where(b >= BY, 1, 0)
            spot = jnp.where(b < 0, -4000, bx * pitch + 8 * (b - BY * bx)) - per_brick * j
            inside = (row >= per_brick * j) & (row < per_brick * j + per_brick)
            wanted = wanted + jnp.where(inside, spot, 0)
        return jnp.where(column == wanted, 1.0, 0.0).astype(BF16)

    tall = ny + 32
    core_pick = picks(CORE, 2 * tall, 0, BRICK, tall, 16)
    frame_pick = [picks(ROWS, 2 * tall, 0, W, tall, 13 + oy) for oy in range(3)]
    pick_in[...] = jnp.concatenate(frame_pick + [core_pick], axis=0)
    pick_bounds[...] = jnp.concatenate([frame_pick[1], core_pick], axis=0)
    pick_target[...] = picks(CORE, 2 * ny, 0, BRICK, ny, 0)
    put_out[...] = picks(CORE, 2 * ny, 1, BRICK, ny, 0)
    put_grad[...] = picks(ROWS, 2 * (ny + 16), 1, W, ny + 16, 6)

    inputs[2].wait()
    def cut_target(x, carry):
        rows = jnp.concatenate([cot[x], cot[8 + x]], axis=0)
        spot = pl.ds(pl.multiple_of(x * CORE, CORE), CORE)
        target[spot, :] = jnp.dot(pick_target[...], rows, preferred_element_type=F32)
        return carry

    lax.fori_loop(0, 8, cut_target, 0, unroll=8)

    def mask_in(xs, ys):
        mask = height_mask(elh[xs, ys, :].astype(F32))
        for c in range(4):
            lanes = slice(128 * c, 128 * c + 128)
            value = ext[xs, ys, lanes].astype(F32)
            ext[xs, ys, lanes] = jnp.where(mask[c], value, 0.0).astype(BF16)

    def mask_inner(i, carry):
        mask_in(pl.ds(2 + 2 * i, 2), slice(16, ny + 16))
        return carry

    own.wait()
    lax.fori_loop(0, nx // 2, mask_inner, 0, unroll=2)
    if comm:
        margin = (nx + 4) * tall - nx * ny
        for k, ref in enumerate((ext, elh)):
            all_wait(ref.at[0 : margin // ny, 0:ny], halo_recv.at[k])
    if comm:
        for spot, inside in (
            ((slice(0, 2), slice(None)), gx > 0),
            ((slice(nx + 2, nx + 4), slice(None)), gx < n_gx - 1),
            ((slice(None), slice(0, 16)), gy > 0),
            ((slice(None), slice(ny + 16, ny + 32)), gy < n_gy - 1),
        ):
            value = elh[spot[0], spot[1], :].astype(F32)
            elh[spot[0], spot[1], :] = (
                value * jnp.where(inside, 1.0, 0.0).astype(F32)
            ).astype(BF16)
    else:
        for spot in (slice(0, 2), slice(nx + 2, nx + 4)):
            elh[spot] = jnp.zeros_like(elh[spot])
            ext[spot] = jnp.zeros_like(ext[spot])
        for spot in (slice(0, 16), slice(ny + 16, ny + 32)):
            elh[:, spot] = jnp.zeros_like(elh[:, spot])
            ext[:, spot] = jnp.zeros_like(ext[:, spot])

    for x in range(2, nx + 2, 4):
        mask_in(slice(x, x + 4), slice(0, 16))
        mask_in(slice(x, x + 4), slice(ny + 16, tall))
    for x in (0, 1, nx + 2, nx + 3):
        mask_in(slice(x, x + 1), slice(0, tall))

    def cut(x, carry):
        base = pl.multiple_of(x * ROWS, ROWS)
        core = pl.multiple_of(x * CORE, CORE)
        rows = jnp.concatenate([ext[x], ext[8 + x]], axis=0)
        value = jnp.dot(pick_in[...], rows, preferred_element_type=F32)
        for oy in range(3):
            src_one[oy, pl.ds(base, ROWS), :] = value[
                ROWS * oy : ROWS * oy + ROWS
            ].astype(BF16)
        core_in[pl.ds(core, CORE), :] = value[3 * ROWS :]
        rows = jnp.concatenate([elh[x], elh[8 + x]], axis=0)
        mask = height_mask(
            jnp.dot(pick_bounds[...], rows, preferred_element_type=F32)
        )
        for c in range(4):
            lanes = slice(128 * c, 128 * c + 128)
            value = jnp.where(mask[c], 1.0, 0.0)
            msk[pl.ds(base, ROWS), lanes] = value[:ROWS]
            core_mask[pl.ds(core, CORE), lanes] = value[ROWS:]
        return carry

    lax.fori_loop(0, W, cut, 0, unroll=4)

    scale_one, shift_one, scale_two, shift_two = (
        jnp.concatenate([scales[k]] * 4, axis=1) for k in range(4)
    )

    for g in range(2):
        lanes = slice(256 * g, 256 * g + 256)
        pre = conv(src_one, fwd_one, g, [(0, 10 * ROWS)], ROWS) * scale_one + shift_one
        s = jax.nn.sigmoid(pre)
        mask = msk[ROWS : 11 * ROWS, lanes]
        hidden = pre * s * mask
        slope[:, lanes] = s * (1.0 + pre * (1.0 - s)) * mask * scale_one
        for x in range(10):
            rows = hidden[ROWS * x : ROWS * x + ROWS]
            for oy in range(3):
                for j in range(0, SLOTS, 2):
                    both = [
                        rows[W * i + 1 + oy : W * i + 9 + oy] for i in (j, j + 1)
                    ]
                    src_two[oy, CORE * x + 8 * j : CORE * x + 8 * j + 16, lanes] = (
                        jnp.concatenate(both, axis=0).astype(BF16)
                    )

    middle = slice(2 * CORE, 10 * CORE)
    errors_t = []
    for g in range(2):
        lanes = slice(256 * g, 256 * g + 256)
        pre = conv(src_two, fwd_two, g, [(0, 8 * CORE)], CORE) * scale_two + shift_two
        pre = pre + core_in[middle, lanes]
        s = jax.nn.sigmoid(pre)
        mask = core_mask[middle, lanes]
        result = pre * s * mask
        grad = target[:, lanes] * mask * (s * (1.0 + pre * (1.0 - s)))
        errors_t.append((grad * scale_two).T.astype(BF16))
        res[:, lanes] = result.astype(BF16)
        for x in range(8):
            for j in range(SLOTS):
                spot = CORE * x + 8 * j
                frame[x, W * j + 2 : W * j + 10, lanes] = grad[spot : spot + 8]

    def spread(x, carry):
        base = pl.multiple_of((x + 2) * ROWS, ROWS)
        for g in range(2):
            lanes = slice(256 * g, 256 * g + 256)
            for oy, moved in enumerate(shifted(frame[x, :, lanes] * scale_two)):
                err_two[oy, pl.ds(base, ROWS), lanes] = moved.astype(BF16)
        return carry

    lax.fori_loop(0, 8, spread, 0, unroll=2)

    def send_block(k, b):
        if not comm:
            got_x[k, 0, b] = blocks[k, b]
            return

        @pl.when(gx != b)
        def _():
            remote(
                blocks.at[k, b],
                got_x.at[k, gx, 0],
                sum_send.at[k, 0],
                sum_recv.at[k, 0],
                (b, gy),
            ).start()

        @pl.when(gx == b)
        def _():
            got_x[k, gx, 0] = blocks[k, b]

    def owners(act):
        if comm:
            pl.when(gx < USED)(act)
        else:
            act()

    def reduce_x(k):
        def act():
            if comm:
                all_wait(got_x.at[k, 0 : n_gx - 1], sum_recv.at[k, 0])
            total = got_x[k, 0].astype(F32)
            for s in range(1, n_gx):
                total = total + got_x[k, s].astype(F32)
            half[0, k] = total.astype(BF16)
            for d in range(1, n_gy):
                remote(
                    half.at[0, k],
                    got_y.at[k, gy],
                    sum_send.at[k, 1],
                    sum_recv.at[k, 1],
                    (gx, lax.rem(gy + d, n_gy)),
                ).start()
            got_y[k, gy] = half[0, k]

        owners(act)

    def reduce_y(k):
        def act():
            if comm:
                all_wait(got_y.at[k, 0 : n_gy - 1], sum_recv.at[k, 1])
            total = got_y[k, 0].astype(F32)
            for s in range(1, n_gy):
                total = total + got_y[k, s].astype(F32)
            half[1, k] = total.astype(BF16)
            for d in range(1, n_gx):
                remote(
                    half.at[1, k],
                    full.at[k, gx],
                    sum_send.at[k, 2],
                    sum_recv.at[k, 2],
                    (lax.rem(gx + d, n_gx), gy),
                ).start()
            full[k, gx] = half[1, k]

        owners(act)

    weight_sums(
        errors_t, src_two, 8 * CORE, CORE, folded, blocks, 1, send_block
    )

    errors_t = []
    for g in range(2):
        lanes = slice(256 * g, 256 * g + 256)
        back = conv(err_two, adj_two, g, [(0, 10 * ROWS)], ROWS)
        error = back * slope[:, lanes]
        errors_t.append(error.T.astype(BF16))
        for x in range(10):
            rows = error[ROWS * x : ROWS * x + ROWS]
            spot = slice(ROWS * (x + 2), ROWS * (x + 3))
            for oy, moved in enumerate(shifted(rows)):
                err_one[oy, spot, lanes] = moved.astype(BF16)
    weight_sums(
        errors_t, src_one, 10 * ROWS, ROWS, folded, blocks, 0, send_block
    )
    reduce_x(1)

    def adjoint_one(g, columns):
        lanes = slice(256 * g, 256 * g + 256)
        spans = [(ROWS * x, ROWS * n) for x, n in columns]
        back = conv(err_one, adj_one, g, spans, ROWS)
        done = 0
        for start, n in columns:
            for x in range(start, start + n):
                rows = back[ROWS * done : ROWS * done + ROWS]
                if 2 <= x < 10:
                    rows = rows + frame[x - 2, :, lanes]
                grad_region[x, :, lanes] = rows.astype(BF16)
                done += 1

    def collect(x):
        total = None
        for bx in range(BX):
            if 0 <= x - 8 * bx < W:
                part = jnp.dot(
                    put_grad[bx * (ny + 16) : (bx + 1) * (ny + 16), :],
                    grad_region[x - 8 * bx],
                    preferred_element_type=F32,
                )
                total = part if total is None else total + part
        return total

    for g in range(2):
        adjoint_one(g, [(0, 2), (10, 2)])
    edges = []

    def send_edges(kinds):
        for i, (dx, dy) in enumerate(HALOS):
            if (dx, dy) not in kinds:
                continue
            a, b = (dx + 1) // 2, (dy + 1) // 2
            if dy == 0:
                src, dst = out_x.at[a], in_x.at[1 - a]
            elif dx == 0:
                src, dst = out_y.at[b], in_y.at[1 - b]
            else:
                src, dst = out_c.at[a, b], in_c.at[1 - a, 1 - b]
            copy = remote(
                src, dst, edge_send.at[i], edge_recv.at[i], device(dx, dy)
            )
            copy.start()
            edges.append(copy)

    if comm:
        for a, x in enumerate((0, nx + 2)):
            pair = [collect(x + k) for k in range(2)]
            for k in range(2):
                out_x[a, k] = pair[k][8 : ny + 8].astype(BF16)
            for b, t in enumerate((0, ny + 8)):
                both = [value[t : t + 8] for value in pair]
                out_c[a, b] = jnp.concatenate(both, axis=0).astype(BF16)
        send_edges([h for h in HALOS if h[0]])

    adjoint_one(0, [(2, 8)])
    reduce_x(0)
    adjoint_one(1, [(2, 8)])

    reduce_y(1)

    for x in range(2, nx + 2):
        value = collect(x)
        gsum[x] = value
        if comm:
            rows = slice(2 * (x - 2), 2 * (x - 2) + 2)
            edge_rows[0, rows, :] = value[6:8]
            edge_rows[1, rows, :] = value[ny + 8 : ny + 10]
    if comm:
        out_y[...] = edge_rows[...].astype(BF16)
        send_edges([h for h in HALOS if not h[0]])
    reduce_y(0)

    def deposit(x, carry):
        rows = res[pl.ds(pl.multiple_of(x * CORE, CORE), CORE), :]
        value = jnp.dot(put_out[...], rows, preferred_element_type=F32).astype(BF16)
        out[x] = value[:ny]
        out[8 + x] = value[ny:]
        return carry

    lax.fori_loop(0, 8, deposit, 0, unroll=4)

    if comm:
        for copy in edges:
            copy.wait_recv()
        x_in = [
            jnp.where(inside, 1.0, 0.0).astype(F32)
            for inside in (gx > 0, gx < n_gx - 1)
        ]
        y_in = [
            jnp.where(inside, 1.0, 0.0).astype(F32)
            for inside in (gy > 0, gy < n_gy - 1)
        ]
        for a, x in enumerate((2, nx)):
            gsum[x : x + 2, 8 : ny + 8, :] += in_x[a].astype(F32) * x_in[a]
            for b, t in enumerate((8, ny)):
                rows = in_c[a, b].astype(F32) * (x_in[a] * y_in[b])
                for k in range(2):
                    gsum[x + k, t : t + 8, :] += rows[8 * k : 8 * k + 8]
        for b, t in enumerate((8, ny + 6)):
            rows = in_y[b].astype(F32) * y_in[b]
            for i in range(nx):
                gsum[2 + i, t : t + 2, :] += rows[2 * i : 2 * i + 2]

    def finish(x, carry):
        mask = height_mask(elh[x + 2, 16 : ny + 16, :].astype(F32))
        for c in range(4):
            lanes = slice(128 * c, 128 * c + 128)
            value = gsum[x + 2, 8 : ny + 8, lanes]
            gfeat[x, :, lanes] = jnp.where(mask[c], value, 0.0).astype(BF16)
        return carry

    lax.fori_loop(0, nx, finish, 0, unroll=4)

    if comm:
        for copy in edges:
            copy.wait_send()
        for k, ref in enumerate((ext, elh)):
            all_wait(ref.at[0 : margin // ny, 0:ny], halo_send.at[k])

        @pl.when(gx < USED)
        def _():
            for k in range(2):
                all_wait(full.at[k, 0 : USED - 1], sum_recv.at[k, 2])
                all_wait(blocks.at[k, 0 : USED - 1], sum_send.at[k, 0])
                all_wait(got_y.at[k, 0 : n_gy - 1], sum_send.at[k, 1])
                all_wait(full.at[k, 0 : n_gx - 1], sum_send.at[k, 2])

        @pl.when(gx >= USED)
        def _():
            for k in range(2):
                all_wait(full.at[k, 0:USED], sum_recv.at[k, 2])
                all_wait(blocks.at[k, 0:USED], sum_send.at[k, 0])


def result_kernel(
    factor, per, out_in, gfeat_in, full, out, gfeat, gw_one, gw_two, one, two, sem
):
    copies = [
        pltpu.make_async_copy(out_in, out, sem.at[0]),
        pltpu.make_async_copy(gfeat_in, gfeat, sem.at[1]),
    ]
    for copy in copies:
        copy.start()
    for k, (ref, gw) in enumerate(((one, gw_one), (two, gw_two))):
        unfold(full, per, k, ref, factor)
        copy = pltpu.make_async_copy(ref, gw, sem.at[2 + k])
        copy.start()
        copies.append(copy)
    for copy in copies:
        copy.wait()


def run(
    n_gx,
    n_gy,
    features,
    cotangent,
    low,
    high,
    weight_one,
    weight_two,
    scale_one,
    shift_one,
    scale_two,
    shift_two,
):
    nx, ny = features.shape[0], features.shape[1]
    per = BLOCKS // n_gx
    whole = pl.BlockSpec(memory_space=pltpu.VMEM)
    left = pl.BlockSpec(memory_space=pl.ANY)
    vm = pltpu.VMEM
    dma = pltpu.SemaphoreType.DMA
    scratch = [
        vm((nx, ny, WIDTH), BF16),
        vm((27 * C, C), BF16),
        vm((27 * C, C), BF16),
        vm((nx, ny), jnp.int32),
        vm((nx, ny), jnp.int32),
        vm((4, 1, C), F32),
        vm((nx, ny, 128), BF16),
        vm((nx + 4, ny + 32, WIDTH), BF16),
        vm((nx + 4, ny + 32, 128), BF16),
        vm((3 * ROWS + CORE, 2 * ny + 64), BF16),
        vm((ROWS + CORE, 2 * ny + 64), BF16),
        vm((CORE, 2 * ny), BF16),
        vm((2 * ny, CORE), BF16),
        vm((2 * ny + 32, ROWS), BF16),
        vm((3, W * ROWS, WIDTH), BF16),
        vm((3, 10 * CORE, WIDTH), BF16),
        vm((3, W * ROWS, WIDTH), BF16),
        vm((3, (W + 2) * ROWS, WIDTH), BF16),
        vm((W * ROWS, WIDTH), F32),
        vm((W * CORE, WIDTH), F32),
        vm((W * CORE, WIDTH), F32),
        vm((8 * CORE, WIDTH), F32),
        vm((10 * ROWS, WIDTH), F32),
        vm((8, ROWS, WIDTH), F32),
        vm((8 * CORE, WIDTH), BF16),
        vm((W, ROWS, WIDTH), BF16),
        vm((nx + 4, ny + 16, WIDTH), F32),
        vm((9 * 512, 256), BF16),
        vm((9 * 512, 256), BF16),
        vm((9 * 512, 256), BF16),
        vm((9 * 512, 256), BF16),
        vm((9, 64, 128), F32),
        vm((2, BLOCKS, 64, 128), BF16),
        vm((2, n_gx, per, 64, 128), BF16),
        vm((2, 2, per, 64, 128), BF16),
        vm((2, n_gy, per, 64, 128), BF16),
        vm((2, 2, ny, WIDTH), BF16),
        vm((2, 2, ny, WIDTH), BF16),
        vm((2, 2 * nx, WIDTH), F32),
        vm((2, 2 * nx, WIDTH), BF16),
        vm((2, 2 * nx, WIDTH), BF16),
        vm((2, 2, 16, WIDTH), BF16),
        vm((2, 2, 16, WIDTH), BF16),
        dma((11,)),
        dma((2,)),
        dma((2,)),
        dma((8,)),
        dma((8,)),
        dma((2, 3)),
        dma((2, 3)),
    ]
    comm = n_gx * n_gy > 1
    params = pltpu.CompilerParams(
        collective_id=0 if comm else None,
        has_side_effects=comm,
        vmem_limit_bytes=46 * 2**20,
    )
    in_hbm = functools.partial(
        pltpu.with_memory_space_constraint, memory_space=pltpu.HBM
    )
    columns = jax.ShapeDtypeStruct(features.shape, BF16)
    out, gfeat, full = pl.pallas_call(
        functools.partial(block_kernel, n_gx, n_gy),
        out_shape=(
            columns,
            columns,
            jax.ShapeDtypeStruct((2, n_gx, per, 64, 128), BF16),
        ),
        in_specs=[pl.BlockSpec(memory_space=pltpu.HBM)] * 10,
        out_specs=(whole,) * 3,
        scratch_shapes=scratch,
        compiler_params=params,
        name="residual_block",
    )(
        in_hbm(features),
        in_hbm(cotangent),
        in_hbm(weight_one.reshape(27 * C, C)),
        in_hbm(weight_two.reshape(27 * C, C)),
        in_hbm(low),
        in_hbm(high),
        in_hbm(scale_one.reshape(1, C)),
        in_hbm(shift_one.reshape(1, C)),
        in_hbm(scale_two.reshape(1, C)),
        in_hbm(shift_two.reshape(1, C)),
    )
    sums = jax.ShapeDtypeStruct((27 * C, C), F32)
    out, gfeat, gw_one, gw_two = pl.pallas_call(
        functools.partial(result_kernel, 1.0 / (n_gx * n_gy * SHARE), per),
        out_shape=(columns, columns, sums, sums),
        in_specs=[left, left, whole],
        out_specs=(left,) * 4,
        scratch_shapes=[vm((27 * C, C), F32), vm((27 * C, C), F32), dma((4,))],
        compiler_params=pltpu.CompilerParams(vmem_limit_bytes=8 * 2**20),
        name="results",
    )(out, gfeat, full)
    return out, gfeat, gw_one.reshape(27, C, C), gw_two.reshape(27, C, C)


def solution(mesh):
    columns = P("gx", "gy", None)
    placed = (columns, columns, P("gx", "gy"), P("gx", "gy")) + (P(),) * 6
    return jax.shard_map(
        functools.partial(run, mesh.shape["gx"], mesh.shape["gy"]),
        mesh=mesh,
        in_specs=placed,
        out_specs=(columns, columns, P(), P()),
        check_vma=False,
    )
```

```python
import functools

import jax
import jax.numpy as jnp
from jax import lax
from jax.experimental import pallas as pl
from jax.experimental.pallas import tpu as pltpu
from jax.sharding import PartitionSpec as P

MESH = pl.DeviceIdType.MESH
F32 = jnp.float32
BF16 = jnp.bfloat16
BRICK = 8
C = 64
WIDTH = 512
SLOTS = 4
SHARE = 2
BX, BY = 2, 8
W = 12
ROWS = SLOTS * W
CORE = SLOTS * BRICK
BLOCKS = 16
USED = 14
HALOS = [(dx, dy) for dx in (-1, 0, 1) for dy in (-1, 0, 1) if dx or dy]


def lane(shape):
    return lax.broadcasted_iota(jnp.int32, shape, len(shape) - 1)


def turned(value):
    return pltpu.roll(value, 64, value.ndim - 1)


def height_mask(bounds):
    first = lane(bounds.shape) < 64
    other = turned(bounds)
    low, high = jnp.where(first, bounds, other), jnp.where(first, other, bounds)
    step = jnp.where(first, 0.0, 1.0)
    return [(step + 2.0 * c >= low) & (step + 2.0 * c < high) for c in range(4)]


def toeplitz(one, two, pair_ref, t):
    first = lane(one.shape) < 64
    zero = jnp.zeros(one.shape, BF16)
    start = jnp.where(first, turned(one), 0.0).astype(BF16)
    end = jnp.where(first, 0.0, turned(two)).astype(BF16)
    one, two = one.astype(BF16), two.astype(BF16)
    rows = pl.ds(pl.multiple_of(t * 512, 512), 512)
    columns = (
        [zero, start, one, two, end, zero, zero, zero],
        [zero, zero, zero, start, one, two, end, zero],
    )
    for c in range(2):
        pair_ref[rows, 128 * c : 128 * c + 128] = jnp.concatenate(columns[c], axis=0)


def build_weights(w_ref, forward_ref, adjoint_ref):
    def tap(t, carry):
        rows = w_ref[pl.ds(pl.multiple_of(t * 192, 192), 192), :].astype(F32)
        lower, middle, upper = rows[:64], rows[64:128], rows[128:]
        toeplitz(
            jnp.concatenate([middle, lower], axis=1),
            jnp.concatenate([upper, middle], axis=1),
            forward_ref,
            t,
        )
        toeplitz(rows[64:192].T, rows[0:128].T, adjoint_ref, 8 - t)
        return carry

    lax.fori_loop(0, 9, tap, 0, unroll=3)


def conv(source, band_ref, g, spans, pitch):
    lanes = slice(128 * g, 128 * g + 384)
    parts = [
        jnp.concatenate(
            [
                source[oy, start + ox * pitch : start + ox * pitch + count, lanes]
                for ox in range(3)
                for oy in range(3)
            ],
            axis=1,
        )
        for start, count in spans
    ]
    rows = parts[0] if len(parts) == 1 else jnp.concatenate(parts, axis=0)
    skip = 128 * (1 - g)
    band = jnp.concatenate(
        [band_ref[512 * t + skip : 512 * t + skip + 384, :] for t in range(9)], axis=0
    )
    return jnp.dot(rows, band, preferred_element_type=F32)


def shifted(value):
    count = value.shape[0]
    return (pltpu.roll(value, 1, 0), value, pltpu.roll(value, count - 1, 0))


def fold(results, fold_ref, block_ref, k, t0):
    for oy in range(3):
        sums = {}
        for g in range(2):
            for z in range(4 * g, 4 * g + 4):
                for c in range(3):
                    kind = (z % 2, 2 * g + 2 * c - z)
                    if kind in ((0, 0), (0, -2), (1, -1), (1, 1)):
                        zo = z - 4 * g
                        block = results[g][
                            64 * zo : 64 * zo + 64,
                            384 * oy + 128 * c : 384 * oy + 128 * c + 128,
                        ]
                        sums[kind] = sums[kind] + block if kind in sums else block
        p, u, q, s = sums[0, 0], sums[0, -2], sums[1, -1], sums[1, 1]
        first = lane(p.shape) < 64
        block_ref[k, t0 + oy] = (q + turned(jnp.where(first, p, u))).astype(BF16)
        fold_ref[t0 + oy] = p + turned(s)


def weight_sums(errors_t, source, count, pitch, fold_ref, block_ref, k, send):
    def column(ox, carry):
        base = pl.multiple_of(ox * pitch, 16)
        results = []
        for g in range(2):
            lanes = slice(128 * g, 128 * g + 384)
            window = jnp.concatenate(
                [source[oy, pl.ds(base, count), lanes] for oy in range(3)], axis=1
            )
            results.append(
                jnp.dot(errors_t[g], window, preferred_element_type=F32)
            )
        fold(results, fold_ref, block_ref, k, 3 * ox)
        if send:
            for oy in range(3):
                send(k, 3 * ox + oy)
        return carry

    lax.fori_loop(0, 3, column, 0)
    first = lane((64, 128)) < 64
    for i in range(5):
        even = turned(fold_ref[2 * i])
        odd = fold_ref[2 * i + 1] if i < 4 else jnp.zeros_like(even)
        block_ref[k, 9 + i] = jnp.where(first, even, odd).astype(BF16)
        if send:
            send(k, 9 + i)


def unfold(blocks_ref, per, k, out_ref, factor):
    for t in range(9):
        block = blocks_ref[k, t // per, t % per].astype(F32) * factor
        out_ref[192 * t : 192 * t + 128, :] = block.T
    for i in range(5):
        block = (blocks_ref[k, (9 + i) // per, (9 + i) % per].astype(F32) * factor).T
        out_ref[384 * i + 128 : 384 * i + 192, :] = block[:64]
        if i < 4:
            out_ref[384 * i + 320 : 384 * i + 384, :] = block[64:]


def block_kernel(
    n_gx,
    n_gy,
    feat,
    cot_in,
    w_one_in,
    w_two_in,
    low_in,
    high_in,
    scale_one_in,
    shift_one_in,
    scale_two_in,
    shift_two_in,
    out,
    gfeat,
    full,
    cot,
    w_one,
    w_two,
    low,
    high,
    scales,
    bounds,
    ext,
    elh,
    pick_in,
    pick_bounds,
    pick_target,
    put_out,
    put_grad,
    src_one,
    src_two,
    err_two,
    err_one,
    msk,
    core_in,
    core_mask,
    target,
    slope,
    frame,
    res,
    grad_region,
    gsum,
    fwd_one,
    adj_one,
    fwd_two,
    adj_two,
    folded,
    blocks,
    got_x,
    half,
    got_y,
    out_x,
    in_x,
    edge_rows,
    out_y,
    in_y,
    out_c,
    in_c,
    local_sem,
    halo_send,
    halo_recv,
    edge_send,
    edge_recv,
    sum_send,
    sum_recv,
):
    comm = n_gx * n_gy > 1
    if comm:
        gx, gy = lax.axis_index("gx"), lax.axis_index("gy")
    else:
        gx, gy = 0, 0
    nx, ny = feat.shape[0], feat.shape[1]
    per = BLOCKS // n_gx

    inputs = [
        pltpu.make_async_copy(src, dst, local_sem.at[2 + k])
        for k, (src, dst) in enumerate(
            ((w_one_in, w_one), (w_two_in, w_two), (cot_in, cot))
        )
    ]

    def device(dx, dy):
        return (lax.rem(gx + dx + n_gx, n_gx), lax.rem(gy + dy + n_gy, n_gy))

    if comm:
        for ref in (ext, elh):
            strip = jnp.zeros((nx + 4, 16, ref.shape[2]), BF16)
            ref[:, 0:16, :] = strip
            ref[:, ny + 16 : ny + 32, :] = strip
        barrier = pltpu.get_barrier_semaphore()
        peers = [(d, 0) for d in range(1, n_gx)] + [(0, d) for d in range(1, n_gy)]
        peers += [(dx, dy) for dx, dy in HALOS if dx and dy]
        for dx, dy in peers:
            pl.semaphore_signal(
                barrier, inc=1, device_id=device(dx, dy), device_id_type=MESH
            )

    own = pltpu.make_async_copy(
        feat, ext.at[2 : nx + 2, 16 : ny + 16], local_sem.at[0]
    )
    own.start()
    small = [
        pltpu.make_async_copy(src, dst, local_sem.at[5 + k])
        for k, (src, dst) in enumerate(
            (
                (low_in, low),
                (high_in, high),
                (scale_one_in, scales.at[0]),
                (shift_one_in, scales.at[1]),
                (scale_two_in, scales.at[2]),
                (shift_two_in, scales.at[3]),
            )
        )
    ]
    for copy in small + inputs:
        copy.start()
    for copy in small:
        copy.wait()

    first = lane((ny, 128)) < 64
    square = jnp.zeros((ny, ny), F32)
    lows = jnp.concatenate([low[...].astype(F32), square[nx:]], axis=0).T
    highs = jnp.concatenate([high[...].astype(F32), square[nx:]], axis=0).T
    for x in range(nx):
        both = jnp.where(first, lows[:, x : x + 1], highs[:, x : x + 1]).astype(BF16)
        bounds[x] = both
        elh[x + 2, 16 : ny + 16, :] = both
    def all_wait(like, sem):
        pltpu.make_async_copy(like, like, sem).wait()

    def remote(src, dst, send, recv, to):
        return pltpu.make_async_remote_copy(
            src_ref=src,
            dst_ref=dst,
            send_sem=send,
            recv_sem=recv,
            device_id=to,
            device_id_type=MESH,
        )


    if comm:
        pl.semaphore_wait(barrier, len(peers))
    if comm:
        x_from = {-1: slice(0, 2), 0: slice(0, nx), 1: slice(nx - 2, nx)}
        x_to = {-1: slice(nx + 2, nx + 4), 0: slice(2, nx + 2), 1: slice(0, 2)}
        y_from = {-1: slice(0, 2), 0: slice(0, ny), 1: slice(ny - 2, ny)}
        y_to = {
            -1: slice(ny + 16, ny + 18),
            0: slice(16, ny + 16),
            1: slice(14, 16),
        }
        order = sorted(HALOS, key=lambda h: -(2 * abs(h[0]) - abs(h[1])))
        for dx, dy in order:
            for k, (src, dst) in enumerate(((feat, ext), (bounds, elh))):
                copy = remote(
                    src.at[x_from[dx], y_from[dy]],
                    dst.at[x_to[dx], y_to[dy]],
                    halo_send.at[k],
                    halo_recv.at[k],
                    device(dx, dy),
                )
                copy.start()
    inputs[0].wait()
    build_weights(w_one, fwd_one, adj_one)
    inputs[1].wait()
    build_weights(w_two, fwd_two, adj_two)
    nothing = jnp.zeros((3, 2 * ROWS, WIDTH), BF16)
    err_two[:, 0 : 2 * ROWS, :] = nothing
    err_two[:, 10 * ROWS : 12 * ROWS, :] = nothing
    err_one[:, 0 : 2 * ROWS, :] = nothing
    err_one[:, 12 * ROWS : 14 * ROWS, :] = nothing
    frame[...] = jnp.zeros_like(frame)

    occupied = jnp.where(high[...] > low[...], 1, 0)
    by_lane = lane((8, ny))
    count = jnp.int32(0)
    brick = [jnp.int32(-1000)] * SLOTS
    for bx in range(BX):
        rows = occupied[8 * bx : 8 * bx + 8]
        for by in range(BY):
            inside = (by_lane >= 8 * by) & (by_lane < 8 * by + 8)
            filled = jnp.max(jnp.where(inside, rows, 0))
            for j in range(SLOTS):
                hit = (filled > 0) & (count == j)
                brick[j] = jnp.where(hit, 8 * bx + by, brick[j])
            count = count + filled

    def picks(rows, columns, row_dim, per_brick, pitch, offset):
        shape = (rows, columns) if row_dim == 0 else (columns, rows)
        row = lax.broadcasted_iota(jnp.int32, shape, row_dim)
        column = lax.broadcasted_iota(jnp.int32, shape, 1 - row_dim)
        wanted = row + offset
        for j in range(SLOTS):
            b = brick[j]
            bx = jnp.where(b >= BY, 1, 0)
            spot = jnp.where(b < 0, -4000, bx * pitch + 8 * (b - BY * bx)) - per_brick * j
            inside = (row >= per_brick * j) & (row < per_brick * j + per_brick)
            wanted = wanted + jnp.where(inside, spot, 0)
        return jnp.where(column == wanted, 1.0, 0.0).astype(BF16)

    tall = ny + 32
    core_pick = picks(CORE, 2 * tall, 0, BRICK, tall, 16)
    frame_pick = [picks(ROWS, 2 * tall, 0, W, tall, 13 + oy) for oy in range(3)]
    pick_in[...] = jnp.concatenate(frame_pick + [core_pick], axis=0)
    pick_bounds[...] = jnp.concatenate([frame_pick[1], core_pick], axis=0)
    pick_target[...] = picks(CORE, 2 * ny, 0, BRICK, ny, 0)
    put_out[...] = picks(CORE, 2 * ny, 1, BRICK, ny, 0)
    put_grad[...] = picks(ROWS, 2 * (ny + 16), 1, W, ny + 16, 6)

    inputs[2].wait()
    def cut_target(x, carry):
        rows = jnp.concatenate([cot[x], cot[8 + x]], axis=0)
        spot = pl.ds(pl.multiple_of(x * CORE, CORE), CORE)
        target[spot, :] = jnp.dot(pick_target[...], rows, preferred_element_type=F32)
        return carry

    lax.fori_loop(0, 8, cut_target, 0, unroll=8)

    def mask_in(xs, ys):
        mask = height_mask(elh[xs, ys, :].astype(F32))
        for c in range(4):
            lanes = slice(128 * c, 128 * c + 128)
            value = ext[xs, ys, lanes].astype(F32)
            ext[xs, ys, lanes] = jnp.where(mask[c], value, 0.0).astype(BF16)

    def mask_inner(i, carry):
        mask_in(pl.ds(2 + 2 * i, 2), slice(16, ny + 16))
        return carry

    own.wait()
    lax.fori_loop(0, nx // 2, mask_inner, 0, unroll=2)
    if comm:
        margin = (nx + 4) * (ny + 4) - nx * ny
        for k, ref in enumerate((ext, elh)):
            all_wait(ref.at[0 : margin // 48, 0:48], halo_recv.at[k])
    if comm:
        for spot, inside in (
            ((slice(0, 2), slice(None)), gx > 0),
            ((slice(nx + 2, nx + 4), slice(None)), gx < n_gx - 1),
            ((slice(None), slice(0, 16)), gy > 0),
            ((slice(None), slice(ny + 16, ny + 32)), gy < n_gy - 1),
        ):
            value = elh[spot[0], spot[1], :].astype(F32)
            elh[spot[0], spot[1], :] = (
                value * jnp.where(inside, 1.0, 0.0).astype(F32)
            ).astype(BF16)
    else:
        for spot in (slice(0, 2), slice(nx + 2, nx + 4)):
            elh[spot] = jnp.zeros_like(elh[spot])
            ext[spot] = jnp.zeros_like(ext[spot])
        for spot in (slice(0, 16), slice(ny + 16, ny + 32)):
            elh[:, spot] = jnp.zeros_like(elh[:, spot])
            ext[:, spot] = jnp.zeros_like(ext[:, spot])

    for x in range(2, nx + 2, 4):
        mask_in(slice(x, x + 4), slice(0, 16))
        mask_in(slice(x, x + 4), slice(ny + 16, tall))
    for x in (0, 1, nx + 2, nx + 3):
        mask_in(slice(x, x + 1), slice(0, tall))

    def cut(x, carry):
        base = pl.multiple_of(x * ROWS, ROWS)
        core = pl.multiple_of(x * CORE, CORE)
        rows = jnp.concatenate([ext[x], ext[8 + x]], axis=0)
        value = jnp.dot(pick_in[...], rows, preferred_element_type=F32)
        for oy in range(3):
            src_one[oy, pl.ds(base, ROWS), :] = value[
                ROWS * oy : ROWS * oy + ROWS
            ].astype(BF16)
        core_in[pl.ds(core, CORE), :] = value[3 * ROWS :]
        rows = jnp.concatenate([elh[x], elh[8 + x]], axis=0)
        mask = height_mask(
            jnp.dot(pick_bounds[...], rows, preferred_element_type=F32)
        )
        for c in range(4):
            lanes = slice(128 * c, 128 * c + 128)
            value = jnp.where(mask[c], 1.0, 0.0)
            msk[pl.ds(base, ROWS), lanes] = value[:ROWS]
            core_mask[pl.ds(core, CORE), lanes] = value[ROWS:]
        return carry

    lax.fori_loop(0, W, cut, 0, unroll=4)

    scale_one, shift_one, scale_two, shift_two = (
        jnp.concatenate([scales[k]] * 4, axis=1) for k in range(4)
    )

    for g in range(2):
        lanes = slice(256 * g, 256 * g + 256)
        pre = conv(src_one, fwd_one, g, [(0, 10 * ROWS)], ROWS) * scale_one + shift_one
        s = jax.nn.sigmoid(pre)
        mask = msk[ROWS : 11 * ROWS, lanes]
        hidden = pre * s * mask
        slope[:, lanes] = s * (1.0 + pre * (1.0 - s)) * mask * scale_one
        for x in range(10):
            rows = hidden[ROWS * x : ROWS * x + ROWS]
            for oy in range(3):
                for j in range(0, SLOTS, 2):
                    both = [
                        rows[W * i + 1 + oy : W * i + 9 + oy] for i in (j, j + 1)
                    ]
                    src_two[oy, CORE * x + 8 * j : CORE * x + 8 * j + 16, lanes] = (
                        jnp.concatenate(both, axis=0).astype(BF16)
                    )

    middle = slice(2 * CORE, 10 * CORE)
    errors_t = []
    for g in range(2):
        lanes = slice(256 * g, 256 * g + 256)
        pre = conv(src_two, fwd_two, g, [(0, 8 * CORE)], CORE) * scale_two + shift_two
        pre = pre + core_in[middle, lanes]
        s = jax.nn.sigmoid(pre)
        mask = core_mask[middle, lanes]
        result = pre * s * mask
        grad = target[:, lanes] * mask * (s * (1.0 + pre * (1.0 - s)))
        errors_t.append((grad * scale_two).T.astype(BF16))
        res[:, lanes] = result.astype(BF16)
        for x in range(8):
            for j in range(SLOTS):
                spot = CORE * x + 8 * j
                frame[x, W * j + 2 : W * j + 10, lanes] = grad[spot : spot + 8]

    def spread(x, carry):
        base = pl.multiple_of((x + 2) * ROWS, ROWS)
        for g in range(2):
            lanes = slice(256 * g, 256 * g + 256)
            for oy, moved in enumerate(shifted(frame[x, :, lanes] * scale_two)):
                err_two[oy, pl.ds(base, ROWS), lanes] = moved.astype(BF16)
        return carry

    lax.fori_loop(0, 8, spread, 0, unroll=2)

    def send_block(k, b):
        if not comm:
            got_x[k, 0, b] = blocks[k, b]
            return

        @pl.when(gx != b)
        def _():
            remote(
                blocks.at[k, b],
                got_x.at[k, gx, 0],
                sum_send.at[k, 0],
                sum_recv.at[k, 0],
                (b, gy),
            ).start()

        @pl.when(gx == b)
        def _():
            got_x[k, gx, 0] = blocks[k, b]

    def owners(act):
        if comm:
            pl.when(gx < USED)(act)
        else:
            act()

    def reduce_x(k):
        def act():
            if comm:
                all_wait(got_x.at[k, 0 : n_gx - 1], sum_recv.at[k, 0])
            total = got_x[k, 0].astype(F32)
            for s in range(1, n_gx):
                total = total + got_x[k, s].astype(F32)
            half[0, k] = total.astype(BF16)
            for d in range(1, n_gy):
                remote(
                    half.at[0, k],
                    got_y.at[k, gy],
                    sum_send.at[k, 1],
                    sum_recv.at[k, 1],
                    (gx, lax.rem(gy + d, n_gy)),
                ).start()
            got_y[k, gy] = half[0, k]

        owners(act)

    def reduce_y(k):
        def act():
            if comm:
                all_wait(got_y.at[k, 0 : n_gy - 1], sum_recv.at[k, 1])
            total = got_y[k, 0].astype(F32)
            for s in range(1, n_gy):
                total = total + got_y[k, s].astype(F32)
            half[1, k] = total.astype(BF16)
            for d in range(1, n_gx):
                remote(
                    half.at[1, k],
                    full.at[k, gx],
                    sum_send.at[k, 2],
                    sum_recv.at[k, 2],
                    (lax.rem(gx + d, n_gx), gy),
                ).start()
            full[k, gx] = half[1, k]

        owners(act)

    weight_sums(
        errors_t, src_two, 8 * CORE, CORE, folded, blocks, 1, send_block
    )

    errors_t = []
    for g in range(2):
        lanes = slice(256 * g, 256 * g + 256)
        back = conv(err_two, adj_two, g, [(0, 10 * ROWS)], ROWS)
        error = back * slope[:, lanes]
        errors_t.append(error.T.astype(BF16))
        for x in range(10):
            rows = error[ROWS * x : ROWS * x + ROWS]
            spot = slice(ROWS * (x + 2), ROWS * (x + 3))
            for oy, moved in enumerate(shifted(rows)):
                err_one[oy, spot, lanes] = moved.astype(BF16)
    weight_sums(
        errors_t, src_one, 10 * ROWS, ROWS, folded, blocks, 0, send_block
    )
    reduce_x(1)

    def adjoint_one(g, columns):
        lanes = slice(256 * g, 256 * g + 256)
        spans = [(ROWS * x, ROWS * n) for x, n in columns]
        back = conv(err_one, adj_one, g, spans, ROWS)
        done = 0
        for start, n in columns:
            for x in range(start, start + n):
                rows = back[ROWS * done : ROWS * done + ROWS]
                if 2 <= x < 10:
                    rows = rows + frame[x - 2, :, lanes]
                grad_region[x, :, lanes] = rows.astype(BF16)
                done += 1

    def collect(x):
        total = None
        for bx in range(BX):
            if 0 <= x - 8 * bx < W:
                part = jnp.dot(
                    put_grad[bx * (ny + 16) : (bx + 1) * (ny + 16), :],
                    grad_region[x - 8 * bx],
                    preferred_element_type=F32,
                )
                total = part if total is None else total + part
        return total

    for g in range(2):
        adjoint_one(g, [(0, 2), (10, 2)])
    edges = []

    def send_edges(kinds):
        for i, (dx, dy) in enumerate(HALOS):
            if (dx, dy) not in kinds:
                continue
            a, b = (dx + 1) // 2, (dy + 1) // 2
            if dy == 0:
                src, dst = out_x.at[a], in_x.at[1 - a]
            elif dx == 0:
                src, dst = out_y.at[b], in_y.at[1 - b]
            else:
                src, dst = out_c.at[a, b], in_c.at[1 - a, 1 - b]
            copy = remote(
                src, dst, edge_send.at[i], edge_recv.at[i], device(dx, dy)
            )
            copy.start()
            edges.append(copy)

    if comm:
        for a, x in enumerate((0, nx + 2)):
            pair = [collect(x + k) for k in range(2)]
            for k in range(2):
                out_x[a, k] = pair[k][8 : ny + 8].astype(BF16)
            for b, t in enumerate((0, ny + 8)):
                both = [value[t : t + 8] for value in pair]
                out_c[a, b] = jnp.concatenate(both, axis=0).astype(BF16)
        send_edges([h for h in HALOS if h[0]])

    adjoint_one(0, [(2, 8)])
    reduce_x(0)
    adjoint_one(1, [(2, 8)])

    reduce_y(1)

    for x in range(2, nx + 2):
        value = collect(x)
        gsum[x] = value
        if comm:
            rows = slice(2 * (x - 2), 2 * (x - 2) + 2)
            edge_rows[0, rows, :] = value[6:8]
            edge_rows[1, rows, :] = value[ny + 8 : ny + 10]
    if comm:
        out_y[...] = edge_rows[...].astype(BF16)
        send_edges([h for h in HALOS if not h[0]])
    reduce_y(0)

    def deposit(x, carry):
        rows = res[pl.ds(pl.multiple_of(x * CORE, CORE), CORE), :]
        value = jnp.dot(put_out[...], rows, preferred_element_type=F32).astype(BF16)
        out[x] = value[:ny]
        out[8 + x] = value[ny:]
        return carry

    lax.fori_loop(0, 8, deposit, 0, unroll=4)

    if comm:
        for copy in edges:
            copy.wait_recv()
        x_in = [
            jnp.where(inside, 1.0, 0.0).astype(F32)
            for inside in (gx > 0, gx < n_gx - 1)
        ]
        y_in = [
            jnp.where(inside, 1.0, 0.0).astype(F32)
            for inside in (gy > 0, gy < n_gy - 1)
        ]
        for a, x in enumerate((2, nx)):
            gsum[x : x + 2, 8 : ny + 8, :] += in_x[a].astype(F32) * x_in[a]
            for b, t in enumerate((8, ny)):
                rows = in_c[a, b].astype(F32) * (x_in[a] * y_in[b])
                for k in range(2):
                    gsum[x + k, t : t + 8, :] += rows[8 * k : 8 * k + 8]
        for b, t in enumerate((8, ny + 6)):
            rows = in_y[b].astype(F32) * y_in[b]
            for i in range(nx):
                gsum[2 + i, t : t + 2, :] += rows[2 * i : 2 * i + 2]

    def finish(x, carry):
        mask = height_mask(elh[x + 2, 16 : ny + 16, :].astype(F32))
        for c in range(4):
            lanes = slice(128 * c, 128 * c + 128)
            value = gsum[x + 2, 8 : ny + 8, lanes]
            gfeat[x, :, lanes] = jnp.where(mask[c], value, 0.0).astype(BF16)
        return carry

    lax.fori_loop(0, nx, finish, 0, unroll=4)

    if comm:
        for copy in edges:
            copy.wait_send()
        for k, ref in enumerate((ext, elh)):
            all_wait(ref.at[0 : margin // 48, 0:48], halo_send.at[k])

        @pl.when(gx < USED)
        def _():
            for k in range(2):
                all_wait(full.at[k, 0 : USED - 1], sum_recv.at[k, 2])
                all_wait(blocks.at[k, 0 : USED - 1], sum_send.at[k, 0])
                all_wait(got_y.at[k, 0 : n_gy - 1], sum_send.at[k, 1])
                all_wait(full.at[k, 0 : n_gx - 1], sum_send.at[k, 2])

        @pl.when(gx >= USED)
        def _():
            for k in range(2):
                all_wait(full.at[k, 0:USED], sum_recv.at[k, 2])
                all_wait(blocks.at[k, 0:USED], sum_send.at[k, 0])


def result_kernel(
    factor, per, out_in, gfeat_in, full, out, gfeat, gw_one, gw_two, one, two, sem
):
    copies = [
        pltpu.make_async_copy(out_in, out, sem.at[0]),
        pltpu.make_async_copy(gfeat_in, gfeat, sem.at[1]),
    ]
    for copy in copies:
        copy.start()
    for k, (ref, gw) in enumerate(((one, gw_one), (two, gw_two))):
        unfold(full, per, k, ref, factor)
        copy = pltpu.make_async_copy(ref, gw, sem.at[2 + k])
        copy.start()
        copies.append(copy)
    for copy in copies:
        copy.wait()


def run(
    n_gx,
    n_gy,
    features,
    cotangent,
    low,
    high,
    weight_one,
    weight_two,
    scale_one,
    shift_one,
    scale_two,
    shift_two,
):
    nx, ny = features.shape[0], features.shape[1]
    per = BLOCKS // n_gx
    whole = pl.BlockSpec(memory_space=pltpu.VMEM)
    left = pl.BlockSpec(memory_space=pl.ANY)
    vm = pltpu.VMEM
    dma = pltpu.SemaphoreType.DMA
    scratch = [
        vm((nx, ny, WIDTH), BF16),
        vm((27 * C, C), BF16),
        vm((27 * C, C), BF16),
        vm((nx, ny), jnp.int32),
        vm((nx, ny), jnp.int32),
        vm((4, 1, C), F32),
        vm((nx, ny, 128), BF16),
        vm((nx + 4, ny + 32, WIDTH), BF16),
        vm((nx + 4, ny + 32, 128), BF16),
        vm((3 * ROWS + CORE, 2 * ny + 64), BF16),
        vm((ROWS + CORE, 2 * ny + 64), BF16),
        vm((CORE, 2 * ny), BF16),
        vm((2 * ny, CORE), BF16),
        vm((2 * ny + 32, ROWS), BF16),
        vm((3, W * ROWS, WIDTH), BF16),
        vm((3, 10 * CORE, WIDTH), BF16),
        vm((3, W * ROWS, WIDTH), BF16),
        vm((3, (W + 2) * ROWS, WIDTH), BF16),
        vm((W * ROWS, WIDTH), F32),
        vm((W * CORE, WIDTH), F32),
        vm((W * CORE, WIDTH), F32),
        vm((8 * CORE, WIDTH), F32),
        vm((10 * ROWS, WIDTH), F32),
        vm((8, ROWS, WIDTH), F32),
        vm((8 * CORE, WIDTH), BF16),
        vm((W, ROWS, WIDTH), BF16),
        vm((nx + 4, ny + 16, WIDTH), F32),
        vm((9 * 512, 256), BF16),
        vm((9 * 512, 256), BF16),
        vm((9 * 512, 256), BF16),
        vm((9 * 512, 256), BF16),
        vm((9, 64, 128), F32),
        vm((2, BLOCKS, 64, 128), BF16),
        vm((2, n_gx, per, 64, 128), BF16),
        vm((2, 2, per, 64, 128), BF16),
        vm((2, n_gy, per, 64, 128), BF16),
        vm((2, 2, ny, WIDTH), BF16),
        vm((2, 2, ny, WIDTH), BF16),
        vm((2, 2 * nx, WIDTH), F32),
        vm((2, 2 * nx, WIDTH), BF16),
        vm((2, 2 * nx, WIDTH), BF16),
        vm((2, 2, 16, WIDTH), BF16),
        vm((2, 2, 16, WIDTH), BF16),
        dma((11,)),
        dma((2,)),
        dma((2,)),
        dma((8,)),
        dma((8,)),
        dma((2, 3)),
        dma((2, 3)),
    ]
    comm = n_gx * n_gy > 1
    params = pltpu.CompilerParams(
        collective_id=0 if comm else None,
        has_side_effects=comm,
        vmem_limit_bytes=46 * 2**20,
    )
    in_hbm = functools.partial(
        pltpu.with_memory_space_constraint, memory_space=pltpu.HBM
    )
    columns = jax.ShapeDtypeStruct(features.shape, BF16)
    out, gfeat, full = pl.pallas_call(
        functools.partial(block_kernel, n_gx, n_gy),
        out_shape=(
            columns,
            columns,
            jax.ShapeDtypeStruct((2, n_gx, per, 64, 128), BF16),
        ),
        in_specs=[pl.BlockSpec(memory_space=pltpu.HBM)] * 10,
        out_specs=(whole,) * 3,
        scratch_shapes=scratch,
        compiler_params=params,
        name="residual_block",
    )(
        in_hbm(features),
        in_hbm(cotangent),
        in_hbm(weight_one.reshape(27 * C, C)),
        in_hbm(weight_two.reshape(27 * C, C)),
        in_hbm(low),
        in_hbm(high),
        in_hbm(scale_one.reshape(1, C)),
        in_hbm(shift_one.reshape(1, C)),
        in_hbm(scale_two.reshape(1, C)),
        in_hbm(shift_two.reshape(1, C)),
    )
    sums = jax.ShapeDtypeStruct((27 * C, C), F32)
    out, gfeat, gw_one, gw_two = pl.pallas_call(
        functools.partial(result_kernel, 1.0 / (n_gx * n_gy * SHARE), per),
        out_shape=(columns, columns, sums, sums),
        in_specs=[left, left, whole],
        out_specs=(left,) * 4,
        scratch_shapes=[vm((27 * C, C), F32), vm((27 * C, C), F32), dma((4,))],
        compiler_params=pltpu.CompilerParams(vmem_limit_bytes=8 * 2**20),
        name="results",
    )(out, gfeat, full)
    return out, gfeat, gw_one.reshape(27, C, C), gw_two.reshape(27, C, C)


def solution(mesh):
    columns = P("gx", "gy", None)
    placed = (columns, columns, P("gx", "gy"), P("gx", "gy")) + (P(),) * 6
    return jax.shard_map(
        functools.partial(run, mesh.shape["gx"], mesh.shape["gy"]),
        mesh=mesh,
        in_specs=placed,
        out_specs=(columns, columns, P(), P()),
        check_vma=False,
    )
```

```python
import functools

import jax
import jax.numpy as jnp
from jax import lax
from jax.experimental import pallas as pl
from jax.experimental.pallas import tpu as pltpu
from jax.sharding import PartitionSpec as P

MESH = pl.DeviceIdType.MESH
F32 = jnp.float32
BF16 = jnp.bfloat16
BRICK = 8
C = 64
WIDTH = 512
SLOTS = 4
SHARE = 2
BX, BY = 2, 8
W = 12
ROWS = SLOTS * W
CORE = SLOTS * BRICK
BLOCKS = 16
USED = 14
HALOS = [(dx, dy) for dx in (-1, 0, 1) for dy in (-1, 0, 1) if dx or dy]


def lane(shape):
    return lax.broadcasted_iota(jnp.int32, shape, len(shape) - 1)


def turned(value):
    return pltpu.roll(value, 64, value.ndim - 1)


def height_mask(bounds):
    first = lane(bounds.shape) < 64
    other = turned(bounds)
    low, high = jnp.where(first, bounds, other), jnp.where(first, other, bounds)
    step = jnp.where(first, 0.0, 1.0)
    return [(step + 2.0 * c >= low) & (step + 2.0 * c < high) for c in range(4)]


def toeplitz(one, two, pair_ref, t):
    first = lane(one.shape) < 64
    zero = jnp.zeros(one.shape, BF16)
    start = jnp.where(first, turned(one), 0.0).astype(BF16)
    end = jnp.where(first, 0.0, turned(two)).astype(BF16)
    one, two = one.astype(BF16), two.astype(BF16)
    rows = pl.ds(pl.multiple_of(t * 512, 512), 512)
    columns = (
        [zero, start, one, two, end, zero, zero, zero],
        [zero, zero, zero, start, one, two, end, zero],
    )
    for c in range(2):
        pair_ref[rows, 128 * c : 128 * c + 128] = jnp.concatenate(columns[c], axis=0)


def build_weights(w_ref, forward_ref, adjoint_ref):
    def tap(t, carry):
        rows = w_ref[pl.ds(pl.multiple_of(t * 192, 192), 192), :].astype(F32)
        lower, middle, upper = rows[:64], rows[64:128], rows[128:]
        toeplitz(
            jnp.concatenate([middle, lower], axis=1),
            jnp.concatenate([upper, middle], axis=1),
            forward_ref,
            t,
        )
        toeplitz(rows[64:192].T, rows[0:128].T, adjoint_ref, 8 - t)
        return carry

    lax.fori_loop(0, 9, tap, 0, unroll=3)


def conv(source, band_ref, g, spans, pitch):
    lanes = slice(128 * g, 128 * g + 384)
    parts = [
        jnp.concatenate(
            [
                source[oy, start + ox * pitch : start + ox * pitch + count, lanes]
                for ox in range(3)
                for oy in range(3)
            ],
            axis=1,
        )
        for start, count in spans
    ]
    rows = parts[0] if len(parts) == 1 else jnp.concatenate(parts, axis=0)
    skip = 128 * (1 - g)
    band = jnp.concatenate(
        [band_ref[512 * t + skip : 512 * t + skip + 384, :] for t in range(9)], axis=0
    )
    return jnp.dot(rows, band, preferred_element_type=F32)


def shifted(value):
    count = value.shape[0]
    return (pltpu.roll(value, 1, 0), value, pltpu.roll(value, count - 1, 0))


def fold(results, fold_ref, block_ref, k, t0):
    for oy in range(3):
        sums = {}
        for g in range(2):
            for z in range(4 * g, 4 * g + 4):
                for c in range(3):
                    kind = (z % 2, 2 * g + 2 * c - z)
                    if kind in ((0, 0), (0, -2), (1, -1), (1, 1)):
                        zo = z - 4 * g
                        block = results[g][
                            64 * zo : 64 * zo + 64,
                            384 * oy + 128 * c : 384 * oy + 128 * c + 128,
                        ]
                        sums[kind] = sums[kind] + block if kind in sums else block
        p, u, q, s = sums[0, 0], sums[0, -2], sums[1, -1], sums[1, 1]
        first = lane(p.shape) < 64
        block_ref[k, t0 + oy] = (q + turned(jnp.where(first, p, u))).astype(BF16)
        fold_ref[t0 + oy] = p + turned(s)


def weight_sums(errors_t, source, count, pitch, fold_ref, block_ref, k, send):
    for ox in range(3):
        base = ox * pitch
        results = []
        for g in range(2):
            lanes = slice(128 * g, 128 * g + 384)
            window = jnp.concatenate(
                [source[oy, pl.ds(base, count), lanes] for oy in range(3)], axis=1
            )
            results.append(
                jnp.dot(errors_t[g], window, preferred_element_type=F32)
            )
        fold(results, fold_ref, block_ref, k, 3 * ox)
        if send:
            for oy in range(3):
                send(k, 3 * ox + oy)
    first = lane((64, 128)) < 64
    for i in range(5):
        even = turned(fold_ref[2 * i])
        odd = fold_ref[2 * i + 1] if i < 4 else jnp.zeros_like(even)
        block_ref[k, 9 + i] = jnp.where(first, even, odd).astype(BF16)
        if send:
            send(k, 9 + i)


def unfold(blocks_ref, per, k, out_ref, factor):
    for t in range(9):
        block = blocks_ref[k, t // per, t % per].astype(F32) * factor
        out_ref[192 * t : 192 * t + 128, :] = block.T
    for i in range(5):
        block = (blocks_ref[k, (9 + i) // per, (9 + i) % per].astype(F32) * factor).T
        out_ref[384 * i + 128 : 384 * i + 192, :] = block[:64]
        if i < 4:
            out_ref[384 * i + 320 : 384 * i + 384, :] = block[64:]


def block_kernel(
    n_gx,
    n_gy,
    feat,
    cot_in,
    w_one_in,
    w_two_in,
    low_in,
    high_in,
    scale_one_in,
    shift_one_in,
    scale_two_in,
    shift_two_in,
    out,
    gfeat,
    full,
    cot,
    w_one,
    w_two,
    low,
    high,
    scales,
    bounds,
    ext,
    elh,
    pick_in,
    pick_bounds,
    pick_target,
    put_out,
    put_grad,
    src_one,
    src_two,
    err_two,
    err_one,
    msk,
    core_in,
    core_mask,
    target,
    slope,
    frame,
    res,
    grad_region,
    gsum,
    fwd_one,
    adj_one,
    fwd_two,
    adj_two,
    folded,
    blocks,
    got_x,
    half,
    got_y,
    out_x,
    in_x,
    edge_rows,
    out_y,
    in_y,
    out_c,
    in_c,
    local_sem,
    halo_send,
    halo_recv,
    edge_send,
    edge_recv,
    sum_send,
    sum_recv,
):
    comm = n_gx * n_gy > 1
    if comm:
        gx, gy = lax.axis_index("gx"), lax.axis_index("gy")
    else:
        gx, gy = 0, 0
    nx, ny = feat.shape[0], feat.shape[1]
    per = BLOCKS // n_gx

    inputs = [
        pltpu.make_async_copy(src, dst, local_sem.at[2 + k])
        for k, (src, dst) in enumerate(
            ((w_one_in, w_one), (w_two_in, w_two), (cot_in, cot))
        )
    ]

    def device(dx, dy):
        return (lax.rem(gx + dx + n_gx, n_gx), lax.rem(gy + dy + n_gy, n_gy))

    if comm:
        for ref in (ext, elh):
            strip = jnp.zeros((nx + 4, 16, ref.shape[2]), BF16)
            ref[:, 0:16, :] = strip
            ref[:, ny + 16 : ny + 32, :] = strip
        barrier = pltpu.get_barrier_semaphore()
        peers = [(d, 0) for d in range(1, n_gx)] + [(0, d) for d in range(1, n_gy)]
        peers += [(dx, dy) for dx, dy in HALOS if dx and dy]
        for dx, dy in peers:
            pl.semaphore_signal(
                barrier, inc=1, device_id=device(dx, dy), device_id_type=MESH
            )

    own = pltpu.make_async_copy(
        feat, ext.at[2 : nx + 2, 16 : ny + 16], local_sem.at[0]
    )
    own.start()
    small = [
        pltpu.make_async_copy(src, dst, local_sem.at[5 + k])
        for k, (src, dst) in enumerate(
            (
                (low_in, low),
                (high_in, high),
                (scale_one_in, scales.at[0]),
                (shift_one_in, scales.at[1]),
                (scale_two_in, scales.at[2]),
                (shift_two_in, scales.at[3]),
            )
        )
    ]
    for copy in small + inputs:
        copy.start()
    for copy in small:
        copy.wait()

    first = lane((ny, 128)) < 64
    square = jnp.zeros((ny, ny), F32)
    lows = jnp.concatenate([low[...].astype(F32), square[nx:]], axis=0).T
    highs = jnp.concatenate([high[...].astype(F32), square[nx:]], axis=0).T
    for x in range(nx):
        both = jnp.where(first, lows[:, x : x + 1], highs[:, x : x + 1]).astype(BF16)
        bounds[x] = both
        elh[x + 2, 16 : ny + 16, :] = both
    def all_wait(like, sem):
        pltpu.make_async_copy(like, like, sem).wait()

    def remote(src, dst, send, recv, to):
        return pltpu.make_async_remote_copy(
            src_ref=src,
            dst_ref=dst,
            send_sem=send,
            recv_sem=recv,
            device_id=to,
            device_id_type=MESH,
        )


    if comm:
        pl.semaphore_wait(barrier, len(peers))
    if comm:
        x_from = {-1: slice(0, 2), 0: slice(0, nx), 1: slice(nx - 2, nx)}
        x_to = {-1: slice(nx + 2, nx + 4), 0: slice(2, nx + 2), 1: slice(0, 2)}
        y_from = {-1: slice(0, 2), 0: slice(0, ny), 1: slice(ny - 2, ny)}
        y_to = {
            -1: slice(ny + 16, ny + 18),
            0: slice(16, ny + 16),
            1: slice(14, 16),
        }
        order = sorted(HALOS, key=lambda h: -(2 * abs(h[0]) - abs(h[1])))
        for dx, dy in order:
            for k, (src, dst) in enumerate(((feat, ext), (bounds, elh))):
                copy = remote(
                    src.at[x_from[dx], y_from[dy]],
                    dst.at[x_to[dx], y_to[dy]],
                    halo_send.at[k],
                    halo_recv.at[k],
                    device(dx, dy),
                )
                copy.start()
    inputs[0].wait()
    build_weights(w_one, fwd_one, adj_one)
    inputs[1].wait()
    build_weights(w_two, fwd_two, adj_two)
    nothing = jnp.zeros((3, 2 * ROWS, WIDTH), BF16)
    err_two[:, 0 : 2 * ROWS, :] = nothing
    err_two[:, 10 * ROWS : 12 * ROWS, :] = nothing
    err_one[:, 0 : 2 * ROWS, :] = nothing
    err_one[:, 12 * ROWS : 14 * ROWS, :] = nothing
    frame[...] = jnp.zeros_like(frame)

    occupied = jnp.where(high[...] > low[...], 1, 0)
    by_lane = lane((8, ny))
    count = jnp.int32(0)
    brick = [jnp.int32(-1000)] * SLOTS
    for bx in range(BX):
        rows = occupied[8 * bx : 8 * bx + 8]
        for by in range(BY):
            inside = (by_lane >= 8 * by) & (by_lane < 8 * by + 8)
            filled = jnp.max(jnp.where(inside, rows, 0))
            for j in range(SLOTS):
                hit = (filled > 0) & (count == j)
                brick[j] = jnp.where(hit, 8 * bx + by, brick[j])
            count = count + filled

    def picks(rows, columns, row_dim, per_brick, pitch, offset):
        shape = (rows, columns) if row_dim == 0 else (columns, rows)
        row = lax.broadcasted_iota(jnp.int32, shape, row_dim)
        column = lax.broadcasted_iota(jnp.int32, shape, 1 - row_dim)
        wanted = row + offset
        for j in range(SLOTS):
            b = brick[j]
            bx = jnp.where(b >= BY, 1, 0)
            spot = jnp.where(b < 0, -4000, bx * pitch + 8 * (b - BY * bx)) - per_brick * j
            inside = (row >= per_brick * j) & (row < per_brick * j + per_brick)
            wanted = wanted + jnp.where(inside, spot, 0)
        return jnp.where(column == wanted, 1.0, 0.0).astype(BF16)

    tall = ny + 32
    core_pick = picks(CORE, 2 * tall, 0, BRICK, tall, 16)
    frame_pick = [picks(ROWS, 2 * tall, 0, W, tall, 13 + oy) for oy in range(3)]
    pick_in[...] = jnp.concatenate(frame_pick + [core_pick], axis=0)
    pick_bounds[...] = jnp.concatenate([frame_pick[1], core_pick], axis=0)
    pick_target[...] = picks(CORE, 2 * ny, 0, BRICK, ny, 0)
    put_out[...] = picks(CORE, 2 * ny, 1, BRICK, ny, 0)
    put_grad[...] = picks(ROWS, 2 * (ny + 16), 1, W, ny + 16, 6)

    inputs[2].wait()
    def cut_target(x, carry):
        rows = jnp.concatenate([cot[x], cot[8 + x]], axis=0)
        spot = pl.ds(pl.multiple_of(x * CORE, CORE), CORE)
        target[spot, :] = jnp.dot(pick_target[...], rows, preferred_element_type=F32)
        return carry

    lax.fori_loop(0, 8, cut_target, 0, unroll=8)

    def mask_in(xs, ys):
        mask = height_mask(elh[xs, ys, :].astype(F32))
        for c in range(4):
            lanes = slice(128 * c, 128 * c + 128)
            value = ext[xs, ys, lanes].astype(F32)
            ext[xs, ys, lanes] = jnp.where(mask[c], value, 0.0).astype(BF16)

    def mask_inner(i, carry):
        mask_in(pl.ds(2 + 2 * i, 2), slice(16, ny + 16))
        return carry

    own.wait()
    lax.fori_loop(0, nx // 2, mask_inner, 0, unroll=2)
    if comm:
        margin = (nx + 4) * (ny + 4) - nx * ny
        for k, ref in enumerate((ext, elh)):
            all_wait(ref.at[0 : margin // 48, 0:48], halo_recv.at[k])
    if comm:
        for spot, inside in (
            ((slice(0, 2), slice(None)), gx > 0),
            ((slice(nx + 2, nx + 4), slice(None)), gx < n_gx - 1),
            ((slice(None), slice(0, 16)), gy > 0),
            ((slice(None), slice(ny + 16, ny + 32)), gy < n_gy - 1),
        ):
            value = elh[spot[0], spot[1], :].astype(F32)
            elh[spot[0], spot[1], :] = (
                value * jnp.where(inside, 1.0, 0.0).astype(F32)
            ).astype(BF16)
    else:
        for spot in (slice(0, 2), slice(nx + 2, nx + 4)):
            elh[spot] = jnp.zeros_like(elh[spot])
            ext[spot] = jnp.zeros_like(ext[spot])
        for spot in (slice(0, 16), slice(ny + 16, ny + 32)):
            elh[:, spot] = jnp.zeros_like(elh[:, spot])
            ext[:, spot] = jnp.zeros_like(ext[:, spot])

    for x in range(2, nx + 2, 4):
        mask_in(slice(x, x + 4), slice(0, 16))
        mask_in(slice(x, x + 4), slice(ny + 16, tall))
    for x in (0, 1, nx + 2, nx + 3):
        mask_in(slice(x, x + 1), slice(0, tall))

    def cut(x, carry):
        base = pl.multiple_of(x * ROWS, ROWS)
        core = pl.multiple_of(x * CORE, CORE)
        rows = jnp.concatenate([ext[x], ext[8 + x]], axis=0)
        value = jnp.dot(pick_in[...], rows, preferred_element_type=F32)
        for oy in range(3):
            src_one[oy, pl.ds(base, ROWS), :] = value[
                ROWS * oy : ROWS * oy + ROWS
            ].astype(BF16)
        core_in[pl.ds(core, CORE), :] = value[3 * ROWS :]
        rows = jnp.concatenate([elh[x], elh[8 + x]], axis=0)
        mask = height_mask(
            jnp.dot(pick_bounds[...], rows, preferred_element_type=F32)
        )
        for c in range(4):
            lanes = slice(128 * c, 128 * c + 128)
            value = jnp.where(mask[c], 1.0, 0.0)
            msk[pl.ds(base, ROWS), lanes] = value[:ROWS]
            core_mask[pl.ds(core, CORE), lanes] = value[ROWS:]
        return carry

    lax.fori_loop(0, W, cut, 0, unroll=12)

    scale_one, shift_one, scale_two, shift_two = (
        jnp.concatenate([scales[k]] * 4, axis=1) for k in range(4)
    )

    for g in range(2):
        lanes = slice(256 * g, 256 * g + 256)
        pre = conv(src_one, fwd_one, g, [(0, 10 * ROWS)], ROWS) * scale_one + shift_one
        s = jax.nn.sigmoid(pre)
        mask = msk[ROWS : 11 * ROWS, lanes]
        hidden = pre * s * mask
        slope[:, lanes] = s * (1.0 + pre * (1.0 - s)) * mask * scale_one
        for x in range(10):
            rows = hidden[ROWS * x : ROWS * x + ROWS]
            for oy in range(3):
                for j in range(0, SLOTS, 2):
                    both = [
                        rows[W * i + 1 + oy : W * i + 9 + oy] for i in (j, j + 1)
                    ]
                    src_two[oy, CORE * x + 8 * j : CORE * x + 8 * j + 16, lanes] = (
                        jnp.concatenate(both, axis=0).astype(BF16)
                    )

    middle = slice(2 * CORE, 10 * CORE)
    errors_t = []
    for g in range(2):
        lanes = slice(256 * g, 256 * g + 256)
        pre = conv(src_two, fwd_two, g, [(0, 8 * CORE)], CORE) * scale_two + shift_two
        pre = pre + core_in[middle, lanes]
        s = jax.nn.sigmoid(pre)
        mask = core_mask[middle, lanes]
        result = pre * s * mask
        grad = target[:, lanes] * mask * (s * (1.0 + pre * (1.0 - s)))
        errors_t.append((grad * scale_two).T.astype(BF16))
        res[:, lanes] = result.astype(BF16)
        for x in range(8):
            for j in range(SLOTS):
                spot = CORE * x + 8 * j
                frame[x, W * j + 2 : W * j + 10, lanes] = grad[spot : spot + 8]

    def spread(x, carry):
        base = pl.multiple_of((x + 2) * ROWS, ROWS)
        for g in range(2):
            lanes = slice(256 * g, 256 * g + 256)
            for oy, moved in enumerate(shifted(frame[x, :, lanes] * scale_two)):
                err_two[oy, pl.ds(base, ROWS), lanes] = moved.astype(BF16)
        return carry

    lax.fori_loop(0, 8, spread, 0, unroll=2)

    def send_block(k, b):
        if not comm:
            got_x[k, 0, b] = blocks[k, b]
            return

        @pl.when(gx != b)
        def _():
            remote(
                blocks.at[k, b],
                got_x.at[k, gx, 0],
                sum_send.at[k, 0],
                sum_recv.at[k, 0],
                (b, gy),
            ).start()

        @pl.when(gx == b)
        def _():
            got_x[k, gx, 0] = blocks[k, b]

    def owners(act):
        if comm:
            pl.when(gx < USED)(act)
        else:
            act()

    def reduce_x(k):
        def act():
            if comm:
                all_wait(got_x.at[k, 0 : n_gx - 1], sum_recv.at[k, 0])
            total = got_x[k, 0].astype(F32)
            for s in range(1, n_gx):
                total = total + got_x[k, s].astype(F32)
            half[0, k] = total.astype(BF16)
            for d in range(1, n_gy):
                remote(
                    half.at[0, k],
                    got_y.at[k, gy],
                    sum_send.at[k, 1],
                    sum_recv.at[k, 1],
                    (gx, lax.rem(gy + d, n_gy)),
                ).start()
            got_y[k, gy] = half[0, k]

        owners(act)

    def reduce_y(k):
        def act():
            if comm:
                all_wait(got_y.at[k, 0 : n_gy - 1], sum_recv.at[k, 1])
            total = got_y[k, 0].astype(F32)
            for s in range(1, n_gy):
                total = total + got_y[k, s].astype(F32)
            half[1, k] = total.astype(BF16)
            for d in range(1, n_gx):
                remote(
                    half.at[1, k],
                    full.at[k, gx],
                    sum_send.at[k, 2],
                    sum_recv.at[k, 2],
                    (lax.rem(gx + d, n_gx), gy),
                ).start()
            full[k, gx] = half[1, k]

        owners(act)

    weight_sums(
        errors_t, src_two, 8 * CORE, CORE, folded, blocks, 1, send_block
    )

    errors_t = []
    for g in range(2):
        lanes = slice(256 * g, 256 * g + 256)
        back = conv(err_two, adj_two, g, [(0, 10 * ROWS)], ROWS)
        error = back * slope[:, lanes]
        errors_t.append(error.T.astype(BF16))
        for x in range(10):
            rows = error[ROWS * x : ROWS * x + ROWS]
            spot = slice(ROWS * (x + 2), ROWS * (x + 3))
            for oy, moved in enumerate(shifted(rows)):
                err_one[oy, spot, lanes] = moved.astype(BF16)
    weight_sums(
        errors_t, src_one, 10 * ROWS, ROWS, folded, blocks, 0, send_block
    )
    reduce_x(1)

    def adjoint_one(g, columns):
        lanes = slice(256 * g, 256 * g + 256)
        spans = [(ROWS * x, ROWS * n) for x, n in columns]
        back = conv(err_one, adj_one, g, spans, ROWS)
        done = 0
        for start, n in columns:
            for x in range(start, start + n):
                rows = back[ROWS * done : ROWS * done + ROWS]
                if 2 <= x < 10:
                    rows = rows + frame[x - 2, :, lanes]
                grad_region[x, :, lanes] = rows.astype(BF16)
                done += 1

    def collect(x):
        total = None
        for bx in range(BX):
            if 0 <= x - 8 * bx < W:
                part = jnp.dot(
                    put_grad[bx * (ny + 16) : (bx + 1) * (ny + 16), :],
                    grad_region[x - 8 * bx],
                    preferred_element_type=F32,
                )
                total = part if total is None else total + part
        return total

    for g in range(2):
        adjoint_one(g, [(0, 2), (10, 2)])
    edges = []

    def send_edges(kinds):
        for i, (dx, dy) in enumerate(HALOS):
            if (dx, dy) not in kinds:
                continue
            a, b = (dx + 1) // 2, (dy + 1) // 2
            if dy == 0:
                src, dst = out_x.at[a], in_x.at[1 - a]
            elif dx == 0:
                src, dst = out_y.at[b], in_y.at[1 - b]
            else:
                src, dst = out_c.at[a, b], in_c.at[1 - a, 1 - b]
            copy = remote(
                src, dst, edge_send.at[i], edge_recv.at[i], device(dx, dy)
            )
            copy.start()
            edges.append(copy)

    if comm:
        for a, x in enumerate((0, nx + 2)):
            pair = [collect(x + k) for k in range(2)]
            for k in range(2):
                out_x[a, k] = pair[k][8 : ny + 8].astype(BF16)
            for b, t in enumerate((0, ny + 8)):
                both = [value[t : t + 8] for value in pair]
                out_c[a, b] = jnp.concatenate(both, axis=0).astype(BF16)
        send_edges([h for h in HALOS if h[0]])

    adjoint_one(0, [(2, 8)])
    reduce_x(0)
    adjoint_one(1, [(2, 8)])

    reduce_y(1)

    for x in range(2, nx + 2):
        value = collect(x)
        gsum[x] = value
        if comm:
            rows = slice(2 * (x - 2), 2 * (x - 2) + 2)
            edge_rows[0, rows, :] = value[6:8]
            edge_rows[1, rows, :] = value[ny + 8 : ny + 10]
    if comm:
        out_y[...] = edge_rows[...].astype(BF16)
        send_edges([h for h in HALOS if not h[0]])
    reduce_y(0)

    def deposit(x, carry):
        rows = res[pl.ds(pl.multiple_of(x * CORE, CORE), CORE), :]
        value = jnp.dot(put_out[...], rows, preferred_element_type=F32).astype(BF16)
        out[x] = value[:ny]
        out[8 + x] = value[ny:]
        return carry

    lax.fori_loop(0, 8, deposit, 0, unroll=4)

    if comm:
        for copy in edges:
            copy.wait_recv()
        x_in = [
            jnp.where(inside, 1.0, 0.0).astype(F32)
            for inside in (gx > 0, gx < n_gx - 1)
        ]
        y_in = [
            jnp.where(inside, 1.0, 0.0).astype(F32)
            for inside in (gy > 0, gy < n_gy - 1)
        ]
        for a, x in enumerate((2, nx)):
            gsum[x : x + 2, 8 : ny + 8, :] += in_x[a].astype(F32) * x_in[a]
            for b, t in enumerate((8, ny)):
                rows = in_c[a, b].astype(F32) * (x_in[a] * y_in[b])
                for k in range(2):
                    gsum[x + k, t : t + 8, :] += rows[8 * k : 8 * k + 8]
        for b, t in enumerate((8, ny + 6)):
            rows = in_y[b].astype(F32) * y_in[b]
            for i in range(nx):
                gsum[2 + i, t : t + 2, :] += rows[2 * i : 2 * i + 2]

    def finish(x, carry):
        mask = height_mask(elh[x + 2, 16 : ny + 16, :].astype(F32))
        for c in range(4):
            lanes = slice(128 * c, 128 * c + 128)
            value = gsum[x + 2, 8 : ny + 8, lanes]
            gfeat[x, :, lanes] = jnp.where(mask[c], value, 0.0).astype(BF16)
        return carry

    lax.fori_loop(0, nx, finish, 0, unroll=4)

    if comm:
        for copy in edges:
            copy.wait_send()
        for k, ref in enumerate((ext, elh)):
            all_wait(ref.at[0 : margin // 48, 0:48], halo_send.at[k])

        @pl.when(gx < USED)
        def _():
            for k in range(2):
                all_wait(full.at[k, 0 : USED - 1], sum_recv.at[k, 2])
                all_wait(blocks.at[k, 0 : USED - 1], sum_send.at[k, 0])
                all_wait(got_y.at[k, 0 : n_gy - 1], sum_send.at[k, 1])
                all_wait(full.at[k, 0 : n_gx - 1], sum_send.at[k, 2])

        @pl.when(gx >= USED)
        def _():
            for k in range(2):
                all_wait(full.at[k, 0:USED], sum_recv.at[k, 2])
                all_wait(blocks.at[k, 0:USED], sum_send.at[k, 0])


def result_kernel(
    factor, per, out_in, gfeat_in, full, out, gfeat, gw_one, gw_two, one, two, sem
):
    copies = [
        pltpu.make_async_copy(out_in, out, sem.at[0]),
        pltpu.make_async_copy(gfeat_in, gfeat, sem.at[1]),
    ]
    for copy in copies:
        copy.start()
    for k, (ref, gw) in enumerate(((one, gw_one), (two, gw_two))):
        unfold(full, per, k, ref, factor)
        copy = pltpu.make_async_copy(ref, gw, sem.at[2 + k])
        copy.start()
        copies.append(copy)
    for copy in copies:
        copy.wait()


def run(
    n_gx,
    n_gy,
    features,
    cotangent,
    low,
    high,
    weight_one,
    weight_two,
    scale_one,
    shift_one,
    scale_two,
    shift_two,
):
    nx, ny = features.shape[0], features.shape[1]
    per = BLOCKS // n_gx
    whole = pl.BlockSpec(memory_space=pltpu.VMEM)
    left = pl.BlockSpec(memory_space=pl.ANY)
    vm = pltpu.VMEM
    dma = pltpu.SemaphoreType.DMA
    scratch = [
        vm((nx, ny, WIDTH), BF16),
        vm((27 * C, C), BF16),
        vm((27 * C, C), BF16),
        vm((nx, ny), jnp.int32),
        vm((nx, ny), jnp.int32),
        vm((4, 1, C), F32),
        vm((nx, ny, 128), BF16),
        vm((nx + 4, ny + 32, WIDTH), BF16),
        vm((nx + 4, ny + 32, 128), BF16),
        vm((3 * ROWS + CORE, 2 * ny + 64), BF16),
        vm((ROWS + CORE, 2 * ny + 64), BF16),
        vm((CORE, 2 * ny), BF16),
        vm((2 * ny, CORE), BF16),
        vm((2 * ny + 32, ROWS), BF16),
        vm((3, W * ROWS, WIDTH), BF16),
        vm((3, 10 * CORE, WIDTH), BF16),
        vm((3, W * ROWS, WIDTH), BF16),
        vm((3, (W + 2) * ROWS, WIDTH), BF16),
        vm((W * ROWS, WIDTH), F32),
        vm((W * CORE, WIDTH), F32),
        vm((W * CORE, WIDTH), F32),
        vm((8 * CORE, WIDTH), F32),
        vm((10 * ROWS, WIDTH), F32),
        vm((8, ROWS, WIDTH), F32),
        vm((8 * CORE, WIDTH), BF16),
        vm((W, ROWS, WIDTH), BF16),
        vm((nx + 4, ny + 16, WIDTH), F32),
        vm((9 * 512, 256), BF16),
        vm((9 * 512, 256), BF16),
        vm((9 * 512, 256), BF16),
        vm((9 * 512, 256), BF16),
        vm((9, 64, 128), F32),
        vm((2, BLOCKS, 64, 128), BF16),
        vm((2, n_gx, per, 64, 128), BF16),
        vm((2, 2, per, 64, 128), BF16),
        vm((2, n_gy, per, 64, 128), BF16),
        vm((2, 2, ny, WIDTH), BF16),
        vm((2, 2, ny, WIDTH), BF16),
        vm((2, 2 * nx, WIDTH), F32),
        vm((2, 2 * nx, WIDTH), BF16),
        vm((2, 2 * nx, WIDTH), BF16),
        vm((2, 2, 16, WIDTH), BF16),
        vm((2, 2, 16, WIDTH), BF16),
        dma((11,)),
        dma((2,)),
        dma((2,)),
        dma((8,)),
        dma((8,)),
        dma((2, 3)),
        dma((2, 3)),
    ]
    comm = n_gx * n_gy > 1
    params = pltpu.CompilerParams(
        collective_id=0 if comm else None,
        has_side_effects=comm,
        vmem_limit_bytes=46 * 2**20,
    )
    in_hbm = functools.partial(
        pltpu.with_memory_space_constraint, memory_space=pltpu.HBM
    )
    columns = jax.ShapeDtypeStruct(features.shape, BF16)
    out, gfeat, full = pl.pallas_call(
        functools.partial(block_kernel, n_gx, n_gy),
        out_shape=(
            columns,
            columns,
            jax.ShapeDtypeStruct((2, n_gx, per, 64, 128), BF16),
        ),
        in_specs=[pl.BlockSpec(memory_space=pltpu.HBM)] * 10,
        out_specs=(whole,) * 3,
        scratch_shapes=scratch,
        compiler_params=params,
        name="residual_block",
    )(
        in_hbm(features),
        in_hbm(cotangent),
        in_hbm(weight_one.reshape(27 * C, C)),
        in_hbm(weight_two.reshape(27 * C, C)),
        in_hbm(low),
        in_hbm(high),
        in_hbm(scale_one.reshape(1, C)),
        in_hbm(shift_one.reshape(1, C)),
        in_hbm(scale_two.reshape(1, C)),
        in_hbm(shift_two.reshape(1, C)),
    )
    sums = jax.ShapeDtypeStruct((27 * C, C), F32)
    out, gfeat, gw_one, gw_two = pl.pallas_call(
        functools.partial(result_kernel, 1.0 / (n_gx * n_gy * SHARE), per),
        out_shape=(columns, columns, sums, sums),
        in_specs=[left, left, whole],
        out_specs=(left,) * 4,
        scratch_shapes=[vm((27 * C, C), F32), vm((27 * C, C), F32), dma((4,))],
        compiler_params=pltpu.CompilerParams(vmem_limit_bytes=8 * 2**20),
        name="results",
    )(out, gfeat, full)
    return out, gfeat, gw_one.reshape(27, C, C), gw_two.reshape(27, C, C)


def solution(mesh):
    columns = P("gx", "gy", None)
    placed = (columns, columns, P("gx", "gy"), P("gx", "gy")) + (P(),) * 6
    return jax.shard_map(
        functools.partial(run, mesh.shape["gx"], mesh.shape["gy"]),
        mesh=mesh,
        in_specs=placed,
        out_specs=(columns, columns, P(), P()),
        check_vma=False,
    )
```

```python
import functools

import jax
import jax.numpy as jnp
from jax import lax
from jax.experimental import pallas as pl
from jax.experimental.pallas import tpu as pltpu
from jax.sharding import PartitionSpec as P

MESH = pl.DeviceIdType.MESH
F32 = jnp.float32
BF16 = jnp.bfloat16
BRICK = 8
C = 64
WIDTH = 512
SLOTS = 4
SHARE = 2
BX, BY = 2, 8
W = 12
ROWS = SLOTS * W
CORE = SLOTS * BRICK
BLOCKS = 16
USED = 14
HALOS = [(dx, dy) for dx in (-1, 0, 1) for dy in (-1, 0, 1) if dx or dy]


def lane(shape):
    return lax.broadcasted_iota(jnp.int32, shape, len(shape) - 1)


def turned(value):
    return pltpu.roll(value, 64, value.ndim - 1)


def height_mask(bounds):
    first = lane(bounds.shape) < 64
    other = turned(bounds)
    low, high = jnp.where(first, bounds, other), jnp.where(first, other, bounds)
    step = jnp.where(first, 0.0, 1.0)
    return [(step + 2.0 * c >= low) & (step + 2.0 * c < high) for c in range(4)]


def toeplitz(one, two, pair_ref, t):
    first = lane(one.shape) < 64
    zero = jnp.zeros(one.shape, BF16)
    start = jnp.where(first, turned(one), 0.0).astype(BF16)
    end = jnp.where(first, 0.0, turned(two)).astype(BF16)
    one, two = one.astype(BF16), two.astype(BF16)
    rows = pl.ds(pl.multiple_of(t * 512, 512), 512)
    columns = (
        [zero, start, one, two, end, zero, zero, zero],
        [zero, zero, zero, start, one, two, end, zero],
    )
    for c in range(2):
        pair_ref[rows, 128 * c : 128 * c + 128] = jnp.concatenate(columns[c], axis=0)


def build_weights(w_ref, forward_ref, adjoint_ref):
    def tap(t, carry):
        rows = w_ref[pl.ds(pl.multiple_of(t * 192, 192), 192), :].astype(F32)
        lower, middle, upper = rows[:64], rows[64:128], rows[128:]
        toeplitz(
            jnp.concatenate([middle, lower], axis=1),
            jnp.concatenate([upper, middle], axis=1),
            forward_ref,
            t,
        )
        toeplitz(rows[64:192].T, rows[0:128].T, adjoint_ref, 8 - t)
        return carry

    lax.fori_loop(0, 9, tap, 0, unroll=3)


def conv(source, band_ref, g, spans, pitch):
    lanes = slice(128 * g, 128 * g + 384)
    parts = [
        jnp.concatenate(
            [
                source[oy, start + ox * pitch : start + ox * pitch + count, lanes]
                for ox in range(3)
                for oy in range(3)
            ],
            axis=1,
        )
        for start, count in spans
    ]
    rows = parts[0] if len(parts) == 1 else jnp.concatenate(parts, axis=0)
    skip = 128 * (1 - g)
    band = jnp.concatenate(
        [band_ref[512 * t + skip : 512 * t + skip + 384, :] for t in range(9)], axis=0
    )
    return jnp.dot(rows, band, preferred_element_type=F32)


def shifted(value):
    count = value.shape[0]
    return (pltpu.roll(value, 1, 0), value, pltpu.roll(value, count - 1, 0))


def fold(results, fold_ref, block_ref, k, t0):
    for oy in range(3):
        sums = {}
        for g in range(2):
            for z in range(4 * g, 4 * g + 4):
                for c in range(3):
                    kind = (z % 2, 2 * g + 2 * c - z)
                    if kind in ((0, 0), (0, -2), (1, -1), (1, 1)):
                        zo = z - 4 * g
                        block = results[g][
                            64 * zo : 64 * zo + 64,
                            384 * oy + 128 * c : 384 * oy + 128 * c + 128,
                        ]
                        sums[kind] = sums[kind] + block if kind in sums else block
        p, u, q, s = sums[0, 0], sums[0, -2], sums[1, -1], sums[1, 1]
        first = lane(p.shape) < 64
        block_ref[k, t0 + oy] = (q + turned(jnp.where(first, p, u))).astype(BF16)
        fold_ref[t0 + oy] = p + turned(s)


def weight_sums(errors_t, source, count, pitch, fold_ref, block_ref, k, send):
    for ox in range(3):
        base = ox * pitch
        results = []
        for g in range(2):
            lanes = slice(128 * g, 128 * g + 384)
            window = jnp.concatenate(
                [source[oy, pl.ds(base, count), lanes] for oy in range(3)], axis=1
            )
            results.append(
                jnp.dot(errors_t[g], window, preferred_element_type=F32)
            )
        fold(results, fold_ref, block_ref, k, 3 * ox)
        if send:
            for oy in range(3):
                send(k, 3 * ox + oy)
    first = lane((64, 128)) < 64
    for i in range(5):
        even = turned(fold_ref[2 * i])
        odd = fold_ref[2 * i + 1] if i < 4 else jnp.zeros_like(even)
        block_ref[k, 9 + i] = jnp.where(first, even, odd).astype(BF16)
        if send:
            send(k, 9 + i)


def unfold(blocks_ref, per, k, out_ref, factor):
    for t in range(9):
        block = blocks_ref[k, t // per, t % per].astype(F32) * factor
        out_ref[192 * t : 192 * t + 128, :] = block.T
    for i in range(5):
        block = (blocks_ref[k, (9 + i) // per, (9 + i) % per].astype(F32) * factor).T
        out_ref[384 * i + 128 : 384 * i + 192, :] = block[:64]
        if i < 4:
            out_ref[384 * i + 320 : 384 * i + 384, :] = block[64:]


def block_kernel(
    n_gx,
    n_gy,
    feat,
    cot_in,
    w_one_in,
    w_two_in,
    low_in,
    high_in,
    scale_one_in,
    shift_one_in,
    scale_two_in,
    shift_two_in,
    out,
    gfeat,
    full,
    cot,
    w_one,
    w_two,
    low,
    high,
    scales,
    bounds,
    ext,
    elh,
    pick_in,
    pick_bounds,
    pick_target,
    put_out,
    put_grad,
    src_one,
    src_two,
    err_two,
    err_one,
    msk,
    core_in,
    core_mask,
    target,
    slope,
    frame,
    res,
    grad_region,
    gsum,
    fwd_one,
    adj_one,
    fwd_two,
    adj_two,
    folded,
    blocks,
    got_x,
    half,
    got_y,
    out_x,
    in_x,
    edge_rows,
    out_y,
    in_y,
    out_c,
    in_c,
    local_sem,
    halo_send,
    halo_recv,
    edge_send,
    edge_recv,
    sum_send,
    sum_recv,
):
    comm = n_gx * n_gy > 1
    if comm:
        gx, gy = lax.axis_index("gx"), lax.axis_index("gy")
    else:
        gx, gy = 0, 0
    nx, ny = feat.shape[0], feat.shape[1]
    per = BLOCKS // n_gx

    inputs = [
        pltpu.make_async_copy(src, dst, local_sem.at[2 + k])
        for k, (src, dst) in enumerate(
            ((w_one_in, w_one), (w_two_in, w_two), (cot_in, cot))
        )
    ]

    def device(dx, dy):
        return (lax.rem(gx + dx + n_gx, n_gx), lax.rem(gy + dy + n_gy, n_gy))

    if comm:
        for ref in (ext, elh):
            strip = jnp.zeros((nx + 4, 16, ref.shape[2]), BF16)
            ref[:, 0:16, :] = strip
            ref[:, ny + 16 : ny + 32, :] = strip
        barrier = pltpu.get_barrier_semaphore()
        peers = [(d, 0) for d in range(1, n_gx)] + [(0, d) for d in range(1, n_gy)]
        peers += [(dx, dy) for dx, dy in HALOS if dx and dy]
        for dx, dy in peers:
            pl.semaphore_signal(
                barrier, inc=1, device_id=device(dx, dy), device_id_type=MESH
            )

    own = pltpu.make_async_copy(
        feat, ext.at[2 : nx + 2, 16 : ny + 16], local_sem.at[0]
    )
    own.start()
    small = [
        pltpu.make_async_copy(src, dst, local_sem.at[5 + k])
        for k, (src, dst) in enumerate(
            (
                (low_in, low),
                (high_in, high),
                (scale_one_in, scales.at[0]),
                (shift_one_in, scales.at[1]),
                (scale_two_in, scales.at[2]),
                (shift_two_in, scales.at[3]),
            )
        )
    ]
    for copy in small + inputs:
        copy.start()
    for copy in small:
        copy.wait()

    first = lane((ny, 128)) < 64
    square = jnp.zeros((ny, ny), F32)
    lows = jnp.concatenate([low[...].astype(F32), square[nx:]], axis=0).T
    highs = jnp.concatenate([high[...].astype(F32), square[nx:]], axis=0).T
    for x in range(nx):
        both = jnp.where(first, lows[:, x : x + 1], highs[:, x : x + 1]).astype(BF16)
        bounds[x] = both
        elh[x + 2, 16 : ny + 16, :] = both
    def all_wait(like, sem):
        pltpu.make_async_copy(like, like, sem).wait()

    def remote(src, dst, send, recv, to):
        return pltpu.make_async_remote_copy(
            src_ref=src,
            dst_ref=dst,
            send_sem=send,
            recv_sem=recv,
            device_id=to,
            device_id_type=MESH,
        )


    if comm:
        pl.semaphore_wait(barrier, len(peers))
    if comm:
        x_from = {-1: slice(0, 2), 0: slice(0, nx), 1: slice(nx - 2, nx)}
        x_to = {-1: slice(nx + 2, nx + 4), 0: slice(2, nx + 2), 1: slice(0, 2)}
        y_from = {-1: slice(0, 2), 0: slice(0, ny), 1: slice(ny - 2, ny)}
        y_to = {
            -1: slice(ny + 16, ny + 18),
            0: slice(16, ny + 16),
            1: slice(14, 16),
        }
        order = sorted(HALOS, key=lambda h: -(2 * abs(h[0]) - abs(h[1])))
        for dx, dy in order:
            for k, (src, dst) in enumerate(((feat, ext), (bounds, elh))):
                copy = remote(
                    src.at[x_from[dx], y_from[dy]],
                    dst.at[x_to[dx], y_to[dy]],
                    halo_send.at[k],
                    halo_recv.at[k],
                    device(dx, dy),
                )
                copy.start()
    inputs[0].wait()
    build_weights(w_one, fwd_one, adj_one)
    inputs[1].wait()
    build_weights(w_two, fwd_two, adj_two)
    nothing = jnp.zeros((3, 2 * ROWS, WIDTH), BF16)
    err_two[:, 0 : 2 * ROWS, :] = nothing
    err_two[:, 10 * ROWS : 12 * ROWS, :] = nothing
    err_one[:, 0 : 2 * ROWS, :] = nothing
    err_one[:, 12 * ROWS : 14 * ROWS, :] = nothing
    frame[...] = jnp.zeros_like(frame)

    occupied = jnp.where(high[...] > low[...], 1, 0)
    by_lane = lane((8, ny))
    count = jnp.int32(0)
    brick = [jnp.int32(-1000)] * SLOTS
    for bx in range(BX):
        rows = occupied[8 * bx : 8 * bx + 8]
        for by in range(BY):
            inside = (by_lane >= 8 * by) & (by_lane < 8 * by + 8)
            filled = jnp.max(jnp.where(inside, rows, 0))
            for j in range(SLOTS):
                hit = (filled > 0) & (count == j)
                brick[j] = jnp.where(hit, 8 * bx + by, brick[j])
            count = count + filled

    def picks(rows, columns, row_dim, per_brick, pitch, offset):
        shape = (rows, columns) if row_dim == 0 else (columns, rows)
        row = lax.broadcasted_iota(jnp.int32, shape, row_dim)
        column = lax.broadcasted_iota(jnp.int32, shape, 1 - row_dim)
        wanted = row + offset
        for j in range(SLOTS):
            b = brick[j]
            bx = jnp.where(b >= BY, 1, 0)
            spot = jnp.where(b < 0, -4000, bx * pitch + 8 * (b - BY * bx)) - per_brick * j
            inside = (row >= per_brick * j) & (row < per_brick * j + per_brick)
            wanted = wanted + jnp.where(inside, spot, 0)
        return jnp.where(column == wanted, 1.0, 0.0).astype(BF16)

    tall = ny + 32
    core_pick = picks(CORE, 2 * tall, 0, BRICK, tall, 16)
    frame_pick = [picks(ROWS, 2 * tall, 0, W, tall, 13 + oy) for oy in range(3)]
    pick_in[...] = jnp.concatenate(frame_pick + [core_pick], axis=0)
    pick_bounds[...] = jnp.concatenate([frame_pick[1], core_pick], axis=0)
    pick_target[...] = picks(CORE, 2 * ny, 0, BRICK, ny, 0)
    put_out[...] = picks(CORE, 2 * ny, 1, BRICK, ny, 0)
    put_grad[...] = picks(ROWS, 2 * (ny + 16), 1, W, ny + 16, 6)

    inputs[2].wait()
    def cut_target(x, carry):
        rows = jnp.concatenate([cot[x], cot[8 + x]], axis=0)
        spot = pl.ds(pl.multiple_of(x * CORE, CORE), CORE)
        target[spot, :] = jnp.dot(pick_target[...], rows, preferred_element_type=F32)
        return carry

    lax.fori_loop(0, 8, cut_target, 0, unroll=8)

    def mask_in(xs, ys):
        mask = height_mask(elh[xs, ys, :].astype(F32))
        for c in range(4):
            lanes = slice(128 * c, 128 * c + 128)
            value = ext[xs, ys, lanes].astype(F32)
            ext[xs, ys, lanes] = jnp.where(mask[c], value, 0.0).astype(BF16)

    def mask_inner(i, carry):
        mask_in(pl.ds(2 + 2 * i, 2), slice(16, ny + 16))
        return carry

    own.wait()
    lax.fori_loop(0, nx // 2, mask_inner, 0, unroll=2)
    if comm:
        margin = (nx + 4) * (ny + 4) - nx * ny
        for k, ref in enumerate((ext, elh)):
            all_wait(ref.at[0 : margin // 48, 0:48], halo_recv.at[k])
    if comm:
        for spot, inside in (
            ((slice(0, 2), slice(None)), gx > 0),
            ((slice(nx + 2, nx + 4), slice(None)), gx < n_gx - 1),
            ((slice(None), slice(0, 16)), gy > 0),
            ((slice(None), slice(ny + 16, ny + 32)), gy < n_gy - 1),
        ):
            value = elh[spot[0], spot[1], :].astype(F32)
            elh[spot[0], spot[1], :] = (
                value * jnp.where(inside, 1.0, 0.0).astype(F32)
            ).astype(BF16)
    else:
        for spot in (slice(0, 2), slice(nx + 2, nx + 4)):
            elh[spot] = jnp.zeros_like(elh[spot])
            ext[spot] = jnp.zeros_like(ext[spot])
        for spot in (slice(0, 16), slice(ny + 16, ny + 32)):
            elh[:, spot] = jnp.zeros_like(elh[:, spot])
            ext[:, spot] = jnp.zeros_like(ext[:, spot])

    for x in range(2, nx + 2, 4):
        mask_in(slice(x, x + 4), slice(0, 16))
        mask_in(slice(x, x + 4), slice(ny + 16, tall))
    for x in (0, 1, nx + 2, nx + 3):
        mask_in(slice(x, x + 1), slice(0, tall))

    def cut(x, carry):
        base = pl.multiple_of(x * ROWS, ROWS)
        core = pl.multiple_of(x * CORE, CORE)
        rows = jnp.concatenate([ext[x], ext[8 + x]], axis=0)
        value = jnp.dot(pick_in[...], rows, preferred_element_type=F32)
        for oy in range(3):
            src_one[oy, pl.ds(base, ROWS), :] = value[
                ROWS * oy : ROWS * oy + ROWS
            ].astype(BF16)
        core_in[pl.ds(core, CORE), :] = value[3 * ROWS :]
        rows = jnp.concatenate([elh[x], elh[8 + x]], axis=0)
        mask = height_mask(
            jnp.dot(pick_bounds[...], rows, preferred_element_type=F32)
        )
        for c in range(4):
            lanes = slice(128 * c, 128 * c + 128)
            value = jnp.where(mask[c], 1.0, 0.0)
            msk[pl.ds(base, ROWS), lanes] = value[:ROWS]
            core_mask[pl.ds(core, CORE), lanes] = value[ROWS:]
        return carry

    lax.fori_loop(0, W, cut, 0, unroll=12)

    scale_one, shift_one, scale_two, shift_two = (
        jnp.concatenate([scales[k]] * 4, axis=1) for k in range(4)
    )

    for g in range(2):
        lanes = slice(256 * g, 256 * g + 256)
        pre = conv(src_one, fwd_one, g, [(0, 10 * ROWS)], ROWS) * scale_one + shift_one
        s = jax.nn.sigmoid(pre)
        mask = msk[ROWS : 11 * ROWS, lanes]
        hidden = pre * s * mask
        slope[:, lanes] = s * (1.0 + pre * (1.0 - s)) * mask * scale_one
        for x in range(10):
            rows = hidden[ROWS * x : ROWS * x + ROWS]
            for oy in range(3):
                for j in range(0, SLOTS, 2):
                    both = [
                        rows[W * i + 1 + oy : W * i + 9 + oy] for i in (j, j + 1)
                    ]
                    src_two[oy, CORE * x + 8 * j : CORE * x + 8 * j + 16, lanes] = (
                        jnp.concatenate(both, axis=0).astype(BF16)
                    )

    middle = slice(2 * CORE, 10 * CORE)
    errors_t = []
    for g in range(2):
        lanes = slice(256 * g, 256 * g + 256)
        pre = conv(src_two, fwd_two, g, [(0, 8 * CORE)], CORE) * scale_two + shift_two
        pre = pre + core_in[middle, lanes]
        s = jax.nn.sigmoid(pre)
        mask = core_mask[middle, lanes]
        result = pre * s * mask
        grad = target[:, lanes] * mask * (s * (1.0 + pre * (1.0 - s)))
        errors_t.append((grad * scale_two).T.astype(BF16))
        res[:, lanes] = result.astype(BF16)
        for x in range(8):
            for j in range(SLOTS):
                spot = CORE * x + 8 * j
                frame[x, W * j + 2 : W * j + 10, lanes] = grad[spot : spot + 8]

    def spread(x, carry):
        base = pl.multiple_of((x + 2) * ROWS, ROWS)
        for g in range(2):
            lanes = slice(256 * g, 256 * g + 256)
            for oy, moved in enumerate(shifted(frame[x, :, lanes] * scale_two)):
                err_two[oy, pl.ds(base, ROWS), lanes] = moved.astype(BF16)
        return carry

    lax.fori_loop(0, 8, spread, 0, unroll=8)

    def send_block(k, b):
        if not comm:
            got_x[k, 0, b] = blocks[k, b]
            return

        @pl.when(gx != b)
        def _():
            remote(
                blocks.at[k, b],
                got_x.at[k, gx, 0],
                sum_send.at[k, 0],
                sum_recv.at[k, 0],
                (b, gy),
            ).start()

        @pl.when(gx == b)
        def _():
            got_x[k, gx, 0] = blocks[k, b]

    def owners(act):
        if comm:
            pl.when(gx < USED)(act)
        else:
            act()

    def reduce_x(k):
        def act():
            if comm:
                all_wait(got_x.at[k, 0 : n_gx - 1], sum_recv.at[k, 0])
            total = got_x[k, 0].astype(F32)
            for s in range(1, n_gx):
                total = total + got_x[k, s].astype(F32)
            half[0, k] = total.astype(BF16)
            for d in range(1, n_gy):
                remote(
                    half.at[0, k],
                    got_y.at[k, gy],
                    sum_send.at[k, 1],
                    sum_recv.at[k, 1],
                    (gx, lax.rem(gy + d, n_gy)),
                ).start()
            got_y[k, gy] = half[0, k]

        owners(act)

    def reduce_y(k):
        def act():
            if comm:
                all_wait(got_y.at[k, 0 : n_gy - 1], sum_recv.at[k, 1])
            total = got_y[k, 0].astype(F32)
            for s in range(1, n_gy):
                total = total + got_y[k, s].astype(F32)
            half[1, k] = total.astype(BF16)
            for d in range(1, n_gx):
                remote(
                    half.at[1, k],
                    full.at[k, gx],
                    sum_send.at[k, 2],
                    sum_recv.at[k, 2],
                    (lax.rem(gx + d, n_gx), gy),
                ).start()
            full[k, gx] = half[1, k]

        owners(act)

    weight_sums(
        errors_t, src_two, 8 * CORE, CORE, folded, blocks, 1, send_block
    )

    errors_t = []
    for g in range(2):
        lanes = slice(256 * g, 256 * g + 256)
        back = conv(err_two, adj_two, g, [(0, 10 * ROWS)], ROWS)
        error = back * slope[:, lanes]
        errors_t.append(error.T.astype(BF16))
        for x in range(10):
            rows = error[ROWS * x : ROWS * x + ROWS]
            spot = slice(ROWS * (x + 2), ROWS * (x + 3))
            for oy, moved in enumerate(shifted(rows)):
                err_one[oy, spot, lanes] = moved.astype(BF16)
    weight_sums(
        errors_t, src_one, 10 * ROWS, ROWS, folded, blocks, 0, send_block
    )
    reduce_x(1)

    def adjoint_one(g, columns):
        lanes = slice(256 * g, 256 * g + 256)
        spans = [(ROWS * x, ROWS * n) for x, n in columns]
        back = conv(err_one, adj_one, g, spans, ROWS)
        done = 0
        for start, n in columns:
            for x in range(start, start + n):
                rows = back[ROWS * done : ROWS * done + ROWS]
                if 2 <= x < 10:
                    rows = rows + frame[x - 2, :, lanes]
                grad_region[x, :, lanes] = rows.astype(BF16)
                done += 1

    def collect(x):
        total = None
        for bx in range(BX):
            if 0 <= x - 8 * bx < W:
                part = jnp.dot(
                    put_grad[bx * (ny + 16) : (bx + 1) * (ny + 16), :],
                    grad_region[x - 8 * bx],
                    preferred_element_type=F32,
                )
                total = part if total is None else total + part
        return total

    for g in range(2):
        adjoint_one(g, [(0, 2), (10, 2)])
    edges = []

    def send_edges(kinds):
        for i, (dx, dy) in enumerate(HALOS):
            if (dx, dy) not in kinds:
                continue
            a, b = (dx + 1) // 2, (dy + 1) // 2
            if dy == 0:
                src, dst = out_x.at[a], in_x.at[1 - a]
            elif dx == 0:
                src, dst = out_y.at[b], in_y.at[1 - b]
            else:
                src, dst = out_c.at[a, b], in_c.at[1 - a, 1 - b]
            copy = remote(
                src, dst, edge_send.at[i], edge_recv.at[i], device(dx, dy)
            )
            copy.start()
            edges.append(copy)

    if comm:
        for a, x in enumerate((0, nx + 2)):
            pair = [collect(x + k) for k in range(2)]
            for k in range(2):
                out_x[a, k] = pair[k][8 : ny + 8].astype(BF16)
            for b, t in enumerate((0, ny + 8)):
                both = [value[t : t + 8] for value in pair]
                out_c[a, b] = jnp.concatenate(both, axis=0).astype(BF16)
        send_edges([h for h in HALOS if h[0]])

    adjoint_one(0, [(2, 8)])
    reduce_x(0)
    adjoint_one(1, [(2, 8)])

    reduce_y(1)

    for x in range(2, nx + 2):
        value = collect(x)
        gsum[x] = value
        if comm:
            rows = slice(2 * (x - 2), 2 * (x - 2) + 2)
            edge_rows[0, rows, :] = value[6:8]
            edge_rows[1, rows, :] = value[ny + 8 : ny + 10]
    if comm:
        out_y[...] = edge_rows[...].astype(BF16)
        send_edges([h for h in HALOS if not h[0]])
    reduce_y(0)

    def deposit(x, carry):
        rows = res[pl.ds(pl.multiple_of(x * CORE, CORE), CORE), :]
        value = jnp.dot(put_out[...], rows, preferred_element_type=F32).astype(BF16)
        out[x] = value[:ny]
        out[8 + x] = value[ny:]
        return carry

    lax.fori_loop(0, 8, deposit, 0, unroll=8)

    if comm:
        for copy in edges:
            copy.wait_recv()
        x_in = [
            jnp.where(inside, 1.0, 0.0).astype(F32)
            for inside in (gx > 0, gx < n_gx - 1)
        ]
        y_in = [
            jnp.where(inside, 1.0, 0.0).astype(F32)
            for inside in (gy > 0, gy < n_gy - 1)
        ]
        for a, x in enumerate((2, nx)):
            gsum[x : x + 2, 8 : ny + 8, :] += in_x[a].astype(F32) * x_in[a]
            for b, t in enumerate((8, ny)):
                rows = in_c[a, b].astype(F32) * (x_in[a] * y_in[b])
                for k in range(2):
                    gsum[x + k, t : t + 8, :] += rows[8 * k : 8 * k + 8]
        for b, t in enumerate((8, ny + 6)):
            rows = in_y[b].astype(F32) * y_in[b]
            for i in range(nx):
                gsum[2 + i, t : t + 2, :] += rows[2 * i : 2 * i + 2]

    def finish(x, carry):
        mask = height_mask(elh[x + 2, 16 : ny + 16, :].astype(F32))
        for c in range(4):
            lanes = slice(128 * c, 128 * c + 128)
            value = gsum[x + 2, 8 : ny + 8, lanes]
            gfeat[x, :, lanes] = jnp.where(mask[c], value, 0.0).astype(BF16)
        return carry

    lax.fori_loop(0, nx, finish, 0, unroll=4)

    if comm:
        for copy in edges:
            copy.wait_send()
        for k, ref in enumerate((ext, elh)):
            all_wait(ref.at[0 : margin // 48, 0:48], halo_send.at[k])

        @pl.when(gx < USED)
        def _():
            for k in range(2):
                all_wait(full.at[k, 0 : USED - 1], sum_recv.at[k, 2])
                all_wait(blocks.at[k, 0 : USED - 1], sum_send.at[k, 0])
                all_wait(got_y.at[k, 0 : n_gy - 1], sum_send.at[k, 1])
                all_wait(full.at[k, 0 : n_gx - 1], sum_send.at[k, 2])

        @pl.when(gx >= USED)
        def _():
            for k in range(2):
                all_wait(full.at[k, 0:USED], sum_recv.at[k, 2])
                all_wait(blocks.at[k, 0:USED], sum_send.at[k, 0])


def result_kernel(
    factor, per, out_in, gfeat_in, full, out, gfeat, gw_one, gw_two, one, two, sem
):
    copies = [
        pltpu.make_async_copy(out_in, out, sem.at[0]),
        pltpu.make_async_copy(gfeat_in, gfeat, sem.at[1]),
    ]
    for copy in copies:
        copy.start()
    for k, (ref, gw) in enumerate(((one, gw_one), (two, gw_two))):
        unfold(full, per, k, ref, factor)
        copy = pltpu.make_async_copy(ref, gw, sem.at[2 + k])
        copy.start()
        copies.append(copy)
    for copy in copies:
        copy.wait()


def run(
    n_gx,
    n_gy,
    features,
    cotangent,
    low,
    high,
    weight_one,
    weight_two,
    scale_one,
    shift_one,
    scale_two,
    shift_two,
):
    nx, ny = features.shape[0], features.shape[1]
    per = BLOCKS // n_gx
    whole = pl.BlockSpec(memory_space=pltpu.VMEM)
    left = pl.BlockSpec(memory_space=pl.ANY)
    vm = pltpu.VMEM
    dma = pltpu.SemaphoreType.DMA
    scratch = [
        vm((nx, ny, WIDTH), BF16),
        vm((27 * C, C), BF16),
        vm((27 * C, C), BF16),
        vm((nx, ny), jnp.int32),
        vm((nx, ny), jnp.int32),
        vm((4, 1, C), F32),
        vm((nx, ny, 128), BF16),
        vm((nx + 4, ny + 32, WIDTH), BF16),
        vm((nx + 4, ny + 32, 128), BF16),
        vm((3 * ROWS + CORE, 2 * ny + 64), BF16),
        vm((ROWS + CORE, 2 * ny + 64), BF16),
        vm((CORE, 2 * ny), BF16),
        vm((2 * ny, CORE), BF16),
        vm((2 * ny + 32, ROWS), BF16),
        vm((3, W * ROWS, WIDTH), BF16),
        vm((3, 10 * CORE, WIDTH), BF16),
        vm((3, W * ROWS, WIDTH), BF16),
        vm((3, (W + 2) * ROWS, WIDTH), BF16),
        vm((W * ROWS, WIDTH), F32),
        vm((W * CORE, WIDTH), F32),
        vm((W * CORE, WIDTH), F32),
        vm((8 * CORE, WIDTH), F32),
        vm((10 * ROWS, WIDTH), F32),
        vm((8, ROWS, WIDTH), F32),
        vm((8 * CORE, WIDTH), BF16),
        vm((W, ROWS, WIDTH), BF16),
        vm((nx + 4, ny + 16, WIDTH), F32),
        vm((9 * 512, 256), BF16),
        vm((9 * 512, 256), BF16),
        vm((9 * 512, 256), BF16),
        vm((9 * 512, 256), BF16),
        vm((9, 64, 128), F32),
        vm((2, BLOCKS, 64, 128), BF16),
        vm((2, n_gx, per, 64, 128), BF16),
        vm((2, 2, per, 64, 128), BF16),
        vm((2, n_gy, per, 64, 128), BF16),
        vm((2, 2, ny, WIDTH), BF16),
        vm((2, 2, ny, WIDTH), BF16),
        vm((2, 2 * nx, WIDTH), F32),
        vm((2, 2 * nx, WIDTH), BF16),
        vm((2, 2 * nx, WIDTH), BF16),
        vm((2, 2, 16, WIDTH), BF16),
        vm((2, 2, 16, WIDTH), BF16),
        dma((11,)),
        dma((2,)),
        dma((2,)),
        dma((8,)),
        dma((8,)),
        dma((2, 3)),
        dma((2, 3)),
    ]
    comm = n_gx * n_gy > 1
    params = pltpu.CompilerParams(
        collective_id=0 if comm else None,
        has_side_effects=comm,
        vmem_limit_bytes=46 * 2**20,
    )
    in_hbm = functools.partial(
        pltpu.with_memory_space_constraint, memory_space=pltpu.HBM
    )
    columns = jax.ShapeDtypeStruct(features.shape, BF16)
    out, gfeat, full = pl.pallas_call(
        functools.partial(block_kernel, n_gx, n_gy),
        out_shape=(
            columns,
            columns,
            jax.ShapeDtypeStruct((2, n_gx, per, 64, 128), BF16),
        ),
        in_specs=[pl.BlockSpec(memory_space=pltpu.HBM)] * 10,
        out_specs=(whole,) * 3,
        scratch_shapes=scratch,
        compiler_params=params,
        name="residual_block",
    )(
        in_hbm(features),
        in_hbm(cotangent),
        in_hbm(weight_one.reshape(27 * C, C)),
        in_hbm(weight_two.reshape(27 * C, C)),
        in_hbm(low),
        in_hbm(high),
        in_hbm(scale_one.reshape(1, C)),
        in_hbm(shift_one.reshape(1, C)),
        in_hbm(scale_two.reshape(1, C)),
        in_hbm(shift_two.reshape(1, C)),
    )
    sums = jax.ShapeDtypeStruct((27 * C, C), F32)
    out, gfeat, gw_one, gw_two = pl.pallas_call(
        functools.partial(result_kernel, 1.0 / (n_gx * n_gy * SHARE), per),
        out_shape=(columns, columns, sums, sums),
        in_specs=[left, left, whole],
        out_specs=(left,) * 4,
        scratch_shapes=[vm((27 * C, C), F32), vm((27 * C, C), F32), dma((4,))],
        compiler_params=pltpu.CompilerParams(vmem_limit_bytes=8 * 2**20),
        name="results",
    )(out, gfeat, full)
    return out, gfeat, gw_one.reshape(27, C, C), gw_two.reshape(27, C, C)


def solution(mesh):
    columns = P("gx", "gy", None)
    placed = (columns, columns, P("gx", "gy"), P("gx", "gy")) + (P(),) * 6
    return jax.shard_map(
        functools.partial(run, mesh.shape["gx"], mesh.shape["gy"]),
        mesh=mesh,
        in_specs=placed,
        out_specs=(columns, columns, P(), P()),
        check_vma=False,
    )
```
